32 devices in a mesh: cond: 4 (over y, core), seq: 8 (over z, x).
Axes of the slice: x: 2, y: 2, z: 4, core: 2. Of those that a mesh axis runs over, the one named last changes fastest.
Arguments:
- inputs: bfloat16 [4, 4096, 1024], P(None, 'seq', 'cond'), may hold values from -100 to 100
- coarse_ids: int32 [4, 1024], P(None, 'seq'), may hold values from 0 to 2047
- segment_ids: int32 [4, 4096], P(None, 'seq'), may hold values from 0 to 31, never falling along the last dimension, each value on 1 to 256 neighbouring positions
- cotangent: bfloat16 [4, 4096, 1024], P(None, 'seq', 'cond'), may hold values from -6 to 6
- embed_table: bfloat16 [2048, 1024], P('seq', 'cond'), may hold values from -6 to 6
- conv_weight: bfloat16 [3, 1024, 1024], P(None, 'cond', 'seq'), may hold values from -0.109375 to 0.109375
- res_weight: bfloat16 [1024, 1024], P('seq', 'cond'), may hold values from -0.1875 to 0.1875
- up_weight: bfloat16 [1024, 4096], P('cond', 'seq'), may hold values from -0.1875 to 0.1875
- gain_one: bfloat16 [1024], P(('cond', 'seq')), may hold values from 0.5 to 1.5
- shift_one: bfloat16 [1024], P(('cond', 'seq')), may hold values from -2 to 2
- qkv_weight: bfloat16 [1024, 3, 1024], P('seq', None, 'cond'), may hold values from -0.1875 to 0.1875
- out_weight: bfloat16 [1024, 1024], P('cond', 'seq'), may hold values from -0.5 to 0.5
- gain_two: bfloat16 [1024], P(('cond', 'seq')), may hold values from 0.5 to 1.5
- shift_two: bfloat16 [1024], P(('cond', 'seq')), may hold values from -2 to 2
- in_weight: bfloat16 [1024, 4096], P('seq', 'cond'), may hold values from -0.1875 to 0.1875
- down_weight: bfloat16 [4096, 1024], P('cond', 'seq'), may hold values from -0.09375 to 0.09375
Outputs:
- activation: bfloat16 [4, 4096, 1024], P(None, 'seq', 'cond')
- input_grad: bfloat16 [4, 4096, 1024], P(None, 'seq', 'cond')
- grad_table: float32 [2048, 1024], P('seq', 'cond')
- grad_conv: float32 [3, 1024, 1024], P(None, 'cond', 'seq')
- grad_res: float32 [1024, 1024], P('seq', 'cond')
- grad_up: float32 [1024, 4096], P('cond', 'seq')
- grad_gain_one: float32 [1024], P(('cond', 'seq'))
- grad_shift_one: float32 [1024], P(('cond', 'seq'))
- grad_qkv: float32 [1024, 3, 1024], P('seq', None, 'cond')
- grad_out: float32 [1024, 1024], P('cond', 'seq')
- grad_gain_two: float32 [1024], P(('cond', 'seq'))
- grad_shift_two: float32 [1024], P(('cond', 'seq'))
- grad_in: float32 [1024, 4096], P('seq', 'cond')
- grad_down: float32 [4096, 1024], P('cond', 'seq')
The draws below stay inside these ranges and needn't reach their ends.
All inputs are finite; a program needn't handle non-finite values.
Results may differ from the reference program's by a relative error of at most 0.02.
Values may be sent and summed in bfloat16 or wider, within the bound.
No kernel may reach another device: no remote copies, remote signals or barrier semaphores. Data moves between devices by JAX's collectives and lax.ppermute only.
A program may use at most 112 MiB of HBM per device.

```python
import math
import jax
import jax.numpy as jnp
import numpy as np
from jax import lax

D = 1024
HEADS = 16
HEAD = 64
FF = 4096
VOCAB = 2048
ROW = 64
CONV_DILATION = 27
MICRO = 4
L = 4096
LC = 1024


def draw_inputs(key, part):
    base_key = jax.random.fold_in(key, 11)
    col_key = jax.random.fold_in(key, 12)
    row_key = jax.random.fold_in(key, 13)
    base = jax.random.normal(base_key, (MICRO, L, D), jnp.float32)
    cols = jnp.exp(2.302585 * jax.random.uniform(col_key, (D,), jnp.float32, -0.5, 0.5))
    rows = jnp.exp(2.302585 * jax.random.uniform(row_key, (MICRO, L, 1), jnp.float32, -0.5, 0.5))
    return (base * cols * rows).astype(jnp.bfloat16)


def touch_ends(values, stream_key, smallest, high):
    longest = values.shape.index(max(values.shape))
    spots = []
    for shift in (0, 1):
        where = [jax.random.randint(jax.random.fold_in(stream_key, axis), (), 0, length) for axis, length in enumerate(values.shape)]
        where[longest] = (where[longest] + shift) % values.shape[longest]
        spots.append(tuple(where))
    return values.at[spots[0]].set(smallest).at[spots[1]].set(high)


def levels(rng, extent, pieces, low, largest):
    level, own = 1.0, jax.random.fold_in(rng, 6)
    for dim, blocks in pieces:
        draws = jnp.exp(jax.random.uniform(jax.random.fold_in(own, dim), (blocks,), jnp.float32, low / len(pieces), largest / len(pieces)))
        level = level * jnp.repeat(draws, extent[dim] // blocks).reshape([-1 if axis == dim else 1 for axis in range(len(extent))])
    return level


def profile(number_of, total, reach, lean):
    loads = [(1 << 20) // math.isqrt(standing ** lean) + 1 for standing in range(2, number_of + 1)]
    surplus, counts = total - reach - (number_of - 1), [1] * (number_of - 1)
    while surplus > 0:
        candidates = [i for i in range(number_of - 1) if counts[i] < reach]
        whole, remaining = sum([loads[i] for i in candidates]), surplus
        for i in candidates:
            extra = min(reach - counts[i], max(1, remaining * loads[i] // whole), surplus)
            counts[i] = counts[i] + extra
            surplus = surplus - extra
    return np.array([reach] + counts)


def ragged_sizes(stream_key, count, total, bound, lean):
    if count == 2:
        one = jax.random.randint(stream_key, (), max(1, total - bound), min(bound, total - 1) + 1)
        return jnp.stack([one, total - one])
    sizes = jnp.asarray(profile(count, total, bound, lean), jnp.int32)
    twos = (count - 1) // 2
    donor, receiver = sizes[1:1 + 2 * twos:2], sizes[2:2 + 2 * twos:2]
    margin = jnp.minimum(donor - 1, bound - receiver)
    shifted = jax.random.randint(jax.random.fold_in(stream_key, 1), (twos,), 0, 1 << 20) % (margin + 1)
    sizes = sizes.at[1:1 + 2 * twos:2].set(donor - shifted).at[2:2 + 2 * twos:2].set(receiver + shifted)
    return sizes[jax.random.permutation(jax.random.fold_in(stream_key, 2), count)]


def bell_draw(stream_key, extent, width, reach, shards=(), dtype=jnp.bfloat16):
    drawn = jax.random.normal(stream_key, extent, jnp.float32) * width
    if len(shards) > 0:
        drawn = levels(stream_key, extent, shards, -0.22, 0.18) * drawn
    return jnp.clip(drawn, min=-reach, max=reach).astype(dtype)


def setup_inputs(seed: int = 0) -> dict:
    seeds = jax.random.split(jax.random.key(seed), 17)
    return {
        "inputs": draw_inputs(jax.random.fold_in(seeds[16], 71), 0),
        "coarse_ids": touch_ends(jax.random.randint(seeds[1], (MICRO, LC), 0, VOCAB), jax.random.fold_in(seeds[1], 1), 0, VOCAB - 1).astype(jnp.int32),
        "segment_ids": jax.vmap(lambda own: jnp.searchsorted(jnp.cumsum(ragged_sizes(own, L // 128, L, 256, 1)), jnp.arange(L), side="right"))(jax.random.split(seeds[2], MICRO)).reshape((MICRO, L)).astype(jnp.int32),
        "cotangent": bell_draw(seeds[3], (MICRO, L, D), 1.0, 6.0, ((1, 8), (2, 4))),
        "embed_table": bell_draw(seeds[4], (VOCAB, D), 1.0, 6.0, ((0, 8), (1, 4))),
        "conv_weight": bell_draw(seeds[5], (3, D, D), (3 * D) ** -0.5, 0.109375, ((1, 4), (2, 8))),
        "res_weight": bell_draw(seeds[6], (D, D), D ** -0.5, 0.1875, ((0, 8), (1, 4))),
        "up_weight": bell_draw(seeds[7], (D, 4 * D), D ** -0.5, 0.1875, ((0, 4), (1, 8))),
        "gain_one": jnp.clip(1.0 + 0.1 * jax.random.normal(seeds[8], (D,), jnp.float32), 0.5, 1.5).astype(jnp.bfloat16),
        "shift_one": bell_draw(seeds[9], (D,), 0.3, 2.0, ((0, 32),)),
        "qkv_weight": bell_draw(seeds[10], (D, 3, D), D ** -0.5, 0.1875, ((0, 8), (2, 4))),
        "out_weight": bell_draw(seeds[11], (D, D), (D // 8) ** -0.5, 0.5, ((0, 4), (1, 8))),
        "gain_two": jnp.clip(1.0 + 0.1 * jax.random.normal(seeds[12], (D,), jnp.float32), 0.5, 1.5).astype(jnp.bfloat16),
        "shift_two": bell_draw(seeds[13], (D,), 0.3, 2.0, ((0, 32),)),
        "in_weight": bell_draw(seeds[14], (D, FF), D ** -0.5, 0.1875, ((0, 8), (1, 4))),
        "down_weight": bell_draw(seeds[15], (FF, D), FF ** -0.5, 0.09375, ((0, 4), (1, 8))),
    }


@jax.custom_vjp
def low(v):
    return lax.optimization_barrier(v.astype(jnp.bfloat16)).astype(jnp.float32)

@jax.custom_vjp
def low_back(v):
    return v

def low_keep(v):
    return (low(v), None)

def low_pass(kept, grad):
    return (grad,)

def back_keep(v):
    return (v, None)

def back_low(kept, grad):
    return (low(grad),)
low.defvjp(low_keep, low_pass)
low_back.defvjp(back_keep, back_low)
HIGHEST = lax.Precision.HIGHEST
EPSILON = 1e-05
NEG_FILL = -1e+30

def gelu_exact(value):
    return jax.nn.gelu(value, approximate=False)

def layer_norm(value, gain, shift):
    mean_row = lax.optimization_barrier(jnp.mean(value, axis=-1, keepdims=True))
    centred = value - mean_row
    var_row = lax.optimization_barrier(jnp.mean(centred * centred, axis=-1, keepdims=True))
    return centred * lax.rsqrt(var_row + EPSILON) * gain + shift

def forward(stream, coarse, segments, embed_table, conv_weight, res_weight, up_weight, gain_one, shift_one, qkv_weight, out_weight, gain_two, shift_two, in_weight, down_weight):
    seq_len, model_width = stream.shape
    coarse_length = coarse.shape[0]
    embed = low_back(embed_table[coarse])
    coarse_activation_rows = low(gelu_exact(embed))
    padded_input = jnp.pad(coarse_activation_rows, ((CONV_DILATION, CONV_DILATION), (0, 0)))
    kernel_tap_rows = jnp.concatenate([padded_input[kernel_tap * CONV_DILATION:kernel_tap * CONV_DILATION + coarse_length] for kernel_tap in range(3)], axis=1)
    conv_out = low_back(jnp.dot(kernel_tap_rows, conv_weight.reshape(3 * model_width, model_width), precision=HIGHEST))
    mixed_act = low(gelu_exact(conv_out))
    res_out = low_back(jnp.dot(mixed_act, res_weight, precision=HIGHEST))
    hidden_cond = low(embed + res_out)
    up_terms = low_back(jnp.dot(hidden_cond, up_weight, precision=HIGHEST)).reshape(seq_len, model_width)
    stream_zero = stream + up_terms
    norm_one = low(layer_norm(stream_zero, gain_one, shift_one))
    qkv_all = low(low_back(jnp.einsum('td,dje->tje', norm_one, qkv_weight, precision=HIGHEST)))
    row_count = seq_len // ROW
    block_shape = (row_count, ROW, HEADS, HEAD)
    query_part = qkv_all[:, 0].reshape(block_shape)
    key_part = qkv_all[:, 1].reshape(block_shape)
    value_part = qkv_all[:, 2].reshape(block_shape)
    seg_rows = segments.reshape(row_count, ROW)
    places = jnp.arange(ROW)
    allowed = ((seg_rows[:, :, None] == seg_rows[:, None, :]) & (places[:, None] >= places[None, :])[None])[:, None]
    scores = low_back(jnp.einsum('bqhd,bkhd->bhqk', query_part, key_part, precision=HIGHEST) * (1.0 / math.sqrt(HEAD)))
    masked = jnp.where(allowed, scores, NEG_FILL)
    attn_probs = low(jax.nn.softmax(masked, axis=-1))
    context = low(low_back(jnp.einsum('bhqk,bkhd->bqhd', attn_probs, value_part, precision=HIGHEST)))
    context = context.reshape(seq_len, model_width)
    stream_one = stream_zero + low_back(jnp.dot(context, out_weight, precision=HIGHEST))
    norm_two = low(layer_norm(stream_one, gain_two, shift_two))
    mlp_pre = low_back(jnp.dot(norm_two, in_weight, precision=HIGHEST))
    mlp_act = low(gelu_exact(mlp_pre))
    return stream_one + low_back(jnp.dot(mlp_act, down_weight, precision=HIGHEST))

def reference(inputs, coarse_ids, segment_ids, cotangent, embed_table, conv_weight, res_weight, up_weight, gain_one, shift_one, qkv_weight, out_weight, gain_two, shift_two, in_weight, down_weight):
    params = tuple((weight_arg.astype(jnp.float32) for weight_arg in (embed_table, conv_weight, res_weight, up_weight, gain_one, shift_one, qkv_weight, out_weight, gain_two, shift_two, in_weight, down_weight)))
    outputs = []
    in_grads = []
    summed = None
    for index in range(MICRO):

        def apply_layer(stream, *weights, index=index):
            return forward(stream, coarse_ids[index], segment_ids[index], *weights)
        result, pull = jax.vjp(apply_layer, inputs[index].astype(jnp.float32), *params)
        grads = pull(cotangent[index].astype(jnp.float32))
        outputs.append(result.astype(jnp.bfloat16))
        in_grads.append(grads[0].astype(jnp.bfloat16))
        summed = tuple(grads[1:]) if summed is None else jax.tree.map(jnp.add, summed, tuple(grads[1:]))
    return (jnp.stack(outputs), jnp.stack(in_grads), summed[0], summed[1], summed[2], summed[3], summed[4], summed[5], summed[6], summed[7], summed[8], summed[9], summed[10], summed[11])
```

```python
import math

import jax
import jax.numpy as jnp
from jax import lax
from jax.experimental import pallas as pl
from jax.experimental.pallas import tpu as pltpu
from jax.sharding import PartitionSpec as P

HEAD = 64
ROW = 64
CONV_DILATION = 27
EPSILON = 1e-05
NEG_FILL = -1e30
LANES = 128
BF16 = jnp.bfloat16
F32 = jnp.float32


def tuned():
    return lax.axis_size("seq") == 8


def swap(x, j):
    return lax.ppermute(x, "cond", [(i, i ^ j) for i in range(4)])


def hop(x, k):
    return lax.ppermute(x, "seq", [(i, i ^ k) for i in range(8)])


def place():
    c = lax.axis_index("cond")
    if tuned():
        s = lax.axis_index("seq")
        return c, s >> 1, s & 1
    zero = jnp.zeros((), jnp.int32)
    return c, zero, zero


def dot(a, b, dims=((1,), (0,))):
    return lax.dot_general(a, b, (dims, ((), ())), preferred_element_type=F32)


def gram(a, b):
    return dot(a, b, ((0,), (0,)))


def dot_t(a, b):
    return dot(a, b, ((1,), (1,)))


def gelu(v):
    return 0.5 * v * (1.0 + lax.erf(v * math.sqrt(0.5)))


def gelu_grad(v):
    return 0.5 * (1.0 + lax.erf(v * math.sqrt(0.5))) + v * (
        math.sqrt(0.5 / math.pi) * jnp.exp(-0.5 * v * v)
    )


def pick(items, t):
    low, high = (t & 1) == 1, (t & 2) == 2
    items = [jnp.where(low, items[i ^ 1], items[i]) for i in range(4)]
    return [jnp.where(high, items[i ^ 2], items[i]) for i in range(4)]


def regroup(x, dim, outer, inner):
    n = x.shape[dim] // 8
    shape = x.shape
    x = x.reshape(shape[:dim] + (outer, inner, n) + shape[dim + 1 :])
    return jnp.swapaxes(x, dim, dim + 1).reshape(shape)


def gather(shard, dim):
    if tuned():
        near = jnp.concatenate([shard] + [hop(shard, 2 * k) for k in (1, 2, 3)], axis=dim)
        return jnp.concatenate([near, hop(near, 1)], axis=dim)
    return regroup(lax.all_gather(shard, "seq", axis=dim, tiled=True), dim, 4, 2)


def scatter(full, dim):
    full = full.astype(BF16)
    if tuned():
        near, far = jnp.split(full, 2, axis=dim)
        near = near.astype(F32) + hop(far, 1).astype(F32)
        parts = jnp.split(near, 4, axis=dim)
        total = parts[0]
        for k in (1, 2, 3):
            total = total + hop(parts[k].astype(BF16), 2 * k).astype(F32)
        return total
    return lax.psum_scatter(
        regroup(full, dim, 2, 4), "seq", scatter_dimension=dim, tiled=True
    ).astype(F32)


def spread(x):
    y = swap(x, 2)
    return [x, swap(x, 1), y, swap(y, 1)]


def exchange(items):
    return [items[0]] + [swap(items[j], j) for j in (1, 2, 3)]


def fold(items, wire=BF16, place_rows=None):
    fix = place_rows or (lambda x, j: x)
    one = fix(swap(items[1].astype(wire), 1), 1).astype(F32)
    three = fix(swap(items[3].astype(wire), 1), 1).astype(F32)
    zero = items[0].astype(F32) + one
    two = (items[2].astype(F32) + three).astype(BF16)
    return zero + fix(swap(two, 2), 2).astype(F32)


def copy_block(index_ref, in_ref, out_ref):
    out_ref[...] = in_ref[...]


def move_blocks(x, index):
    rows = x.shape[0]
    count = index.shape[0]
    return pl.pallas_call(
        copy_block,
        out_shape=jax.ShapeDtypeStruct((rows, count * LANES), x.dtype),
        grid_spec=pltpu.PrefetchScalarGridSpec(
            num_scalar_prefetch=1,
            grid=(count,),
            in_specs=[pl.BlockSpec((rows, LANES), lambda i, index: (0, index[i]))],
            out_specs=pl.BlockSpec((rows, LANES), lambda i, index: (0, i)),
        ),
        name="move_blocks",
    )(index, x)


def normalize(stream):
    mean = jnp.mean(stream, axis=1, keepdims=True)
    centred = stream - mean
    rstd = lax.rsqrt(jnp.mean(centred * centred, axis=1, keepdims=True) + EPSILON)
    return centred * rstd, rstd


def normalize_back(normed, rstd, gain, grad):
    scaled = grad * gain
    back = rstd * (
        scaled
        - jnp.mean(scaled, axis=1, keepdims=True)
        - normed * jnp.mean(scaled * normed, axis=1, keepdims=True)
    )
    return back, jnp.sum(grad * normed, axis=0), jnp.sum(grad, axis=0)


def vector_owner(c, z, x):
    i = jnp.arange(32)
    kx, kz, part = i >> 4, (i >> 2) & 3, i & 3
    j = kz ^ z ^ c
    source = ((kx ^ x) << 2) | part
    if tuned():
        piece = j * 8 + ((((source & 1) ^ x) << 2) | ((source >> 1) ^ z))
    else:
        piece = j * 8 + source
    return piece[:, None] == jnp.arange(32)[None, :]


def gather_vectors(vectors, c, z, x):
    pieces = lax.all_gather(vectors, "seq", axis=1, tiled=True) if not tuned() else gather(vectors, 1)
    pieces = jnp.stack(spread(pieces), axis=1)
    count, _, width = pieces.shape
    pieces = pieces.reshape(count, 32, width // 8)
    owner = vector_owner(c, z, x).astype(BF16)
    full = jnp.einsum("dp,vpn->vdn", owner, pieces, preferred_element_type=F32)
    return full.reshape(count, 4 * width)


def scatter_vectors(full, c, z, x):
    count, width = full.shape
    owner = vector_owner(c, z, x).astype(F32)
    pieces = jnp.einsum(
        "dp,vdn->vpn",
        owner,
        full.reshape(count, 32, width // 32),
        precision=lax.Precision.HIGHEST,
        preferred_element_type=F32,
    ).reshape(count, 4, width // 4)
    mine = fold([pieces[:, j] for j in range(4)], F32)
    if tuned():
        return scatter(mine, 1)
    return lax.psum_scatter(mine, "seq", scatter_dimension=1, tiled=True)


def attend(qkv, allowed):
    rows = qkv.shape[0] // ROW
    width = qkv.shape[1] // 3
    shape = (rows, ROW, width // HEAD, HEAD)
    query, key, value = (qkv[:, i * width : (i + 1) * width].reshape(shape) for i in range(3))
    scores = jnp.einsum("bqhd,bkhd->bhqk", query, key, preferred_element_type=F32) * (
        1.0 / math.sqrt(HEAD)
    )
    scores = jnp.where(allowed, scores, NEG_FILL)
    exps = jnp.exp(scores - jnp.max(scores, axis=-1, keepdims=True))
    probs = exps / jnp.sum(exps, axis=-1, keepdims=True)
    context = jnp.einsum("bhqk,bkhd->bqhd", probs.astype(BF16), value, preferred_element_type=F32)
    return context.astype(BF16).reshape(qkv.shape[0], width), probs


def attend_back(qkv, probs, grad_context):
    rows = qkv.shape[0] // ROW
    width = qkv.shape[1] // 3
    shape = (rows, ROW, width // HEAD, HEAD)
    query, key, value = (qkv[:, i * width : (i + 1) * width].reshape(shape) for i in range(3))
    scale = 1.0 / math.sqrt(HEAD)
    grad_context = grad_context.reshape(shape)
    grad_probs = jnp.einsum("bqhd,bkhd->bhqk", grad_context, value, preferred_element_type=F32)
    inner = jnp.sum(probs * grad_probs, axis=-1, keepdims=True)
    grad_scores = (probs * (grad_probs - inner)).astype(BF16)
    grads = (
        jnp.einsum("bhqk,bkhd->bqhd", grad_scores, key, preferred_element_type=F32) * scale,
        jnp.einsum("bhqk,bqhd->bkhd", grad_scores, query, preferred_element_type=F32) * scale,
        jnp.einsum("bhqk,bqhd->bkhd", probs.astype(BF16), grad_context, preferred_element_type=F32),
    )
    return jnp.concatenate(
        [g.astype(BF16).reshape(qkv.shape[0], width) for g in grads], axis=1
    )


def edges(cells):
    count = lax.axis_size("seq")
    head, tail = cells
    return (
        lax.ppermute(tail, "seq", [(i, i + 1) for i in range(count - 1)]),
        lax.ppermute(head, "seq", [(i + 1, i) for i in range(count - 1)]),
    )


def on_device(
    inputs,
    coarse_ids,
    segment_ids,
    cotangent,
    embed_table,
    conv_weight,
    res_weight,
    up_weight,
    gain_one,
    shift_one,
    qkv_weight,
    out_weight,
    gain_two,
    shift_two,
    in_weight,
    down_weight,
):
    c, z, x = place()
    turn = c ^ z
    micros, tokens, quarter = inputs.shape
    width = 4 * quarter
    coarse = coarse_ids.shape[1]
    half = width // 2
    step = CONV_DILATION
    slot = jnp.arange(8, dtype=jnp.int32)
    to_layer = (((slot & 3) ^ turn) << 1) | ((slot >> 2) ^ x)
    to_quarters = (((slot & 1) ^ x) << 2) | ((slot >> 1) ^ turn)

    table = gather(embed_table, 0)
    conv = gather(conv_weight.reshape(3 * quarter, -1), 1)
    res = spread(gather(res_weight, 0))
    up = spread(gather(up_weight, 1))
    vectors = gather_vectors(jnp.stack([gain_one, shift_one, gain_two, shift_two]), c, z, x)
    qkv_w = spread(gather(qkv_weight.reshape(-1, 3 * quarter), 0))
    out_w = spread(gather(out_weight, 1))
    in_w = gather(in_weight, 0)
    down_w = move_blocks(gather(down_weight, 1), to_quarters)
    gain1, shift1, gain2, shift2 = (vectors[i][None, :] for i in range(4))

    mine = pick([inputs[i] for i in range(4)], c)
    stream_in = move_blocks(jnp.concatenate(exchange(mine), axis=1), to_layer)
    cot = jnp.concatenate(pick([cotangent[i] for i in range(4)], c), axis=0)
    cots = [item.reshape(micros, tokens, quarter) for item in spread(cot)]
    cot_all = jnp.concatenate(
        [jnp.concatenate([cots[j][m ^ j] for m in range(4)], axis=0) for j in range(4)], axis=1
    )
    cot_mine = move_blocks(cot_all[:tokens], to_layer)

    ids = jnp.concatenate(pick([coarse_ids[i] for i in range(4)], c))
    vocab = table.shape[0]
    code = jnp.arange(vocab, dtype=jnp.int32)
    block = vocab // 8
    slot_of = code // block
    code = ((((slot_of & 3) ^ z) << 1) | ((slot_of >> 2) ^ x)) * block + code % block
    onehot = (ids[:, None] == code[None, :]).astype(BF16)
    embed = dot(onehot, table)
    act = gelu(embed).astype(BF16).reshape(micros, coarse, quarter)
    before, after = edges((act[:, :step], act[:, coarse - step :]))
    padded = jnp.concatenate([before, act, after], axis=1)
    taps = jnp.concatenate(
        [padded[:, k * step : k * step + coarse] for k in range(3)], axis=2
    ).reshape(micros * coarse, 3 * quarter)
    conv_terms = dot(taps, conv).reshape(micros, coarse, width)
    conv_out = fold([conv_terms[j] for j in range(4)])
    embeds = exchange([e for e in embed.astype(BF16).reshape(micros, coarse, quarter)])

    mixed = gelu(conv_out).astype(BF16)
    hidden = [(embeds[j].astype(F32) + dot(mixed, res[j])).astype(BF16) for j in range(4)]
    up_terms = dot(hidden[0], up[0])
    for j in (1, 2, 3):
        up_terms = up_terms + dot(hidden[j], up[j])
    phase_index = jnp.arange(32, dtype=jnp.int32)
    r, p = phase_index >> 3, phase_index & 7
    bz, bx = (p & 3) ^ z, (p >> 2) ^ x
    from_up = ((bz >> 1) ^ x) * 16 + (r ^ z) * 4 + ((bz & 1) << 1 | bx)
    i = phase_index
    kx, kz, w = i >> 4, (i >> 2) & 3, i & 3
    h = kx ^ x
    bz2, bx2 = (h << 1) | (w >> 1), w & 1
    to_up = (kz ^ z) * 8 + ((bx2 ^ x) << 2 | (bz2 ^ z))
    up_terms = move_blocks(up_terms, from_up).reshape(tokens, width)
    stream_zero = stream_in.astype(F32) + up_terms
    normed_one, rstd_one = normalize(stream_zero)
    norm_one = (normed_one * gain1 + shift1).astype(BF16)
    segments = lax.dynamic_index_in_dim(segment_ids, c, 0, keepdims=False)
    rows = segments.reshape(tokens // ROW, ROW)
    spots = jnp.arange(ROW)
    allowed = (
        (rows[:, :, None] == rows[:, None, :]) & (spots[:, None] >= spots[None, :])[None]
    )[:, None]
    qkv = [dot(norm_one, qkv_w[j]).astype(BF16) for j in range(4)]
    context, probs = zip(*[attend(qkv[j], allowed) for j in range(4)])
    stream_one = stream_zero
    for j in range(4):
        stream_one = stream_one + dot(context[j], out_w[j])
    normed_two, rstd_two = normalize(stream_one)
    norm_two = (normed_two * gain2 + shift2).astype(BF16)

    norm_all = jnp.concatenate(spread(norm_two), axis=0)
    mlp_pre = dot(norm_all, in_w)
    mlp_act = gelu(mlp_pre).astype(BF16)
    grad_down = gram(mlp_act, cot_all).astype(BF16)
    grad_down = scatter(move_blocks(grad_down, to_layer), 1)
    mlp_out = dot(mlp_act, down_w)
    stream_q = move_blocks(stream_one, to_quarters)
    mlp_out = mlp_out.reshape(micros, tokens, width)
    mlp_out = jnp.concatenate([(mlp_out[0] + stream_q)[None], mlp_out[1:]], axis=0)
    result = fold(
        [mlp_out[:, :, j * quarter : (j + 1) * quarter] for j in range(4)],
        place_rows=lambda v, j: jnp.stack([v[m ^ j] for m in range(4)]),
    ).astype(BF16)
    result = jnp.stack(pick([result[m] for m in range(4)], c))

    grad_pre = (gelu_grad(mlp_pre) * dot_t(cot_all, down_w)).astype(BF16)
    grad_in = scatter(gram(norm_all, grad_pre), 0)
    grad_norm_two = dot_t(grad_pre, in_w).reshape(micros, tokens, width)
    grad_norm_two = fold([grad_norm_two[j] for j in range(4)])

    back_two, grad_gain2, grad_shift2 = normalize_back(normed_two, rstd_two, gain2, grad_norm_two)
    grad_stream_one = cot_mine.astype(F32) + back_two
    grad_att = grad_stream_one.astype(BF16)
    grad_out = scatter(fold([gram(context[j], grad_att) for j in range(4)]), 1)
    grad_rows = [
        attend_back(qkv[j], probs[j], dot_t(grad_att, out_w[j]).astype(BF16)) for j in range(4)
    ]
    grad_qkv = scatter(fold([gram(norm_one, grad_rows[j]) for j in range(4)]), 0)
    grad_norm_one = dot_t(grad_rows[0], qkv_w[0])
    for j in (1, 2, 3):
        grad_norm_one = grad_norm_one + dot_t(grad_rows[j], qkv_w[j])
    back_one, grad_gain1, grad_shift1 = normalize_back(normed_one, rstd_one, gain1, grad_norm_one)
    input_grad = (grad_stream_one + back_one).astype(BF16)
    grad_vectors = scatter_vectors(
        jnp.stack([grad_gain1, grad_shift1, grad_gain2, grad_shift2]), c, z, x
    )
    grad_in_q = move_blocks(input_grad, to_quarters)
    grad_in_q = exchange([grad_in_q[:, j * quarter : (j + 1) * quarter] for j in range(4)])
    input_grads = jnp.stack(pick(grad_in_q, c))

    grad_up_rows = move_blocks(input_grad.reshape(coarse, 4 * width), to_up)
    grad_up = scatter(fold([gram(hidden[j], grad_up_rows) for j in range(4)]), 1)
    grad_hidden = [dot_t(grad_up_rows, up[j]).astype(BF16) for j in range(4)]
    grad_res = scatter(fold([gram(mixed, grad_hidden[j]) for j in range(4)]), 0)
    grad_mixed = dot_t(grad_hidden[0], res[0])
    for j in (1, 2, 3):
        grad_mixed = grad_mixed + dot_t(grad_hidden[j], res[j])
    grad_conv_low = (gelu_grad(conv_out) * grad_mixed).astype(BF16)

    grad_conv_all = jnp.concatenate(spread(grad_conv_low), axis=0)
    grad_conv = scatter(gram(taps, grad_conv_all), 1).reshape(conv_weight.shape)
    grad_taps = dot_t(grad_conv_all, conv).reshape(micros, coarse, 3 * quarter)
    tap = [grad_taps[:, :, k * quarter : (k + 1) * quarter] for k in range(3)]
    before, after = edges((tap[0][:, :step].astype(BF16), tap[2][:, coarse - step :].astype(BF16)))
    blank = jnp.zeros((micros, coarse - step, quarter), F32)
    grad_act = (
        tap[1]
        + jnp.concatenate([tap[0][:, step:], after.astype(F32)], axis=1)
        + jnp.concatenate([before.astype(F32), tap[2][:, : coarse - step]], axis=1)
    ).reshape(micros * coarse, quarter)
    grad_hidden_q = jnp.concatenate(exchange(grad_hidden), axis=0)
    grad_embed = (grad_hidden_q.astype(F32) + gelu_grad(embed) * grad_act).astype(BF16)
    grad_table = scatter(gram(onehot, grad_embed), 0)
    return (
        result,
        input_grads,
        grad_table,
        grad_conv,
        grad_res,
        grad_up,
        grad_vectors[0],
        grad_vectors[1],
        grad_qkv.reshape(qkv_weight.shape),
        grad_out,
        grad_vectors[2],
        grad_vectors[3],
        grad_in,
        grad_down,
    )


def solution(mesh):
    wide = P(("cond", "seq"))
    acts = P(None, "seq", "cond")
    weights = (
        P("seq", "cond"),
        P(None, "cond", "seq"),
        P("seq", "cond"),
        P("cond", "seq"),
        wide,
        wide,
        P("seq", None, "cond"),
        P("cond", "seq"),
        wide,
        wide,
        P("seq", "cond"),
        P("cond", "seq"),
    )
    return jax.shard_map(
        on_device,
        mesh=mesh,
        in_specs=(acts, P(None, "seq"), P(None, "seq"), acts) + weights,
        out_specs=(acts, acts) + weights,
        check_vma=False,
    )
```

```python
import math

import jax
import jax.numpy as jnp
from jax import lax
from jax.experimental import pallas as pl
from jax.experimental.pallas import tpu as pltpu
from jax.sharding import PartitionSpec as P

HEAD = 64
ROW = 64
CONV_DILATION = 27
EPSILON = 1e-05
NEG_FILL = -1e30
LANES = 128
BF16 = jnp.bfloat16
F32 = jnp.float32


def tuned():
    return lax.axis_size("seq") == 8


def swap(x, j):
    return lax.ppermute(x, "cond", [(i, i ^ j) for i in range(4)])


def hop(x, k):
    return lax.ppermute(x, "seq", [(i, i ^ k) for i in range(8)])


def place():
    c = lax.axis_index("cond")
    if tuned():
        s = lax.axis_index("seq")
        return c, s >> 1, s & 1
    zero = jnp.zeros((), jnp.int32)
    return c, zero, zero


def dot(a, b, dims=((1,), (0,))):
    return lax.dot_general(a, b, (dims, ((), ())), preferred_element_type=F32)


def gram(a, b):
    return dot(a, b, ((0,), (0,)))


def dot_t(a, b):
    return dot(a, b, ((1,), (1,)))


def gelu(v):
    return 0.5 * v * (1.0 + lax.erf(v * math.sqrt(0.5)))


def gelu_grad(v):
    return 0.5 * (1.0 + lax.erf(v * math.sqrt(0.5))) + v * (
        math.sqrt(0.5 / math.pi) * jnp.exp(-0.5 * v * v)
    )


def pick(items, t):
    low, high = (t & 1) == 1, (t & 2) == 2
    items = [jnp.where(low, items[i ^ 1], items[i]) for i in range(4)]
    return [jnp.where(high, items[i ^ 2], items[i]) for i in range(4)]


def regroup(x, dim, outer, inner):
    n = x.shape[dim] // 8
    shape = x.shape
    x = x.reshape(shape[:dim] + (outer, inner, n) + shape[dim + 1 :])
    return jnp.swapaxes(x, dim, dim + 1).reshape(shape)


def gather(shard, dim):
    if tuned():
        near = jnp.concatenate([shard] + [hop(shard, 2 * k) for k in (1, 2, 3)], axis=dim)
        return jnp.concatenate([near, hop(near, 1)], axis=dim)
    return regroup(lax.all_gather(shard, "seq", axis=dim, tiled=True), dim, 4, 2)


def scatter(full, dim):
    full = full.astype(BF16)
    if tuned():
        near, far = jnp.split(full, 2, axis=dim)
        near = near.astype(F32) + hop(far, 1).astype(F32)
        parts = jnp.split(near, 4, axis=dim)
        total = parts[0]
        for k in (1, 2, 3):
            total = total + hop(parts[k].astype(BF16), 2 * k).astype(F32)
        return total
    return lax.psum_scatter(
        regroup(full, dim, 2, 4), "seq", scatter_dimension=dim, tiled=True
    ).astype(F32)


def spread(x):
    y = swap(x, 2)
    return [x, swap(x, 1), y, swap(y, 1)]


def exchange(items):
    return [items[0]] + [swap(items[j], j) for j in (1, 2, 3)]


def fold(items, wire=BF16, place_rows=None):
    fix = place_rows or (lambda x, j: x)
    one = fix(swap(items[1].astype(wire), 1), 1).astype(F32)
    three = fix(swap(items[3].astype(wire), 1), 1).astype(F32)
    zero = items[0].astype(F32) + one
    two = (items[2].astype(F32) + three).astype(BF16)
    return zero + fix(swap(two, 2), 2).astype(F32)


def lane_block(i):
    return pl.ds(pl.multiple_of(i * LANES, LANES), LANES)


def reorder_tile(index_ref, in_ref, out_ref):
    for i in range(in_ref.shape[1] // LANES):
        out_ref[:, i * LANES : (i + 1) * LANES] = in_ref[:, lane_block(index_ref[i])]


def reorder(x, index):
    rows, width = x.shape
    tile = rows // 4
    block = pl.BlockSpec((tile, width), lambda i, index: (i, 0))
    return pl.pallas_call(
        reorder_tile,
        out_shape=jax.ShapeDtypeStruct(x.shape, x.dtype),
        grid_spec=pltpu.PrefetchScalarGridSpec(
            num_scalar_prefetch=1, grid=(4,), in_specs=[block], out_specs=block
        ),
        name="reorder",
    )(index, x)


def copy_two(index_a, index_b, a_ref, b_ref, out_a, out_b):
    out_a[...] = a_ref[...].reshape(out_a.shape)
    out_b[...] = b_ref[...].reshape(out_b.shape)


def unpack_rows(packed, index_a, index_b):
    _, _, n, w = packed.shape
    shape = jax.ShapeDtypeStruct((8 * n, w), packed.dtype)
    out = pl.BlockSpec((n, w), lambda i, a, b: (i, 0))
    return pl.pallas_call(
        copy_two,
        out_shape=(shape, shape),
        grid_spec=pltpu.PrefetchScalarGridSpec(
            num_scalar_prefetch=2,
            grid=(8,),
            in_specs=[
                pl.BlockSpec((1, 1, n, w), lambda i, a, b: (a[i], 0, 0, 0)),
                pl.BlockSpec((1, 1, n, w), lambda i, a, b: (b[i], 1, 0, 0)),
            ],
            out_specs=(out, out),
        ),
        name="unpack_rows",
    )(index_a, index_b, packed, packed)


def copy_pair(index_a, index_b, a_ref, b_ref, out_ref):
    out_ref[0, 0] = a_ref[...]
    out_ref[0, 1] = b_ref[...]


def pack_rows(a, b, index_a, index_b):
    n, w = a.shape[0] // 8, a.shape[1]
    return pl.pallas_call(
        copy_pair,
        out_shape=jax.ShapeDtypeStruct((8, 2, n, w), a.dtype),
        grid_spec=pltpu.PrefetchScalarGridSpec(
            num_scalar_prefetch=2,
            grid=(8,),
            in_specs=[
                pl.BlockSpec((n, w), lambda i, a, b: (a[i], 0)),
                pl.BlockSpec((n, w), lambda i, a, b: (b[i], 0)),
            ],
            out_specs=pl.BlockSpec((1, 2, n, w), lambda i, a, b: (i, 0, 0, 0)),
        ),
        name="pack_rows",
    )(index_a, index_b, a, b)


VMEM_ROOM = 48 * 1024 * 1024


def enter_body(from_up, to_layer, up_ref, q0, q1, q2, q3, out_ref, held, spaced):
    coarse = up_ref.shape[0]
    quarter = q0.shape[1]
    for j, ref in enumerate((q0, q1, q2, q3)):
        held[:, j * quarter : (j + 1) * quarter] = ref[...]
    for r in range(4):
        for p in range(8):
            spaced[p, pl.ds(r, coarse, stride=4), :] = up_ref[:, lane_block(from_up[r * 8 + p])]
    for p in range(8):
        out_ref[:, p * LANES : (p + 1) * LANES] = spaced[p] + held[
            :, lane_block(to_layer[p])
        ].astype(F32)


def enter(up_terms, quarters, from_up, to_layer):
    coarse, wide = up_terms.shape
    whole = lambda shape: pl.BlockSpec(shape, lambda i, a, b: (0, 0))
    tokens, quarter = quarters[0].shape
    return pl.pallas_call(
        enter_body,
        out_shape=jax.ShapeDtypeStruct((tokens, wide // 4), F32),
        grid_spec=pltpu.PrefetchScalarGridSpec(
            num_scalar_prefetch=2,
            grid=(1,),
            in_specs=[whole((coarse, wide))] + [whole((tokens, quarter))] * 4,
            out_specs=whole((tokens, wide // 4)),
            scratch_shapes=[
                pltpu.VMEM((tokens, wide // 4), BF16),
                pltpu.VMEM((8, tokens, LANES), F32),
            ],
        ),
        compiler_params=pltpu.CompilerParams(vmem_limit_bytes=VMEM_ROOM),
        name="enter",
    )(from_up, to_layer, up_terms, *quarters)


def leave_body(to_up, to_quarters, in_ref, rows_ref, q0, q1, q2, q3, spaced):
    coarse = rows_ref.shape[0]
    for p in range(8):
        spaced[p] = in_ref[:, p * LANES : (p + 1) * LANES]
    for i in range(32):
        source = to_up[i]
        rows_ref[:, i * LANES : (i + 1) * LANES] = spaced[
            source & 7, pl.ds(source >> 3, coarse, stride=4), :
        ].astype(BF16)
    for j, ref in enumerate((q0, q1, q2, q3)):
        for half in range(2):
            ref[:, half * LANES : (half + 1) * LANES] = in_ref[
                :, lane_block(to_quarters[2 * j + half])
            ].astype(BF16)


def leave(grad, to_up, to_quarters):
    tokens, width = grad.shape
    whole = lambda shape: pl.BlockSpec(shape, lambda i, a, b: (0, 0))
    shapes = [(tokens // 4, 4 * width)] + [(tokens, width // 4)] * 4
    return pl.pallas_call(
        leave_body,
        out_shape=[jax.ShapeDtypeStruct(shape, BF16) for shape in shapes],
        grid_spec=pltpu.PrefetchScalarGridSpec(
            num_scalar_prefetch=2,
            grid=(1,),
            in_specs=[whole((tokens, width))],
            out_specs=[whole(shape) for shape in shapes],
            scratch_shapes=[pltpu.VMEM((8, tokens, LANES), F32)],
        ),
        compiler_params=pltpu.CompilerParams(vmem_limit_bytes=VMEM_ROOM),
        name="leave",
    )(to_up, to_quarters, grad)


TILE = 128
SCALE = 1.0 / math.sqrt(HEAD)


def by_head(x):
    heads = x.shape[1] // HEAD
    feature = lax.broadcasted_iota(jnp.int32, x.shape, 1) // HEAD
    return jnp.concatenate(
        [jnp.where(feature == h, x, jnp.zeros_like(x)) for h in range(heads)], axis=0
    )


def of_heads(x):
    heads = x.shape[1] // HEAD
    feature = lax.broadcasted_iota(jnp.int32, (TILE, x.shape[1]), 1) // HEAD
    out = x[:TILE]
    for h in range(1, heads):
        out = jnp.where(feature == h, x[h * TILE : (h + 1) * TILE], out)
    return out


def visible(column, row):
    i = lax.broadcasted_iota(jnp.int32, (TILE, TILE), 0)
    j = lax.broadcasted_iota(jnp.int32, (TILE, TILE), 1)
    return (column == row) & (i >= j) & (i // ROW == j // ROW)


def soft(query, keys, allowed):
    scores = dot_t(query, keys) * SCALE
    probs = []
    for h in range(scores.shape[1] // TILE):
        part = jnp.where(allowed, scores[:, h * TILE : (h + 1) * TILE], NEG_FILL)
        exps = jnp.exp(part - jnp.max(part, axis=1, keepdims=True))
        probs.append(exps * (1.0 / jnp.sum(exps, axis=1, keepdims=True)))
    return probs


def attend_body(column_ref, row_ref, *refs):
    allowed = visible(column_ref[...], row_ref[0])
    for qkv_ref, out_ref in zip(refs[:4], refs[4:]):
        n = out_ref.shape[1]
        probs = soft(qkv_ref[:, :n], by_head(qkv_ref[:, n : 2 * n]), allowed)
        low = jnp.concatenate([p.astype(BF16) for p in probs], axis=1)
        out_ref[...] = dot(low, by_head(qkv_ref[:, 2 * n :])).astype(BF16)


def attend_back_body(column_ref, row_ref, *refs):
    allowed = visible(column_ref[...], row_ref[0])
    for qkv_ref, grad_ref, out_ref in zip(refs[:4], refs[4:8], refs[8:]):
        n = grad_ref.shape[1]
        query, grad = qkv_ref[:, :n], grad_ref[...]
        keys = by_head(qkv_ref[:, n : 2 * n])
        probs = soft(query, keys, allowed)
        grad_probs = dot_t(grad, by_head(qkv_ref[:, 2 * n :]))
        grads = []
        for h, p in enumerate(probs):
            part = grad_probs[:, h * TILE : (h + 1) * TILE]
            inner = jnp.sum(p * part, axis=1, keepdims=True)
            grads.append((p * (part - inner)).astype(BF16))
        grads = jnp.concatenate(grads, axis=1)
        low = jnp.concatenate([p.astype(BF16) for p in probs], axis=1)
        out_ref[:, :n] = (dot(grads, keys) * SCALE).astype(BF16)
        out_ref[:, n : 2 * n] = (of_heads(gram(grads, query)) * SCALE).astype(BF16)
        out_ref[:, 2 * n :] = of_heads(gram(low, grad)).astype(BF16)


def tiled_call(body, segments, arrays, widths, name):
    tokens = arrays[0].shape[0]
    tiles = tokens // TILE
    wide = lambda w: pl.BlockSpec((TILE, w), lambda i: (i, 0))
    return pl.pallas_call(
        body,
        out_shape=[jax.ShapeDtypeStruct((tokens, w), BF16) for w in widths],
        grid=(tiles,),
        in_specs=[wide(1), pl.BlockSpec((1, 1, TILE), lambda i: (i, 0, 0))]
        + [wide(a.shape[1]) for a in arrays],
        out_specs=[wide(w) for w in widths],
        compiler_params=pltpu.CompilerParams(vmem_limit_bytes=VMEM_ROOM),
        name=name,
    )(segments.reshape(tokens, 1), segments.reshape(tiles, 1, TILE), *arrays)


def attend(qkv, segments):
    return tiled_call(attend_body, segments, qkv, [q.shape[1] // 3 for q in qkv], "attend")


def attend_back(qkv, grads, segments):
    return tiled_call(
        attend_back_body, segments, (*qkv, *grads), [q.shape[1] for q in qkv], "attend_back"
    )


def normalize(stream):
    mean = jnp.mean(stream, axis=1, keepdims=True)
    centred = stream - mean
    rstd = lax.rsqrt(jnp.mean(centred * centred, axis=1, keepdims=True) + EPSILON)
    return centred * rstd, rstd


def normalize_back(normed, rstd, gain, grad):
    scaled = grad * gain
    back = rstd * (
        scaled
        - jnp.mean(scaled, axis=1, keepdims=True)
        - normed * jnp.mean(scaled * normed, axis=1, keepdims=True)
    )
    return back, jnp.sum(grad * normed, axis=0), jnp.sum(grad, axis=0)


def vector_owner(c, z, x):
    i = jnp.arange(32)
    kx, kz, part = i >> 4, (i >> 2) & 3, i & 3
    j = kz ^ z ^ c
    source = ((kx ^ x) << 2) | part
    if tuned():
        piece = j * 8 + ((((source & 1) ^ x) << 2) | ((source >> 1) ^ z))
    else:
        piece = j * 8 + source
    return piece[:, None] == jnp.arange(32)[None, :]


def gather_vectors(vectors, c, z, x):
    pieces = lax.all_gather(vectors, "seq", axis=1, tiled=True) if not tuned() else gather(vectors, 1)
    pieces = jnp.stack(spread(pieces), axis=1)
    count, _, width = pieces.shape
    pieces = pieces.reshape(count, 32, width // 8)
    owner = vector_owner(c, z, x).astype(BF16)
    full = jnp.einsum("dp,vpn->vdn", owner, pieces, preferred_element_type=F32)
    return full.reshape(count, 4 * width)


def scatter_vectors(full, c, z, x):
    count, width = full.shape
    owner = vector_owner(c, z, x).astype(F32)
    pieces = jnp.einsum(
        "dp,vdn->vpn",
        owner,
        full.reshape(count, 32, width // 32),
        precision=lax.Precision.HIGHEST,
        preferred_element_type=F32,
    ).reshape(count, 4, width // 4)
    mine = fold([pieces[:, j] for j in range(4)], F32)
    if tuned():
        return scatter(mine, 1)
    return lax.psum_scatter(mine, "seq", scatter_dimension=1, tiled=True)


def join_rows(packed):
    pieces, _, n, w = packed.shape
    return (
        packed.reshape(8, pieces // 8, 2, n, w).swapaxes(1, 2).reshape(8, 2, n * pieces // 8, w)
    )


def split_rows(packed):
    _, _, n, w = packed.shape
    share = lax.axis_size("seq") // 8
    return (
        packed.reshape(8, 2, share, n // share, w).swapaxes(1, 2).reshape(8 * share, 2, n // share, w)
    )


def edges(cells):
    count = lax.axis_size("seq")
    head, tail = cells
    return (
        lax.ppermute(tail, "seq", [(i, i + 1) for i in range(count - 1)]),
        lax.ppermute(head, "seq", [(i + 1, i) for i in range(count - 1)]),
    )


def on_device(
    inputs,
    coarse_ids,
    segment_ids,
    cotangent,
    embed_table,
    conv_weight,
    res_weight,
    up_weight,
    gain_one,
    shift_one,
    qkv_weight,
    out_weight,
    gain_two,
    shift_two,
    in_weight,
    down_weight,
):
    c, z, x = place()
    turn = c ^ z
    micros, tokens, quarter = inputs.shape
    width = 4 * quarter
    coarse = coarse_ids.shape[1]
    half = width // 2
    step = CONV_DILATION
    slot = jnp.arange(8, dtype=jnp.int32)
    to_layer = (((slot & 3) ^ turn) << 1) | ((slot >> 2) ^ x)
    to_quarters = (((slot & 1) ^ x) << 2) | ((slot >> 1) ^ turn)
    natural_of_layer = (((slot & 3) ^ z) << 1) | ((slot >> 2) ^ x)
    natural_of_quarters = (((slot >> 1) ^ c) << 1) | (slot & 1)
    layer_of_natural = (((slot & 1) ^ x) << 2) | ((slot >> 1) ^ z)
    quarters_of_natural = natural_of_quarters

    table = gather(embed_table, 0)
    conv = gather(conv_weight.reshape(3 * quarter, -1), 1)
    res = spread(gather(res_weight, 0))
    up = spread(gather(up_weight, 1))
    vectors = gather_vectors(jnp.stack([gain_one, shift_one, gain_two, shift_two]), c, z, x)
    qkv_w = spread(gather(qkv_weight.reshape(-1, 3 * quarter), 0))
    out_w = spread(gather(out_weight, 1))
    mlp_w = lax.all_gather(jnp.stack([in_weight, down_weight.T]), "seq", axis=0)
    mlp_w = join_rows(mlp_w)
    in_w, down_t = unpack_rows(mlp_w, natural_of_layer, natural_of_quarters)
    gain1, shift1, gain2, shift2 = (vectors[i][None, :] for i in range(4))

    mine = pick([inputs[i] for i in range(4)], c)
    stream_in = exchange(mine)
    cot = jnp.concatenate(pick([cotangent[i] for i in range(4)], c), axis=0)
    cots = [item.reshape(micros, tokens, quarter) for item in spread(cot)]
    cot_all = jnp.concatenate(
        [jnp.concatenate([cots[j][m ^ j] for m in range(4)], axis=0) for j in range(4)], axis=1
    )
    cot_mine = reorder(cot_all[:tokens], to_layer)

    ids = jnp.concatenate(pick([coarse_ids[i] for i in range(4)], c))
    vocab = table.shape[0]
    code = jnp.arange(vocab, dtype=jnp.int32)
    block = vocab // 8
    slot_of = code // block
    code = ((((slot_of & 3) ^ z) << 1) | ((slot_of >> 2) ^ x)) * block + code % block
    onehot = (ids[:, None] == code[None, :]).astype(BF16)
    embed = dot(onehot, table)
    act = gelu(embed).astype(BF16).reshape(micros, coarse, quarter)
    before, after = edges((act[:, :step], act[:, coarse - step :]))
    padded = jnp.concatenate([before, act, after], axis=1)
    taps = jnp.concatenate(
        [padded[:, k * step : k * step + coarse] for k in range(3)], axis=2
    ).reshape(micros * coarse, 3 * quarter)
    conv_terms = dot(taps, conv).reshape(micros, coarse, width)
    conv_out = fold([conv_terms[j] for j in range(4)])
    embeds = exchange([e for e in embed.astype(BF16).reshape(micros, coarse, quarter)])

    mixed = gelu(conv_out).astype(BF16)
    hidden = [(embeds[j].astype(F32) + dot(mixed, res[j])).astype(BF16) for j in range(4)]
    up_terms = dot(hidden[0], up[0])
    for j in (1, 2, 3):
        up_terms = up_terms + dot(hidden[j], up[j])
    phase_index = jnp.arange(32, dtype=jnp.int32)
    r, p = phase_index >> 3, phase_index & 7
    bz, bx = (p & 3) ^ z, (p >> 2) ^ x
    from_up = ((bz >> 1) ^ x) * 16 + (r ^ z) * 4 + ((bz & 1) << 1 | bx)
    i = phase_index
    kx, kz, w = i >> 4, (i >> 2) & 3, i & 3
    h = kx ^ x
    bz2, bx2 = (h << 1) | (w >> 1), w & 1
    to_up = (kz ^ z) * 8 + ((bx2 ^ x) << 2 | (bz2 ^ z))
    stream_zero = enter(up_terms, stream_in, from_up, to_layer)
    normed_one, rstd_one = normalize(stream_zero)
    norm_one = (normed_one * gain1 + shift1).astype(BF16)
    segments = lax.dynamic_index_in_dim(segment_ids, c, 0, keepdims=False)
    qkv = [dot(norm_one, qkv_w[j]).astype(BF16) for j in range(4)]
    context = attend(qkv, segments)
    stream_one = stream_zero
    for j in range(4):
        stream_one = stream_one + dot(context[j], out_w[j])
    normed_two, rstd_two = normalize(stream_one)
    norm_two = (normed_two * gain2 + shift2).astype(BF16)

    norm_all = jnp.concatenate(spread(norm_two), axis=0)
    mlp_pre = dot(norm_all, in_w)
    mlp_act = gelu(mlp_pre).astype(BF16)
    grad_down = gram(cot_all, mlp_act).astype(BF16)
    mlp_out = dot_t(mlp_act, down_t)
    stream_q = reorder(stream_one, to_quarters)
    mlp_out = mlp_out.reshape(micros, tokens, width)
    mlp_out = jnp.concatenate([(mlp_out[0] + stream_q)[None], mlp_out[1:]], axis=0)
    result = fold(
        [mlp_out[:, :, j * quarter : (j + 1) * quarter] for j in range(4)],
        place_rows=lambda v, j: jnp.stack([v[m ^ j] for m in range(4)]),
    ).astype(BF16)
    result = jnp.stack(pick([result[m] for m in range(4)], c))

    grad_pre = (gelu_grad(mlp_pre) * dot(cot_all, down_t)).astype(BF16)
    grad_in = gram(norm_all, grad_pre).astype(BF16)
    grad_mlp = pack_rows(grad_in, grad_down, layer_of_natural, quarters_of_natural)
    grad_mlp = lax.psum_scatter(split_rows(grad_mlp), "seq", scatter_dimension=0, tiled=False)
    grad_in, grad_down = grad_mlp[0].astype(F32), grad_mlp[1].astype(F32).T
    grad_norm_two = dot_t(grad_pre, in_w).reshape(micros, tokens, width)
    grad_norm_two = fold([grad_norm_two[j] for j in range(4)])

    back_two, grad_gain2, grad_shift2 = normalize_back(normed_two, rstd_two, gain2, grad_norm_two)
    grad_stream_one = cot_mine.astype(F32) + back_two
    grad_att = grad_stream_one.astype(BF16)
    grad_out = scatter(fold([gram(context[j], grad_att) for j in range(4)]), 1)
    grad_context = [dot_t(grad_att, out_w[j]).astype(BF16) for j in range(4)]
    grad_rows = attend_back(qkv, grad_context, segments)
    grad_qkv = scatter(fold([gram(norm_one, grad_rows[j]) for j in range(4)]), 0)
    grad_norm_one = dot_t(grad_rows[0], qkv_w[0])
    for j in (1, 2, 3):
        grad_norm_one = grad_norm_one + dot_t(grad_rows[j], qkv_w[j])
    back_one, grad_gain1, grad_shift1 = normalize_back(normed_one, rstd_one, gain1, grad_norm_one)
    input_grad = grad_stream_one + back_one
    grad_vectors = scatter_vectors(
        jnp.stack([grad_gain1, grad_shift1, grad_gain2, grad_shift2]), c, z, x
    )
    grad_up_rows, *grad_in_q = leave(input_grad, to_up, to_quarters)
    input_grads = jnp.stack(pick(exchange(grad_in_q), c))
    grad_up = scatter(fold([gram(hidden[j], grad_up_rows) for j in range(4)]), 1)
    grad_hidden = [dot_t(grad_up_rows, up[j]).astype(BF16) for j in range(4)]
    grad_res = scatter(fold([gram(mixed, grad_hidden[j]) for j in range(4)]), 0)
    grad_mixed = dot_t(grad_hidden[0], res[0])
    for j in (1, 2, 3):
        grad_mixed = grad_mixed + dot_t(grad_hidden[j], res[j])
    grad_conv_low = (gelu_grad(conv_out) * grad_mixed).astype(BF16)

    grad_conv_all = jnp.concatenate(spread(grad_conv_low), axis=0)
    grad_conv = scatter(gram(taps, grad_conv_all), 1).reshape(conv_weight.shape)
    grad_taps = dot_t(grad_conv_all, conv).reshape(micros, coarse, 3 * quarter)
    tap = [grad_taps[:, :, k * quarter : (k + 1) * quarter] for k in range(3)]
    before, after = edges((tap[0][:, :step].astype(BF16), tap[2][:, coarse - step :].astype(BF16)))
    blank = jnp.zeros((micros, coarse - step, quarter), F32)
    grad_act = (
        tap[1]
        + jnp.concatenate([tap[0][:, step:], after.astype(F32)], axis=1)
        + jnp.concatenate([before.astype(F32), tap[2][:, : coarse - step]], axis=1)
    ).reshape(micros * coarse, quarter)
    grad_hidden_q = jnp.concatenate(exchange(grad_hidden), axis=0)
    grad_embed = (grad_hidden_q.astype(F32) + gelu_grad(embed) * grad_act).astype(BF16)
    grad_table = scatter(gram(onehot, grad_embed), 0)
    return (
        result,
        input_grads,
        grad_table,
        grad_conv,
        grad_res,
        grad_up,
        grad_vectors[0],
        grad_vectors[1],
        grad_qkv.reshape(qkv_weight.shape),
        grad_out,
        grad_vectors[2],
        grad_vectors[3],
        grad_in,
        grad_down,
    )


def solution(mesh):
    wide = P(("cond", "seq"))
    acts = P(None, "seq", "cond")
    weights = (
        P("seq", "cond"),
        P(None, "cond", "seq"),
        P("seq", "cond"),
        P("cond", "seq"),
        wide,
        wide,
        P("seq", None, "cond"),
        P("cond", "seq"),
        wide,
        wide,
        P("seq", "cond"),
        P("cond", "seq"),
    )
    return jax.shard_map(
        on_device,
        mesh=mesh,
        in_specs=(acts, P(None, "seq"), P(None, "seq"), acts) + weights,
        out_specs=(acts, acts) + weights,
        check_vma=False,
    )
```

```python
import math

import jax
import jax.numpy as jnp
from jax import lax
from jax.experimental import pallas as pl
from jax.experimental.pallas import tpu as pltpu
from jax.sharding import PartitionSpec as P

HEAD = 64
ROW = 64
CONV_DILATION = 27
EPSILON = 1e-05
NEG_FILL = -1e30
LANES = 128
BF16 = jnp.bfloat16
F32 = jnp.float32


def tuned():
    return lax.axis_size("seq") == 8


def swap(x, j):
    return lax.ppermute(x, "cond", [(i, i ^ j) for i in range(4)])


def hop(x, k):
    return lax.ppermute(x, "seq", [(i, i ^ k) for i in range(8)])


def place():
    c = lax.axis_index("cond")
    return c, (lax.axis_index("seq") & 1 if tuned() else jnp.zeros((), jnp.int32))


def after(value, *before):
    return lax.optimization_barrier((value, *before))[0]


def dot(a, b, dims=((1,), (0,))):
    return lax.dot_general(a, b, (dims, ((), ())), preferred_element_type=F32)


def gram(a, b):
    return dot(a, b, ((0,), (0,)))


def dot_t(a, b):
    return dot(a, b, ((1,), (1,)))


def gelu(v):
    return 0.5 * v * (1.0 + lax.erf(v * math.sqrt(0.5)))


def gelu_grad(v):
    return 0.5 * (1.0 + lax.erf(v * math.sqrt(0.5))) + v * (
        math.sqrt(0.5 / math.pi) * jnp.exp(-0.5 * v * v)
    )


def pick(items, t):
    low, high = (t & 1) == 1, (t & 2) == 2
    items = [jnp.where(low, items[i ^ 1], items[i]) for i in range(4)]
    return [jnp.where(high, items[i ^ 2], items[i]) for i in range(4)]


def regroup(x, dim, outer, inner):
    n = x.shape[dim] // 8
    shape = x.shape
    x = x.reshape(shape[:dim] + (outer, inner, n) + shape[dim + 1 :])
    return jnp.swapaxes(x, dim, dim + 1).reshape(shape)


CELL = 256
ALONG_Z = [[0, 2, 4, 6], [1, 3, 5, 7]]
VMEM_ROOM = 48 * 1024 * 1024


def bundle(shards):
    return jnp.concatenate(
        [s[:, i : i + CELL] for s in shards for i in range(0, s.shape[1], CELL)], axis=0
    )


def along_z(x):
    return lax.all_to_all(x, "seq", 0, 0, axis_index_groups=ALONG_Z, tiled=True)


def unpack_body(shapes, near_ref, far_ref, *outs):
    p = pl.program_id(0)

    def copy(ref):
        at = 0
        for (r, w), out in zip(shapes, outs):
            for i in range(0, w, CELL):
                out[:, i : i + CELL] = ref[0, at : at + r]
                at += r

    pl.when(p < 4)(lambda: copy(near_ref))
    pl.when(p >= 4)(lambda: copy(far_ref))


def unpack(near, far, shapes):
    block = (1,) + near.shape[1:]
    return pl.pallas_call(
        lambda *refs: unpack_body(shapes, *refs),
        out_shape=[jax.ShapeDtypeStruct((8 * r, w), near.dtype) for r, w in shapes],
        grid=(8,),
        in_specs=[
            pl.BlockSpec(block, lambda p: (jnp.minimum(p, 3), 0, 0)),
            pl.BlockSpec(block, lambda p: (jnp.maximum(p - 4, 0), 0, 0)),
        ],
        out_specs=[pl.BlockSpec((r, w), lambda p: (p, 0)) for r, w in shapes],
        compiler_params=pltpu.CompilerParams(vmem_limit_bytes=VMEM_ROOM),
        name="unpack",
    )(near, far)


def gather_plain(shards):
    return [regroup(lax.all_gather(s, "seq", axis=0, tiled=True), 0, 4, 2) for s in shards]


def pack_body(shapes, *refs):
    out = refs[-1]
    at = 0
    for (r, w), near, far in zip(shapes, refs[0::2], refs[1::2]):
        total = (near[...].astype(F32) + far[...].astype(F32)).astype(BF16)
        for i in range(0, w, CELL):
            out[0, at : at + r] = total[:, i : i + CELL]
            at += r


def pack(nears, fars):
    shapes = [(f.shape[0] // 4, f.shape[1]) for f in fars]
    rows = sum(r * w for r, w in shapes) // CELL
    specs = [pl.BlockSpec((r, w), lambda p: (p, 0)) for r, w in shapes for _ in range(2)]
    return pl.pallas_call(
        lambda *refs: pack_body(shapes, *refs),
        out_shape=jax.ShapeDtypeStruct((4, rows, CELL), BF16),
        grid=(4,),
        in_specs=specs,
        out_specs=pl.BlockSpec((1, rows, CELL), lambda p: (p, 0, 0)),
        compiler_params=pltpu.CompilerParams(vmem_limit_bytes=VMEM_ROOM),
        name="pack",
    )(*[x for pair in zip(nears, fars) for x in pair])


def total_body(shapes, in_ref, *outs):
    at = 0
    for (r, w), out in zip(shapes, outs):
        for i in range(0, w, CELL):
            cells = [in_ref[k, at : at + r].astype(F32) for k in range(4)]
            out[:, i : i + CELL] = (cells[0] + cells[1]) + (cells[2] + cells[3])
            at += r


def total(parts, shapes):
    return pl.pallas_call(
        lambda *refs: total_body(shapes, *refs),
        out_shape=[jax.ShapeDtypeStruct(shape, F32) for shape in shapes],
        compiler_params=pltpu.CompilerParams(vmem_limit_bytes=VMEM_ROOM),
        name="total",
    )(parts)


def reduce_rows(grads):
    if tuned():
        grads = [g.astype(BF16) for g in grads]
        fars = [hop(g[g.shape[0] // 2 :], 1) for g in grads]
        shapes = [(g.shape[0] // 8, g.shape[1]) for g in grads]
        return total(along_z(pack(grads, fars)), shapes)
    return [
        lax.psum_scatter(
            regroup(g.astype(BF16), 0, 2, 4), "seq", scatter_dimension=0, tiled=True
        ).astype(F32)
        for g in grads
    ]


def spread(x):
    y = swap(x, 2)
    return [x, swap(x, 1), y, swap(y, 1)]


def exchange(items):
    return [items[0]] + [swap(items[j], j) for j in (1, 2, 3)]


def fold(items, wire=BF16, place_rows=None):
    fix = place_rows or (lambda x, j: x)
    one = fix(swap(items[1].astype(wire), 1), 1).astype(F32)
    three = fix(swap(items[3].astype(wire), 1), 1).astype(F32)
    zero = items[0].astype(F32) + one
    two = (items[2].astype(F32) + three).astype(BF16)
    return zero + fix(swap(two, 2), 2).astype(F32)


def lane_block(i):
    return pl.ds(pl.multiple_of(i * LANES, LANES), LANES)


def reorder_tile(index_ref, in_ref, out_ref):
    for i in range(in_ref.shape[1] // LANES):
        out_ref[:, i * LANES : (i + 1) * LANES] = in_ref[:, lane_block(index_ref[i])]


def reorder(x, index):
    rows, width = x.shape
    tile = rows // 4
    block = pl.BlockSpec((tile, width), lambda i, index: (i, 0))
    return pl.pallas_call(
        reorder_tile,
        out_shape=jax.ShapeDtypeStruct(x.shape, x.dtype),
        grid_spec=pltpu.PrefetchScalarGridSpec(
            num_scalar_prefetch=1, grid=(4,), in_specs=[block], out_specs=block
        ),
        name="reorder",
    )(index, x)


def copy_two(index_a, index_b, a_ref, b_ref, out_a, out_b):
    out_a[...] = a_ref[...].reshape(out_a.shape)
    out_b[...] = b_ref[...].reshape(out_b.shape)


def unpack_rows(packed, index_a, index_b):
    _, _, n, w = packed.shape
    shape = jax.ShapeDtypeStruct((8 * n, w), packed.dtype)
    out = pl.BlockSpec((n, w), lambda i, a, b: (i, 0))
    return pl.pallas_call(
        copy_two,
        out_shape=(shape, shape),
        grid_spec=pltpu.PrefetchScalarGridSpec(
            num_scalar_prefetch=2,
            grid=(8,),
            in_specs=[
                pl.BlockSpec((1, 1, n, w), lambda i, a, b: (a[i], 0, 0, 0)),
                pl.BlockSpec((1, 1, n, w), lambda i, a, b: (b[i], 1, 0, 0)),
            ],
            out_specs=(out, out),
        ),
        name="unpack_rows",
    )(index_a, index_b, packed, packed)


def copy_pair(index_a, index_b, a_ref, b_ref, out_ref):
    out_ref[0, 0] = a_ref[...]
    out_ref[0, 1] = b_ref[...]


def pack_rows(a, b, index_a, index_b):
    n, w = a.shape[0] // 8, a.shape[1]
    return pl.pallas_call(
        copy_pair,
        out_shape=jax.ShapeDtypeStruct((8, 2, n, w), a.dtype),
        grid_spec=pltpu.PrefetchScalarGridSpec(
            num_scalar_prefetch=2,
            grid=(8,),
            in_specs=[
                pl.BlockSpec((n, w), lambda i, a, b: (a[i], 0)),
                pl.BlockSpec((n, w), lambda i, a, b: (b[i], 0)),
            ],
            out_specs=pl.BlockSpec((1, 2, n, w), lambda i, a, b: (i, 0, 0, 0)),
        ),
        name="pack_rows",
    )(index_a, index_b, a, b)


def enter_body(from_up, to_layer, up_ref, q0, q1, q2, q3, out_ref, held, spaced):
    coarse = up_ref.shape[0]
    quarter = q0.shape[1]
    for j, ref in enumerate((q0, q1, q2, q3)):
        held[:, j * quarter : (j + 1) * quarter] = ref[...]
    for r in range(4):
        for p in range(8):
            spaced[p, pl.ds(r, coarse, stride=4), :] = up_ref[:, lane_block(from_up[r * 8 + p])]
    for p in range(8):
        out_ref[:, p * LANES : (p + 1) * LANES] = spaced[p] + held[
            :, lane_block(to_layer[p])
        ].astype(F32)


def enter(up_terms, quarters, from_up, to_layer):
    coarse, wide = up_terms.shape
    whole = lambda shape: pl.BlockSpec(shape, lambda i, a, b: (0, 0))
    tokens, quarter = quarters[0].shape
    return pl.pallas_call(
        enter_body,
        out_shape=jax.ShapeDtypeStruct((tokens, wide // 4), F32),
        grid_spec=pltpu.PrefetchScalarGridSpec(
            num_scalar_prefetch=2,
            grid=(1,),
            in_specs=[whole((coarse, wide))] + [whole((tokens, quarter))] * 4,
            out_specs=whole((tokens, wide // 4)),
            scratch_shapes=[
                pltpu.VMEM((tokens, wide // 4), BF16),
                pltpu.VMEM((8, tokens, LANES), F32),
            ],
        ),
        compiler_params=pltpu.CompilerParams(vmem_limit_bytes=VMEM_ROOM),
        name="enter",
    )(from_up, to_layer, up_terms, *quarters)


def leave_body(to_up, to_quarters, in_ref, rows_ref, q0, q1, q2, q3, spaced):
    coarse = rows_ref.shape[0]
    for p in range(8):
        spaced[p] = in_ref[:, p * LANES : (p + 1) * LANES]
    for i in range(32):
        source = to_up[i]
        rows_ref[:, i * LANES : (i + 1) * LANES] = spaced[
            source & 7, pl.ds(source >> 3, coarse, stride=4), :
        ].astype(BF16)
    for j, ref in enumerate((q0, q1, q2, q3)):
        for half in range(2):
            ref[:, half * LANES : (half + 1) * LANES] = in_ref[
                :, lane_block(to_quarters[2 * j + half])
            ].astype(BF16)


def leave(grad, to_up, to_quarters):
    tokens, width = grad.shape
    whole = lambda shape: pl.BlockSpec(shape, lambda i, a, b: (0, 0))
    shapes = [(tokens // 4, 4 * width)] + [(tokens, width // 4)] * 4
    return pl.pallas_call(
        leave_body,
        out_shape=[jax.ShapeDtypeStruct(shape, BF16) for shape in shapes],
        grid_spec=pltpu.PrefetchScalarGridSpec(
            num_scalar_prefetch=2,
            grid=(1,),
            in_specs=[whole((tokens, width))],
            out_specs=[whole(shape) for shape in shapes],
            scratch_shapes=[pltpu.VMEM((8, tokens, LANES), F32)],
        ),
        compiler_params=pltpu.CompilerParams(vmem_limit_bytes=VMEM_ROOM),
        name="leave",
    )(to_up, to_quarters, grad)


TILE = 128
SCALE = 1.0 / math.sqrt(HEAD)


def by_head(x):
    heads = x.shape[1] // HEAD
    feature = lax.broadcasted_iota(jnp.int32, x.shape, 1) // HEAD
    return jnp.concatenate(
        [jnp.where(feature == h, x, jnp.zeros_like(x)) for h in range(heads)], axis=0
    )


def of_heads(x):
    heads = x.shape[1] // HEAD
    feature = lax.broadcasted_iota(jnp.int32, (TILE, x.shape[1]), 1) // HEAD
    out = x[:TILE]
    for h in range(1, heads):
        out = jnp.where(feature == h, x[h * TILE : (h + 1) * TILE], out)
    return out


def visible(column, row):
    i = lax.broadcasted_iota(jnp.int32, (TILE, TILE), 0)
    j = lax.broadcasted_iota(jnp.int32, (TILE, TILE), 1)
    return (column == row) & (i >= j) & (i // ROW == j // ROW)


def soft(query, keys, allowed):
    scores = dot_t(query, keys) * SCALE
    probs = []
    for h in range(scores.shape[1] // TILE):
        part = jnp.where(allowed, scores[:, h * TILE : (h + 1) * TILE], NEG_FILL)
        exps = jnp.exp(part - jnp.max(part, axis=1, keepdims=True))
        probs.append(exps * (1.0 / jnp.sum(exps, axis=1, keepdims=True)))
    return probs


def attend_body(column_ref, row_ref, *refs):
    allowed = visible(column_ref[...], row_ref[0])
    for qkv_ref, out_ref in zip(refs[:4], refs[4:]):
        n = out_ref.shape[1]
        probs = soft(qkv_ref[:, :n], by_head(qkv_ref[:, n : 2 * n]), allowed)
        low = jnp.concatenate([p.astype(BF16) for p in probs], axis=1)
        out_ref[...] = dot(low, by_head(qkv_ref[:, 2 * n :])).astype(BF16)


def attend_back_body(column_ref, row_ref, *refs):
    allowed = visible(column_ref[...], row_ref[0])
    for qkv_ref, grad_ref, out_ref in zip(refs[:4], refs[4:8], refs[8:]):
        n = grad_ref.shape[1]
        query, grad = qkv_ref[:, :n], grad_ref[...]
        keys = by_head(qkv_ref[:, n : 2 * n])
        probs = soft(query, keys, allowed)
        grad_probs = dot_t(grad, by_head(qkv_ref[:, 2 * n :]))
        grads = []
        for h, p in enumerate(probs):
            part = grad_probs[:, h * TILE : (h + 1) * TILE]
            inner = jnp.sum(p * part, axis=1, keepdims=True)
            grads.append((p * (part - inner)).astype(BF16))
        grads = jnp.concatenate(grads, axis=1)
        low = jnp.concatenate([p.astype(BF16) for p in probs], axis=1)
        out_ref[:, :n] = (dot(grads, keys) * SCALE).astype(BF16)
        out_ref[:, n : 2 * n] = (of_heads(gram(grads, query)) * SCALE).astype(BF16)
        out_ref[:, 2 * n :] = of_heads(gram(low, grad)).astype(BF16)


def tiled_call(body, segments, arrays, widths, name):
    tokens = arrays[0].shape[0]
    tiles = tokens // TILE
    wide = lambda w: pl.BlockSpec((TILE, w), lambda i: (i, 0))
    return pl.pallas_call(
        body,
        out_shape=[jax.ShapeDtypeStruct((tokens, w), BF16) for w in widths],
        grid=(tiles,),
        in_specs=[wide(1), pl.BlockSpec((1, 1, TILE), lambda i: (i, 0, 0))]
        + [wide(a.shape[1]) for a in arrays],
        out_specs=[wide(w) for w in widths],
        compiler_params=pltpu.CompilerParams(vmem_limit_bytes=VMEM_ROOM),
        name=name,
    )(segments.reshape(tokens, 1), segments.reshape(tiles, 1, TILE), *arrays)


def attend(qkv, segments):
    return tiled_call(attend_body, segments, qkv, [q.shape[1] // 3 for q in qkv], "attend")


def attend_back(qkv, grads, segments):
    return tiled_call(
        attend_back_body, segments, (*qkv, *grads), [q.shape[1] for q in qkv], "attend_back"
    )


def normalize(stream):
    mean = jnp.mean(stream, axis=1, keepdims=True)
    centred = stream - mean
    rstd = lax.rsqrt(jnp.mean(centred * centred, axis=1, keepdims=True) + EPSILON)
    return centred * rstd, rstd


def normalize_back(normed, rstd, gain, grad):
    scaled = grad * gain
    back = rstd * (
        scaled
        - jnp.mean(scaled, axis=1, keepdims=True)
        - normed * jnp.mean(scaled * normed, axis=1, keepdims=True)
    )
    return back, jnp.sum(grad * normed, axis=0), jnp.sum(grad, axis=0)


def vector_owner(c, x):
    i = jnp.arange(32)
    kx, kz, part = i >> 4, (i >> 2) & 3, i & 3
    source = ((kx ^ x) << 2) | part
    piece = (kz ^ c) * 8 + ((((source & 1) ^ x) << 2) | (source >> 1))
    return piece[:, None] == jnp.arange(32)[None, :]


PAD = 16


def vector_rows(vectors):
    ends = [(0, 0)] * (vectors.ndim - 2)
    count, n = vectors.shape[-2:]
    return jnp.pad(vectors, ends + [(0, PAD - count), (0, CELL - n)])


def join_vectors(spreads, n, c, x):
    pieces = jnp.stack([s.reshape(8, -1, PAD, CELL)[:, :, :4, :n] for s in spreads])
    pieces = pieces.transpose(3, 0, 1, 2, 4).reshape(4, 32, -1)
    owner = vector_owner(c, x).astype(BF16)
    full = jnp.einsum("dp,vpn->vdn", owner, pieces, preferred_element_type=F32)
    return full.reshape(4, -1)


def split_vectors(full, n, c, x):
    owner = vector_owner(c, x).astype(F32)
    pieces = jnp.einsum(
        "dp,vdn->pvn",
        owner,
        full.reshape(4, 32, -1),
        precision=lax.Precision.HIGHEST,
        preferred_element_type=F32,
    )
    pieces = pieces.reshape(4, 8, 4, -1, n).swapaxes(2, 3)
    rows = vector_rows(pieces)
    return [rows[j].reshape(-1, CELL) for j in range(4)]


def cot_body(to_layer, q0, q1, q2, q3, all_ref, mine_ref):
    n = q0.shape[1]
    for j, ref in enumerate((q0, q1, q2, q3)):
        all_ref[:, j * n : (j + 1) * n] = ref[...]

    @pl.when(pl.program_id(0) == 0)
    def _():
        for p in range(8):
            mine_ref[:, p * LANES : (p + 1) * LANES] = all_ref[:, lane_block(to_layer[p])]


def join_cotangent(quarters, to_layer):
    rows, n = quarters[0].shape
    tokens = rows // 4
    return pl.pallas_call(
        cot_body,
        out_shape=(
            jax.ShapeDtypeStruct((rows, 4 * n), BF16),
            jax.ShapeDtypeStruct((tokens, 4 * n), BF16),
        ),
        grid_spec=pltpu.PrefetchScalarGridSpec(
            num_scalar_prefetch=1,
            grid=(4,),
            in_specs=[
                pl.BlockSpec((tokens, n), lambda m, t, j=j: (jnp.bitwise_xor(m, j), 0))
                for j in range(4)
            ],
            out_specs=(
                pl.BlockSpec((tokens, 4 * n), lambda m, t: (m, 0)),
                pl.BlockSpec((tokens, 4 * n), lambda m, t: (0, 0)),
            ),
        ),
        compiler_params=pltpu.CompilerParams(vmem_limit_bytes=VMEM_ROOM),
        name="join_cotangent",
    )(to_layer, *quarters)


def join_rows(packed):
    pieces, _, n, w = packed.shape
    return (
        packed.reshape(8, pieces // 8, 2, n, w).swapaxes(1, 2).reshape(8, 2, n * pieces // 8, w)
    )


def split_rows(packed):
    _, _, n, w = packed.shape
    share = lax.axis_size("seq") // 8
    return (
        packed.reshape(8, 2, share, n // share, w).swapaxes(1, 2).reshape(8 * share, 2, n // share, w)
    )


def edges(cells):
    count = lax.axis_size("seq")
    head, tail = cells
    return (
        lax.ppermute(tail, "seq", [(i, i + 1) for i in range(count - 1)]),
        lax.ppermute(head, "seq", [(i + 1, i) for i in range(count - 1)]),
    )


def on_device(
    inputs,
    coarse_ids,
    segment_ids,
    cotangent,
    embed_table,
    conv_weight,
    res_weight,
    up_weight,
    gain_one,
    shift_one,
    qkv_weight,
    out_weight,
    gain_two,
    shift_two,
    in_weight,
    down_weight,
):
    c, x = place()
    micros, tokens, quarter = inputs.shape
    width = 4 * quarter
    coarse = coarse_ids.shape[1]
    step = CONV_DILATION
    slot = jnp.arange(8, dtype=jnp.int32)
    to_layer = (((slot & 3) ^ c) << 1) | ((slot >> 2) ^ x)
    to_quarters = (((slot & 1) ^ x) << 2) | ((slot >> 1) ^ c)
    natural_of_layer = ((slot & 3) << 1) | ((slot >> 2) ^ x)
    natural_of_quarters = (((slot >> 1) ^ c) << 1) | (slot & 1)
    layer_of_natural = (((slot & 1) ^ x) << 2) | (slot >> 1)
    quarters_of_natural = natural_of_quarters

    stream_in = exchange(pick([inputs[i] for i in range(4)], c))

    lot = gain_one.shape[0]
    vectors = vector_rows(jnp.stack([gain_one, shift_one, gain_two, shift_two]))
    conv_shard = conv_weight.transpose(2, 0, 1).reshape(-1, 3 * quarter)
    groups = (
        (res_weight, up_weight.T, vectors),
        (embed_table, conv_shard),
        (qkv_weight.reshape(-1, 3 * quarter), out_weight.T),
    )
    mlp_shard = jnp.stack([in_weight, down_weight.T])
    if tuned():
        nears, fars = [], []
        for group in groups:
            cells = bundle(group)
            cells = after(cells, nears[-1]) if nears else cells
            nears.append(along_z(jnp.broadcast_to(cells, (4,) + cells.shape)))
        for near in nears:
            fars.append(hop(after(near, fars[-1]) if fars else near, 1))
        whole = [
            unpack(near, far, [w.shape for w in group])
            for near, far, group in zip(nears, fars, groups)
        ]
        mlp_shard = after(mlp_shard, nears[1])
    else:
        whole = [gather_plain(group) for group in groups]
    (res, up, vectors), (table, conv), (qkv_w, out_w) = whole
    over_y = [swap(w, 2) for w in (res, up, vectors)]
    over_y += [swap(after(w, *over_y[:2]), 2) for w in (qkv_w, out_w)]
    res, up, vectors, qkv_w, out_w = (
        [w, swap(w, 1), v, swap(v, 1)]
        for w, v in zip((res, up, vectors, qkv_w, out_w), over_y)
    )
    in_w, down_t = unpack_rows(
        join_rows(lax.all_gather(mlp_shard, "seq", axis=0)), natural_of_layer, natural_of_quarters
    )
    vectors = join_vectors(vectors, lot, c, x)
    gain1, shift1, gain2, shift2 = (vectors[i][None, :] for i in range(4))

    cot = jnp.concatenate(pick([cotangent[i] for i in range(4)], c), axis=0)
    cot_all, cot_mine = join_cotangent(spread(after(cot, *over_y[3:])), to_layer)

    ids = jnp.concatenate(pick([coarse_ids[i] for i in range(4)], c))
    vocab = table.shape[0]
    code = jnp.arange(vocab, dtype=jnp.int32)
    block = vocab // 8
    slot_of = code // block
    code = (((slot_of & 3) << 1) | ((slot_of >> 2) ^ x)) * block + code % block
    onehot = (ids[:, None] == code[None, :]).astype(BF16)
    embed = dot(onehot, table)
    act = gelu(embed).astype(BF16).reshape(micros, coarse, quarter)
    prior, later = edges((act[:, :step], act[:, coarse - step :]))
    padded = jnp.concatenate([prior, act, later], axis=1)
    taps = jnp.concatenate(
        [padded[:, k * step : k * step + coarse] for k in range(3)], axis=2
    ).reshape(micros * coarse, 3 * quarter)
    conv_terms = dot_t(taps, conv).reshape(micros, coarse, width)
    conv_out = fold([conv_terms[j] for j in range(4)])
    embeds = exchange([e for e in embed.astype(BF16).reshape(micros, coarse, quarter)])

    mixed = gelu(conv_out).astype(BF16)
    hidden = [(embeds[j].astype(F32) + dot(mixed, res[j])).astype(BF16) for j in range(4)]
    up_terms = dot_t(hidden[0], up[0])
    for j in (1, 2, 3):
        up_terms = up_terms + dot_t(hidden[j], up[j])
    i = jnp.arange(32, dtype=jnp.int32)
    r, bz, bx = i >> 3, i & 3, ((i >> 2) & 1) ^ x
    from_up = ((bz >> 1) ^ x) * 16 + r * 4 + ((bz & 1) << 1 | bx)
    h, r, w = (i >> 4) ^ x, (i >> 2) & 3, i & 3
    to_up = r * 8 + (((w & 1) ^ x) << 2 | h << 1 | w >> 1)
    stream_zero = enter(up_terms, stream_in, from_up, to_layer)
    normed_one, rstd_one = normalize(stream_zero)
    norm_one = (normed_one * gain1 + shift1).astype(BF16)
    segments = lax.dynamic_index_in_dim(segment_ids, c, 0, keepdims=False)
    qkv = [dot(norm_one, qkv_w[j]).astype(BF16) for j in range(4)]
    context = attend(qkv, segments)
    stream_one = stream_zero
    for j in range(4):
        stream_one = stream_one + dot_t(context[j], out_w[j])
    normed_two, rstd_two = normalize(stream_one)
    norm_two = (normed_two * gain2 + shift2).astype(BF16)

    norm_all = jnp.concatenate(spread(norm_two), axis=0)
    mlp_pre = dot(norm_all, in_w)
    mlp_act = gelu(mlp_pre).astype(BF16)
    grad_down = gram(cot_all, mlp_act).astype(BF16)
    mlp_out = dot_t(mlp_act, down_t)
    stream_q = reorder(stream_one, to_quarters)
    mlp_out = mlp_out.reshape(micros, tokens, width)
    mlp_out = jnp.concatenate([(mlp_out[0] + stream_q)[None], mlp_out[1:]], axis=0)
    result = fold(
        [mlp_out[:, :, j * quarter : (j + 1) * quarter] for j in range(4)],
        place_rows=lambda v, j: jnp.stack([v[m ^ j] for m in range(4)]),
    ).astype(BF16)
    result = jnp.stack(pick([result[m] for m in range(4)], c))

    grad_pre = (gelu_grad(mlp_pre) * dot(cot_all, down_t)).astype(BF16)
    grad_in = gram(norm_all, grad_pre).astype(BF16)
    grad_mlp = pack_rows(grad_in, grad_down, layer_of_natural, quarters_of_natural)
    grad_mlp = lax.psum_scatter(split_rows(grad_mlp), "seq", scatter_dimension=0, tiled=False)
    grad_in, grad_down = grad_mlp[0].astype(F32), grad_mlp[1].astype(F32).T
    grad_norm_two = dot_t(grad_pre, in_w).reshape(micros, tokens, width)
    grad_norm_two = fold([grad_norm_two[j] for j in range(4)])

    back_two, grad_gain2, grad_shift2 = normalize_back(normed_two, rstd_two, gain2, grad_norm_two)
    grad_stream_one = cot_mine.astype(F32) + back_two
    grad_att = grad_stream_one.astype(BF16)
    grad_out = fold([gram(grad_att, context[j]) for j in range(4)])
    grad_context = [dot(grad_att, out_w[j]).astype(BF16) for j in range(4)]
    grad_rows = attend_back(qkv, grad_context, segments)
    grad_qkv, grad_out = reduce_rows(
        [fold([gram(norm_one, grad_rows[j]) for j in range(4)]), grad_out]
    )
    grad_norm_one = dot_t(grad_rows[0], qkv_w[0])
    for j in (1, 2, 3):
        grad_norm_one = grad_norm_one + dot_t(grad_rows[j], qkv_w[j])
    back_one, grad_gain1, grad_shift1 = normalize_back(normed_one, rstd_one, gain1, grad_norm_one)
    input_grad = grad_stream_one + back_one
    grad_vectors = split_vectors(
        jnp.stack([grad_gain1, grad_shift1, grad_gain2, grad_shift2]), lot, c, x
    )
    grad_up_rows, *grad_in_q = leave(input_grad, to_up, to_quarters)
    input_grads = jnp.stack(pick(exchange(grad_in_q), c))
    grad_hidden = [dot(grad_up_rows, up[j]).astype(BF16) for j in range(4)]
    grad_up = fold([gram(grad_up_rows, hidden[j]) for j in range(4)])
    grad_res = fold([gram(mixed, grad_hidden[j]) for j in range(4)])
    grad_res, grad_up, grad_vectors = reduce_rows([grad_res, grad_up, fold(grad_vectors)])
    grad_vectors = [grad_vectors[i, :lot] for i in range(4)]
    grad_mixed = dot_t(grad_hidden[0], res[0])
    for j in (1, 2, 3):
        grad_mixed = grad_mixed + dot_t(grad_hidden[j], res[j])
    grad_conv_low = (gelu_grad(conv_out) * grad_mixed).astype(BF16)

    grad_conv_all = jnp.concatenate(spread(grad_conv_low), axis=0)
    grad_taps = dot(grad_conv_all, conv).reshape(micros, coarse, 3 * quarter)
    tap = [grad_taps[:, :, k * quarter : (k + 1) * quarter] for k in range(3)]
    prior, later = edges((tap[0][:, :step].astype(BF16), tap[2][:, coarse - step :].astype(BF16)))
    grad_act = (
        tap[1]
        + jnp.concatenate([tap[0][:, step:], later.astype(F32)], axis=1)
        + jnp.concatenate([prior.astype(F32), tap[2][:, : coarse - step]], axis=1)
    ).reshape(micros * coarse, quarter)
    grad_hidden_q = jnp.concatenate(exchange(grad_hidden), axis=0)
    grad_embed = (grad_hidden_q.astype(F32) + gelu_grad(embed) * grad_act).astype(BF16)
    grad_table, grad_conv = reduce_rows([gram(onehot, grad_embed), gram(grad_conv_all, taps)])
    grad_conv = grad_conv.reshape(-1, 3, quarter).transpose(1, 2, 0)
    return (
        result,
        input_grads,
        grad_table,
        grad_conv,
        grad_res,
        grad_up.T,
        grad_vectors[0],
        grad_vectors[1],
        grad_qkv.reshape(qkv_weight.shape),
        grad_out.T,
        grad_vectors[2],
        grad_vectors[3],
        grad_in,
        grad_down,
    )


def solution(mesh):
    wide = P(("cond", "seq"))
    acts = P(None, "seq", "cond")
    weights = (
        P("seq", "cond"),
        P(None, "cond", "seq"),
        P("seq", "cond"),
        P("cond", "seq"),
        wide,
        wide,
        P("seq", None, "cond"),
        P("cond", "seq"),
        wide,
        wide,
        P("seq", "cond"),
        P("cond", "seq"),
    )
    return jax.shard_map(
        on_device,
        mesh=mesh,
        in_specs=(acts, P(None, "seq"), P(None, "seq"), acts) + weights,
        out_specs=(acts, acts) + weights,
        check_vma=False,
    )
```

```python
import math

import jax
import jax.numpy as jnp
from jax import lax
from jax.experimental import pallas as pl
from jax.experimental.pallas import tpu as pltpu
from jax.sharding import PartitionSpec as P

HEAD = 64
ROW = 64
CONV_DILATION = 27
EPSILON = 1e-05
NEG_FILL = -1e30
LANES = 128
BF16 = jnp.bfloat16
F32 = jnp.float32


def tuned():
    return lax.axis_size("seq") == 8


def swap(x, j):
    return lax.ppermute(x, "cond", [(i, i ^ j) for i in range(4)])


def hop(x, k):
    return lax.ppermute(x, "seq", [(i, i ^ k) for i in range(8)])


def place():
    c = lax.axis_index("cond")
    return c, (lax.axis_index("seq") & 1 if tuned() else jnp.zeros((), jnp.int32))


def after(value, *before):
    return lax.optimization_barrier((value, *before))[0]


def dot(a, b, dims=((1,), (0,))):
    return lax.dot_general(a, b, (dims, ((), ())), preferred_element_type=F32)


def gram(a, b):
    return dot(a, b, ((0,), (0,)))


def dot_t(a, b):
    return dot(a, b, ((1,), (1,)))


def gelu(v):
    return 0.5 * v * (1.0 + lax.erf(v * math.sqrt(0.5)))


def gelu_grad(v):
    return 0.5 * (1.0 + lax.erf(v * math.sqrt(0.5))) + v * (
        math.sqrt(0.5 / math.pi) * jnp.exp(-0.5 * v * v)
    )


def pick(items, t):
    low, high = (t & 1) == 1, (t & 2) == 2
    items = [jnp.where(low, items[i ^ 1], items[i]) for i in range(4)]
    return [jnp.where(high, items[i ^ 2], items[i]) for i in range(4)]


def regroup(x, dim, outer, inner):
    n = x.shape[dim] // 8
    shape = x.shape
    x = x.reshape(shape[:dim] + (outer, inner, n) + shape[dim + 1 :])
    return jnp.swapaxes(x, dim, dim + 1).reshape(shape)


CELL = 256
ALONG_Z = [[0, 2, 4, 6], [1, 3, 5, 7]]
VMEM_ROOM = 48 * 1024 * 1024


def bundle(shards):
    return jnp.concatenate(
        [s[:, i : i + CELL] for s in shards for i in range(0, s.shape[1], CELL)], axis=0
    )


def along_z(x):
    return lax.all_to_all(x, "seq", 0, 0, axis_index_groups=ALONG_Z, tiled=True)


def unpack_body(shapes, near_ref, far_ref, *outs):
    p = pl.program_id(0)

    def copy(ref):
        at = 0
        for (r, w), out in zip(shapes, outs):
            for i in range(0, w, CELL):
                out[:, i : i + CELL] = ref[0, at : at + r]
                at += r

    pl.when(p < 4)(lambda: copy(near_ref))
    pl.when(p >= 4)(lambda: copy(far_ref))


def unpack(near, far, shapes):
    block = (1,) + near.shape[1:]
    return pl.pallas_call(
        lambda *refs: unpack_body(shapes, *refs),
        out_shape=[jax.ShapeDtypeStruct((8 * r, w), near.dtype) for r, w in shapes],
        grid=(8,),
        in_specs=[
            pl.BlockSpec(block, lambda p: (jnp.minimum(p, 3), 0, 0)),
            pl.BlockSpec(block, lambda p: (jnp.maximum(p - 4, 0), 0, 0)),
        ],
        out_specs=[pl.BlockSpec((r, w), lambda p: (p, 0)) for r, w in shapes],
        compiler_params=pltpu.CompilerParams(vmem_limit_bytes=VMEM_ROOM),
        name="unpack",
    )(near, far)


def gather_plain(shards):
    return [regroup(lax.all_gather(s, "seq", axis=0, tiled=True), 0, 4, 2) for s in shards]


def pack_body(shapes, *refs):
    out = refs[-1]
    at = 0
    for (r, w), near, far in zip(shapes, refs[0::2], refs[1::2]):
        total = (near[...].astype(F32) + far[...].astype(F32)).astype(BF16)
        for i in range(0, w, CELL):
            out[0, at : at + r] = total[:, i : i + CELL]
            at += r


def pack(nears, fars):
    shapes = [(f.shape[0] // 4, f.shape[1]) for f in fars]
    rows = sum(r * w for r, w in shapes) // CELL
    specs = [pl.BlockSpec((r, w), lambda p: (p, 0)) for r, w in shapes for _ in range(2)]
    return pl.pallas_call(
        lambda *refs: pack_body(shapes, *refs),
        out_shape=jax.ShapeDtypeStruct((4, rows, CELL), BF16),
        grid=(4,),
        in_specs=specs,
        out_specs=pl.BlockSpec((1, rows, CELL), lambda p: (p, 0, 0)),
        compiler_params=pltpu.CompilerParams(vmem_limit_bytes=VMEM_ROOM),
        name="pack",
    )(*[x for pair in zip(nears, fars) for x in pair])


def total_body(shapes, in_ref, *outs):
    at = 0
    for (r, w), out in zip(shapes, outs):
        for i in range(0, w, CELL):
            cells = [in_ref[k, at : at + r].astype(F32) for k in range(4)]
            out[:, i : i + CELL] = (cells[0] + cells[1]) + (cells[2] + cells[3])
            at += r


def total(parts, shapes):
    return pl.pallas_call(
        lambda *refs: total_body(shapes, *refs),
        out_shape=[jax.ShapeDtypeStruct(shape, F32) for shape in shapes],
        compiler_params=pltpu.CompilerParams(vmem_limit_bytes=VMEM_ROOM),
        name="total",
    )(parts)


def reduce_rows(grads):
    if tuned():
        grads = [g.astype(BF16) for g in grads]
        fars = [hop(g[g.shape[0] // 2 :], 1) for g in grads]
        shapes = [(g.shape[0] // 8, g.shape[1]) for g in grads]
        return total(along_z(pack(grads, fars)), shapes)
    return [
        lax.psum_scatter(
            regroup(g.astype(BF16), 0, 2, 4), "seq", scatter_dimension=0, tiled=True
        ).astype(F32)
        for g in grads
    ]


class Line:
    def __init__(self):
        self.last = ()

    def send(self, *items):
        items = [(after(x, *self.last) if self.last else x, j) for x, j in items]
        self.last = [swap(x, j) for x, j in items]
        return self.last

    def spread(self, x):
        (y,) = self.send((x, 2))
        return [x, swap(x, 1), y, swap(y, 1)]

    def exchange(self, items):
        two, three = self.send((items[2], 2), (items[3], 3))
        return [items[0], swap(items[1], 1), two, three]


def same(x, j):
    return x


def fold_core(items, wire=BF16, fix=same):
    one = fix(swap(items[1].astype(wire), 1), 1).astype(F32)
    three = fix(swap(items[3].astype(wire), 1), 1).astype(F32)
    return items[0].astype(F32) + one, (items[2].astype(F32) + three).astype(wire)


def fold(line, items, wire=BF16, fix=same):
    zero, two = fold_core(items, wire, fix)
    return zero + fix(line.send((two, 2))[0], 2).astype(F32)


def lane_block(i):
    return pl.ds(pl.multiple_of(i * LANES, LANES), LANES)


def split_body(index_ref, in_ref, a_ref, b_ref):
    a_ref[...] = in_ref[:, : a_ref.shape[1]]
    b_ref[...] = in_ref[:, a_ref.shape[1] :]


def join_body(index_ref, a_ref, b_ref, out_ref):
    out_ref[:, : a_ref.shape[1]] = a_ref[...]
    out_ref[:, a_ref.shape[1] :] = b_ref[...]


def split_columns(x, index, first):
    n, w = x.shape[0] // 8, x.shape[1]
    widths = (first, w - first)
    return pl.pallas_call(
        split_body,
        out_shape=[jax.ShapeDtypeStruct((8 * n, v), x.dtype) for v in widths],
        grid_spec=pltpu.PrefetchScalarGridSpec(
            num_scalar_prefetch=1,
            grid=(8,),
            in_specs=[pl.BlockSpec((n, w), lambda i, index: (index[i], 0))],
            out_specs=[pl.BlockSpec((n, v), lambda i, index: (i, 0)) for v in widths],
        ),
        name="split_columns",
    )(index, x)


def join_columns(a, b, index):
    n = a.shape[0] // 8
    widths = (a.shape[1], b.shape[1])
    return pl.pallas_call(
        join_body,
        out_shape=jax.ShapeDtypeStruct((8 * n, sum(widths)), a.dtype),
        grid_spec=pltpu.PrefetchScalarGridSpec(
            num_scalar_prefetch=1,
            grid=(8,),
            in_specs=[pl.BlockSpec((n, v), lambda i, index: (index[i], 0)) for v in widths],
            out_specs=pl.BlockSpec((n, sum(widths)), lambda i, index: (i, 0)),
        ),
        name="join_columns",
    )(index, a, b)


def enter_body(from_up, to_layer, up_ref, q0, q1, q2, q3, out_ref, held, spaced):
    coarse = up_ref.shape[0]
    quarter = q0.shape[1]
    for j, ref in enumerate((q0, q1, q2, q3)):
        held[:, j * quarter : (j + 1) * quarter] = ref[...]
    for r in range(4):
        for p in range(8):
            spaced[p, pl.ds(r, coarse, stride=4), :] = up_ref[:, lane_block(from_up[r * 8 + p])]
    for p in range(8):
        out_ref[:, p * LANES : (p + 1) * LANES] = spaced[p] + held[
            :, lane_block(to_layer[p])
        ].astype(F32)


def enter(up_terms, quarters, from_up, to_layer):
    coarse, wide = up_terms.shape
    whole = lambda shape: pl.BlockSpec(shape, lambda i, a, b: (0, 0))
    tokens, quarter = quarters[0].shape
    return pl.pallas_call(
        enter_body,
        out_shape=jax.ShapeDtypeStruct((tokens, wide // 4), F32),
        grid_spec=pltpu.PrefetchScalarGridSpec(
            num_scalar_prefetch=2,
            grid=(1,),
            in_specs=[whole((coarse, wide))] + [whole((tokens, quarter))] * 4,
            out_specs=whole((tokens, wide // 4)),
            scratch_shapes=[
                pltpu.VMEM((tokens, wide // 4), BF16),
                pltpu.VMEM((8, tokens, LANES), F32),
            ],
        ),
        compiler_params=pltpu.CompilerParams(vmem_limit_bytes=VMEM_ROOM),
        name="enter",
    )(from_up, to_layer, up_terms, *quarters)


def leave_body(to_up, to_quarters, in_ref, rows_ref, q0, q1, q2, q3, spaced):
    coarse = rows_ref.shape[0]
    for p in range(8):
        spaced[p] = in_ref[:, p * LANES : (p + 1) * LANES]
    for i in range(32):
        source = to_up[i]
        rows_ref[:, i * LANES : (i + 1) * LANES] = spaced[
            source & 7, pl.ds(source >> 3, coarse, stride=4), :
        ].astype(BF16)
    for j, ref in enumerate((q0, q1, q2, q3)):
        for half in range(2):
            ref[:, half * LANES : (half + 1) * LANES] = in_ref[
                :, lane_block(to_quarters[2 * j + half])
            ].astype(BF16)


def leave(grad, to_up, to_quarters):
    tokens, width = grad.shape
    whole = lambda shape: pl.BlockSpec(shape, lambda i, a, b: (0, 0))
    shapes = [(tokens // 4, 4 * width)] + [(tokens, width // 4)] * 4
    return pl.pallas_call(
        leave_body,
        out_shape=[jax.ShapeDtypeStruct(shape, BF16) for shape in shapes],
        grid_spec=pltpu.PrefetchScalarGridSpec(
            num_scalar_prefetch=2,
            grid=(1,),
            in_specs=[whole((tokens, width))],
            out_specs=[whole(shape) for shape in shapes],
            scratch_shapes=[pltpu.VMEM((8, tokens, LANES), F32)],
        ),
        compiler_params=pltpu.CompilerParams(vmem_limit_bytes=VMEM_ROOM),
        name="leave",
    )(to_up, to_quarters, grad)


TILE = 128
SCALE = 1.0 / math.sqrt(HEAD)


def by_head(x):
    heads = x.shape[1] // HEAD
    feature = lax.broadcasted_iota(jnp.int32, x.shape, 1) // HEAD
    return jnp.concatenate(
        [jnp.where(feature == h, x, jnp.zeros_like(x)) for h in range(heads)], axis=0
    )


def of_heads(x):
    heads = x.shape[1] // HEAD
    feature = lax.broadcasted_iota(jnp.int32, (TILE, x.shape[1]), 1) // HEAD
    out = x[:TILE]
    for h in range(1, heads):
        out = jnp.where(feature == h, x[h * TILE : (h + 1) * TILE], out)
    return out


def visible(column, row):
    i = lax.broadcasted_iota(jnp.int32, (TILE, TILE), 0)
    j = lax.broadcasted_iota(jnp.int32, (TILE, TILE), 1)
    return (column == row) & (i >= j) & (i // ROW == j // ROW)


def soft(query, keys, allowed):
    scores = dot_t(query, keys) * SCALE
    probs = []
    for h in range(scores.shape[1] // TILE):
        part = jnp.where(allowed, scores[:, h * TILE : (h + 1) * TILE], NEG_FILL)
        exps = jnp.exp(part - jnp.max(part, axis=1, keepdims=True))
        probs.append(exps * (1.0 / jnp.sum(exps, axis=1, keepdims=True)))
    return probs


def attend_body(column_ref, row_ref, *refs):
    allowed = visible(column_ref[...], row_ref[0])
    for qkv_ref, out_ref in zip(refs[:4], refs[4:]):
        n = out_ref.shape[1]
        probs = soft(qkv_ref[:, :n], by_head(qkv_ref[:, n : 2 * n]), allowed)
        low = jnp.concatenate([p.astype(BF16) for p in probs], axis=1)
        out_ref[...] = dot(low, by_head(qkv_ref[:, 2 * n :])).astype(BF16)


def attend_back_body(column_ref, row_ref, *refs):
    allowed = visible(column_ref[...], row_ref[0])
    for qkv_ref, grad_ref, out_ref in zip(refs[:4], refs[4:8], refs[8:]):
        n = grad_ref.shape[1]
        query, grad = qkv_ref[:, :n], grad_ref[...]
        keys = by_head(qkv_ref[:, n : 2 * n])
        probs = soft(query, keys, allowed)
        grad_probs = dot_t(grad, by_head(qkv_ref[:, 2 * n :]))
        grads = []
        for h, p in enumerate(probs):
            part = grad_probs[:, h * TILE : (h + 1) * TILE]
            inner = jnp.sum(p * part, axis=1, keepdims=True)
            grads.append((p * (part - inner)).astype(BF16))
        grads = jnp.concatenate(grads, axis=1)
        low = jnp.concatenate([p.astype(BF16) for p in probs], axis=1)
        out_ref[:, :n] = (dot(grads, keys) * SCALE).astype(BF16)
        out_ref[:, n : 2 * n] = (of_heads(gram(grads, query)) * SCALE).astype(BF16)
        out_ref[:, 2 * n :] = of_heads(gram(low, grad)).astype(BF16)


def tiled_call(body, segments, arrays, widths, name):
    tokens = arrays[0].shape[0]
    tiles = tokens // TILE
    wide = lambda w: pl.BlockSpec((TILE, w), lambda i: (i, 0))
    return pl.pallas_call(
        body,
        out_shape=[jax.ShapeDtypeStruct((tokens, w), BF16) for w in widths],
        grid=(tiles,),
        in_specs=[wide(1), pl.BlockSpec((1, 1, TILE), lambda i: (i, 0, 0))]
        + [wide(a.shape[1]) for a in arrays],
        out_specs=[wide(w) for w in widths],
        compiler_params=pltpu.CompilerParams(vmem_limit_bytes=VMEM_ROOM),
        name=name,
    )(segments.reshape(tokens, 1), segments.reshape(tiles, 1, TILE), *arrays)


def attend(qkv, segments):
    return tiled_call(attend_body, segments, qkv, [q.shape[1] // 3 for q in qkv], "attend")


def attend_back(qkv, grads, segments):
    return tiled_call(
        attend_back_body, segments, (*qkv, *grads), [q.shape[1] for q in qkv], "attend_back"
    )


def normalize(stream):
    mean = jnp.mean(stream, axis=1, keepdims=True)
    centred = stream - mean
    rstd = lax.rsqrt(jnp.mean(centred * centred, axis=1, keepdims=True) + EPSILON)
    return centred * rstd, rstd


def normalize_back(normed, rstd, gain, grad):
    scaled = grad * gain
    back = rstd * (
        scaled
        - jnp.mean(scaled, axis=1, keepdims=True)
        - normed * jnp.mean(scaled * normed, axis=1, keepdims=True)
    )
    return back, jnp.sum(grad * normed, axis=0), jnp.sum(grad, axis=0)


def vector_owner(c, x):
    i = jnp.arange(32)
    kx, kz, part = i >> 4, (i >> 2) & 3, i & 3
    source = ((kx ^ x) << 2) | part
    piece = (kz ^ c) * 8 + ((((source & 1) ^ x) << 2) | (source >> 1))
    return piece[:, None] == jnp.arange(32)[None, :]


PAD = 16


def vector_rows(vectors):
    ends = [(0, 0)] * (vectors.ndim - 2)
    count, n = vectors.shape[-2:]
    return jnp.pad(vectors, ends + [(0, PAD - count), (0, CELL - n)])


def join_vectors(spreads, n, c, x):
    pieces = jnp.stack([s.reshape(8, -1, PAD, CELL)[:, :, :4, :n] for s in spreads])
    pieces = pieces.transpose(3, 0, 1, 2, 4).reshape(4, 32, -1)
    owner = vector_owner(c, x).astype(BF16)
    full = jnp.einsum("dp,vpn->vdn", owner, pieces, preferred_element_type=F32)
    return full.reshape(4, -1)


def split_vectors(full, n, c, x):
    owner = vector_owner(c, x).astype(F32)
    pieces = jnp.einsum(
        "dp,vdn->pvn",
        owner,
        full.reshape(4, 32, -1),
        precision=lax.Precision.HIGHEST,
        preferred_element_type=F32,
    )
    pieces = pieces.reshape(4, 8, 4, -1, n).swapaxes(2, 3)
    rows = vector_rows(pieces)
    return [rows[j].reshape(-1, CELL) for j in range(4)]


MLP_TILE = 256
TURNS = 8


def order_of(k):
    return ((k & 1) << 1) | (k >> 1)


def mlp_body(index, *refs):
    (n0, n1, n2, n3, q0, q1, q2, q3, in_ref, down_ref, stream_ref) = refs[:11]
    (act_ref, grad_ref, norm_ref, cot_ref, d0, d1, d2, d3, keep_ref, send_ref, mine_ref) = refs[11:22]
    wide, other = refs[22:]
    tile = pl.program_id(0)
    k = tile // 2
    layer_of_natural, natural_of_layer, quarter_at = (
        [index[row * 8 + i] for i in range(8)] for row in range(3)
    )
    for at, ref in enumerate((n0, n2, n1, n3)):

        @pl.when(k == at)
        def _(ref=ref):
            for b in range(8):
                norm_ref[:, b * LANES : (b + 1) * LANES] = ref[:, lane_block(layer_of_natural[b])]

    quarters = [pl.ds(pl.multiple_of(quarter_at[j] * 256, 256), 256) for j in range(4)]
    for j, ref in enumerate((q0, q1, q2, q3)):
        cot_ref[:, quarters[j]] = ref[...]
    weight_in = in_ref[...].reshape(-1, in_ref.shape[-1])
    weight_down = down_ref[...].reshape(-1, down_ref.shape[-1])
    pre = dot(norm_ref[...], weight_in)
    half = 0.5 + 0.5 * lax.erf(pre * math.sqrt(0.5))
    act = (pre * half).astype(BF16)
    act_ref[...] = act
    slope = half + pre * (math.sqrt(0.5 / math.pi) * jnp.exp(-0.5 * pre * pre))
    grad = (slope * dot(cot_ref[...], weight_down)).astype(BF16)
    grad_ref[...] = grad
    wide[...] = dot_t(act, weight_down)

    @pl.when(tile < 2)
    def _():
        for b in range(8):
            at = slice(b * LANES, (b + 1) * LANES)
            wide[:, at] = wide[:, at] + stream_ref[:, lane_block(layer_of_natural[b])]
        for p in range(8):
            mine_ref[:, p * LANES : (p + 1) * LANES] = cot_ref[:, lane_block(natural_of_layer[p])]

    for j, ref in enumerate((d0, d1, d2, d3)):
        ref[...] = wide[:, quarters[j]].astype(BF16)
    other[...] = dot_t(grad, weight_in)

    @pl.when(tile < 4)
    def _():
        for p in range(8):
            keep_ref[:, p * LANES : (p + 1) * LANES] = other[:, lane_block(natural_of_layer[p])]

    @pl.when(tile >= 4)
    def _():
        for p in range(8):
            send_ref[:, p * LANES : (p + 1) * LANES] = other[
                :, lane_block(natural_of_layer[p])
            ].astype(BF16)


def mlp(norms, cots, weights, stream, index):
    tokens, width = norms[0].shape
    rows, quarter = cots[0].shape
    hidden = weights.shape[-1]
    n = weights.shape[2]
    tile = MLP_TILE
    per = tokens // tile
    assert per == 2
    held = lambda start, count: lambda i, index: (jnp.clip(i - start, 0, count - 1), 0)
    norm_specs = [
        pl.BlockSpec((tile, width), held(2 * order_of(m), 2)) for m in range(4)
    ]
    cot_specs = [
        pl.BlockSpec(
            (tile, quarter),
            lambda i, index, j=j: (
                jnp.bitwise_xor(order_of(i // 2), j) * 2 + lax.rem(i, 2),
                0,
            ),
        )
        for j in range(4)
    ]
    weight_specs = [
        pl.BlockSpec((8, 1, n, hidden), lambda i, index, k=k: (0, k, 0, 0)) for k in range(2)
    ]
    each = lambda w: pl.BlockSpec((tile, w), lambda i, index: (i, 0))
    shape = jax.ShapeDtypeStruct
    return pl.pallas_call(
        mlp_body,
        out_shape=[
            shape((rows, hidden), BF16),
            shape((rows, hidden), BF16),
            shape((rows, width), BF16),
            shape((rows, width), BF16),
            *[shape((rows, quarter), BF16)] * 4,
            shape((rows // 2, width), F32),
            shape((rows // 2, width), BF16),
            shape((tokens, width), BF16),
        ],
        grid_spec=pltpu.PrefetchScalarGridSpec(
            num_scalar_prefetch=1,
            grid=(TURNS,),
            in_specs=norm_specs
            + cot_specs
            + weight_specs
            + [pl.BlockSpec((tile, width), held(0, 2))],
            out_specs=[each(hidden), each(hidden), each(width), each(width)]
            + [each(quarter)] * 4
            + [
                pl.BlockSpec((tile, width), held(0, 4)),
                pl.BlockSpec((tile, width), held(4, 4)),
                pl.BlockSpec((tile, width), held(0, 2)),
            ],
            scratch_shapes=[pltpu.VMEM((tile, width), F32), pltpu.VMEM((tile, width), F32)],
        ),
        compiler_params=pltpu.CompilerParams(vmem_limit_bytes=VMEM_ROOM),
        name="mlp",
    )(index, *norms, *cots, weights, weights, stream)


def mlp_grads_body(norm_ref, cot_ref, act_ref, grad_ref, out_ref):
    for k, (left, right) in enumerate(((norm_ref, grad_ref), (cot_ref, act_ref))):
        block = gram(left[...], right[...]).astype(BF16)
        n = out_ref.shape[2]
        for i in range(out_ref.shape[0]):
            out_ref[i, k] = block[i * n : (i + 1) * n]


def mlp_grads(norm, cot, act, grad):
    rows, width = norm.shape
    hidden = act.shape[1]
    n = width // 8
    whole = pl.BlockSpec((rows, hidden), lambda i: (0, 0))
    part = pl.BlockSpec((rows, 2 * n), lambda i: (0, i))
    return pl.pallas_call(
        mlp_grads_body,
        out_shape=jax.ShapeDtypeStruct((8, 2, n, hidden), BF16),
        grid=(4,),
        in_specs=[part, part, whole, whole],
        out_specs=pl.BlockSpec((2, 2, n, hidden), lambda i: (i, 0, 0, 0)),
        compiler_params=pltpu.CompilerParams(vmem_limit_bytes=VMEM_ROOM),
        name="mlp_grads",
    )(norm, cot, act, grad)


def join_rows(packed):
    pieces, _, n, w = packed.shape
    return (
        packed.reshape(8, pieces // 8, 2, n, w).swapaxes(1, 2).reshape(8, 2, n * pieces // 8, w)
    )


def split_rows(packed):
    _, _, n, w = packed.shape
    share = lax.axis_size("seq") // 8
    return (
        packed.reshape(8, 2, share, n // share, w).swapaxes(1, 2).reshape(8 * share, 2, n // share, w)
    )


def edges(cells):
    count = lax.axis_size("seq")
    head, tail = cells
    return (
        lax.ppermute(tail, "seq", [(i, i + 1) for i in range(count - 1)]),
        lax.ppermute(head, "seq", [(i + 1, i) for i in range(count - 1)]),
    )


def on_device(
    inputs,
    coarse_ids,
    segment_ids,
    cotangent,
    embed_table,
    conv_weight,
    res_weight,
    up_weight,
    gain_one,
    shift_one,
    qkv_weight,
    out_weight,
    gain_two,
    shift_two,
    in_weight,
    down_weight,
):
    c, x = place()
    micros, tokens, quarter = inputs.shape
    width = 4 * quarter
    coarse = coarse_ids.shape[1]
    step = CONV_DILATION
    slot = jnp.arange(8, dtype=jnp.int32)
    to_layer = (((slot & 3) ^ c) << 1) | ((slot >> 2) ^ x)
    to_quarters = (((slot & 1) ^ x) << 2) | ((slot >> 1) ^ c)
    natural_of_layer = ((slot & 3) << 1) | ((slot >> 2) ^ x)
    layer_of_natural = (((slot & 1) ^ x) << 2) | (slot >> 1)

    line = Line()
    stream_in = line.exchange(pick([inputs[i] for i in range(4)], c))
    cots = line.spread(jnp.concatenate(pick([cotangent[i] for i in range(4)], c), axis=0))

    lot = gain_one.shape[0]
    vectors = vector_rows(jnp.stack([gain_one, shift_one, gain_two, shift_two]))
    conv_shard = conv_weight.transpose(2, 0, 1).reshape(-1, 3 * quarter)
    groups = ((embed_table, conv_shard, vectors), (res_weight, up_weight.T))
    attn_shard = jnp.concatenate([qkv_weight.reshape(-1, 3 * quarter), out_weight.T], axis=1)
    mlp_shard = jnp.stack([in_weight, down_weight.T])
    if tuned():
        first, second = (bundle(group) for group in groups)
        first = along_z(jnp.broadcast_to(first, (4,) + first.shape))
        second = after(second, first)
        second = along_z(jnp.broadcast_to(second, (4,) + second.shape))
        attn_shard = after(attn_shard, second)
        first_far = hop(after(first, *stream_in), 1)
        second_far = hop(after(second, first_far, *cots), 1)
        table, conv, vectors = unpack(first, first_far, [w.shape for w in groups[0]])
        res, up = unpack(second, second_far, [w.shape for w in groups[1]])
    else:
        (table, conv, vectors), (res, up) = (gather_plain(group) for group in groups)
    attn_w = lax.all_gather(attn_shard, "seq", axis=0, tiled=True)
    mlp_w = lax.all_gather(after(mlp_shard, attn_w), "seq", axis=0)
    vectors = join_vectors(line.spread(vectors), lot, c, x)
    gain1, shift1, gain2, shift2 = (vectors[i][None, :] for i in range(4))

    ids = jnp.concatenate(pick([coarse_ids[i] for i in range(4)], c))
    vocab = table.shape[0]
    code = jnp.arange(vocab, dtype=jnp.int32)
    block = vocab // 8
    slot_of = code // block
    code = (((slot_of & 3) << 1) | ((slot_of >> 2) ^ x)) * block + code % block
    onehot = (ids[:, None] == code[None, :]).astype(BF16)
    embed = dot(onehot, table)
    act = gelu(embed).astype(BF16).reshape(micros, coarse, quarter)
    prior, later = edges((act[:, :step], act[:, coarse - step :]))
    padded = jnp.concatenate([prior, act, later], axis=1)
    taps = jnp.concatenate(
        [padded[:, k * step : k * step + coarse] for k in range(3)], axis=2
    ).reshape(micros * coarse, 3 * quarter)
    conv_terms = dot_t(taps, conv).reshape(micros, coarse, width)
    conv_out = fold(line, [conv_terms[j] for j in range(4)])
    mixed = gelu(conv_out).astype(BF16)
    mixed_all = jnp.concatenate(line.spread(mixed), axis=0)
    hidden = (embed + dot(mixed_all, res)).astype(BF16)
    up_terms = dot_t(hidden, up).reshape(micros, coarse, 4 * width)
    up_terms = fold(line, [up_terms[j] for j in range(4)])
    qkv_w, out_w = split_columns(attn_w, natural_of_layer, 3 * quarter)
    qkv_w = line.spread(qkv_w)
    out_w = line.spread(out_w)

    i = jnp.arange(32, dtype=jnp.int32)
    r, bz, bx = i >> 3, i & 3, ((i >> 2) & 1) ^ x
    from_up = ((bz >> 1) ^ x) * 16 + r * 4 + ((bz & 1) << 1 | bx)
    h, r, w = (i >> 4) ^ x, (i >> 2) & 3, i & 3
    to_up = r * 8 + (((w & 1) ^ x) << 2 | h << 1 | w >> 1)
    stream_zero = enter(up_terms, stream_in, from_up, to_layer)
    normed_one, rstd_one = normalize(stream_zero)
    norm_one = (normed_one * gain1 + shift1).astype(BF16)
    segments = lax.dynamic_index_in_dim(segment_ids, c, 0, keepdims=False)
    qkv = [dot(norm_one, qkv_w[j]).astype(BF16) for j in range(4)]
    context = attend(qkv, segments)
    stream_one = stream_zero
    for j in range(4):
        stream_one = stream_one + dot_t(context[j], out_w[j])
    normed_two, rstd_two = normalize(stream_one)
    norm_two = (normed_two * gain2 + shift2).astype(BF16)

    norm_all = line.spread(norm_two)
    index = jnp.concatenate([layer_of_natural, natural_of_layer, jnp.tile(jnp.arange(4) ^ c, 2)])
    mlp_act, grad_pre, norm_rows, cot_rows, *outs, keep, send, cot_mine = mlp(
        norm_all, cots, join_rows(mlp_w), stream_one, index.astype(jnp.int32)
    )
    from_core = swap(send, 1).astype(F32)
    over_y = (keep[tokens:] + from_core[tokens:]).astype(BF16)
    (from_y,) = line.send((over_y, 2))
    grad_mlp = mlp_grads(after(norm_rows, over_y), cot_rows, mlp_act, grad_pre)
    turned = lambda v, j: jnp.stack([v[m ^ order_of(j)] for m in range(4)])
    result, over_y = fold_core(
        [d.reshape(micros, tokens, quarter) for d in outs], fix=turned
    )
    from_y, _, over_y = lax.optimization_barrier((from_y, grad_mlp, over_y))
    grad_norm_two = keep[:tokens] + from_core[:tokens] + from_y.astype(F32)
    (from_y,) = line.send((over_y, 2))
    result = (result + turned(from_y, 2).astype(F32)).astype(BF16)
    result = jnp.stack(pick([result[order_of(m)] for m in range(4)], c))
    grad_mlp = lax.psum_scatter(split_rows(grad_mlp), "seq", scatter_dimension=0, tiled=False)
    grad_in, grad_down = grad_mlp[0].astype(F32), grad_mlp[1].astype(F32).T

    back_two, grad_gain2, grad_shift2 = normalize_back(normed_two, rstd_two, gain2, grad_norm_two)
    grad_stream_one = cot_mine.astype(F32) + back_two
    grad_att = grad_stream_one.astype(BF16)
    grad_out, over_y = fold_core([gram(grad_att, context[j]) for j in range(4)])
    grad_context = [dot(grad_att, out_w[j]).astype(BF16) for j in range(4)]
    grad_context[0] = after(grad_context[0], over_y)
    (from_y,) = line.send((over_y, 2))
    grad_out = (grad_out + from_y.astype(F32)).astype(BF16)
    grad_rows = list(attend_back(qkv, grad_context, segments))
    grad_qkv = [
        fold_core([gram(norm_one, g[:, k * quarter : (k + 1) * quarter]) for g in grad_rows])
        for k in range(3)
    ]
    grad_rows[0] = after(grad_rows[0], grad_qkv[0][1])

    def finish(part):
        zero, two = grad_qkv[part]
        (from_y,) = line.send((two, 2))
        grad_qkv[part] = (zero + from_y.astype(F32)).astype(BF16)

    finish(0)
    grad_norm_one = dot_t(grad_rows[0], qkv_w[0])
    for j in (1, 2, 3):
        grad_norm_one = grad_norm_one + dot_t(grad_rows[j], qkv_w[j])
    back_one, grad_gain1, grad_shift1 = normalize_back(normed_one, rstd_one, gain1, grad_norm_one)
    input_grad = grad_stream_one + back_one
    grad_vectors = split_vectors(
        jnp.stack([grad_gain1, grad_shift1, grad_gain2, grad_shift2]), lot, c, x
    )
    grad_up_rows, *grad_in_q = leave(input_grad, to_up, to_quarters)
    grad_up_rows = jnp.concatenate(line.spread(grad_up_rows), axis=0)
    finish(1)
    grad_hidden = dot(grad_up_rows, up)
    grad_hidden_low = grad_hidden.astype(BF16)
    grad_mixed = dot_t(grad_hidden_low, res).reshape(micros, coarse, width)
    grad_mixed = fold(line, [grad_mixed[j] for j in range(4)])
    finish(2)
    grad_conv_low = (gelu_grad(conv_out) * grad_mixed).astype(BF16)
    grad_up = gram(grad_up_rows, hidden)
    grad_res = gram(mixed_all, grad_hidden_low)
    grad_attn = join_columns(jnp.concatenate(grad_qkv, axis=1), grad_out, layer_of_natural)
    grad_attn = lax.psum_scatter(grad_attn, "seq", scatter_dimension=0, tiled=True).astype(F32)
    grad_qkv, grad_out = grad_attn[:, : 3 * quarter], grad_attn[:, 3 * quarter :]

    grad_conv_all = jnp.concatenate(line.spread(grad_conv_low), axis=0)
    input_grads = jnp.stack(pick(line.exchange(grad_in_q), c))
    grad_taps = dot(grad_conv_all, conv).reshape(micros, coarse, 3 * quarter)
    tap = [grad_taps[:, :, k * quarter : (k + 1) * quarter] for k in range(3)]
    prior, later = edges((tap[0][:, :step].astype(BF16), tap[2][:, coarse - step :].astype(BF16)))
    grad_act = (
        tap[1]
        + jnp.concatenate([tap[0][:, step:], later.astype(F32)], axis=1)
        + jnp.concatenate([prior.astype(F32), tap[2][:, : coarse - step]], axis=1)
    ).reshape(micros * coarse, quarter)
    grad_res, grad_up, grad_vectors = reduce_rows(
        [grad_res, grad_up, fold(line, grad_vectors)]
    )
    grad_vectors = [grad_vectors[i, :lot] for i in range(4)]
    grad_embed = (grad_hidden + gelu_grad(embed) * grad_act).astype(BF16)
    grad_table, grad_conv = reduce_rows([gram(onehot, grad_embed), gram(grad_conv_all, taps)])
    grad_conv = grad_conv.reshape(-1, 3, quarter).transpose(1, 2, 0)
    return (
        result,
        input_grads,
        grad_table,
        grad_conv,
        grad_res,
        grad_up.T,
        grad_vectors[0],
        grad_vectors[1],
        grad_qkv.reshape(qkv_weight.shape),
        grad_out.T,
        grad_vectors[2],
        grad_vectors[3],
        grad_in,
        grad_down,
    )


def solution(mesh):
    wide = P(("cond", "seq"))
    acts = P(None, "seq", "cond")
    weights = (
        P("seq", "cond"),
        P(None, "cond", "seq"),
        P("seq", "cond"),
        P("cond", "seq"),
        wide,
        wide,
        P("seq", None, "cond"),
        P("cond", "seq"),
        wide,
        wide,
        P("seq", "cond"),
        P("cond", "seq"),
    )
    return jax.shard_map(
        on_device,
        mesh=mesh,
        in_specs=(acts, P(None, "seq"), P(None, "seq"), acts) + weights,
        out_specs=(acts, acts) + weights,
        check_vma=False,
    )
```

```python
import math

import jax
import jax.numpy as jnp
from jax import lax
from jax.experimental import pallas as pl
from jax.experimental.pallas import tpu as pltpu
from jax.sharding import PartitionSpec as P

HEAD = 64
ROW = 64
CONV_DILATION = 27
EPSILON = 1e-05
NEG_FILL = -1e30
LANES = 128
BF16 = jnp.bfloat16
F32 = jnp.float32


def tuned():
    return lax.axis_size("seq") == 8


def swap(x, j):
    return lax.ppermute(x, "cond", [(i, i ^ j) for i in range(4)])


def hop(x, k):
    return lax.ppermute(x, "seq", [(i, i ^ k) for i in range(8)])


def place():
    c = lax.axis_index("cond")
    return c, (lax.axis_index("seq") & 1 if tuned() else jnp.zeros((), jnp.int32))


def after(value, *before):
    return lax.optimization_barrier((value, *before))[0]


def dot(a, b, dims=((1,), (0,))):
    return lax.dot_general(a, b, (dims, ((), ())), preferred_element_type=F32)


def gram(a, b):
    return dot(a, b, ((0,), (0,)))


def dot_t(a, b):
    return dot(a, b, ((1,), (1,)))


def gelu(v):
    return 0.5 * v * (1.0 + lax.erf(v * math.sqrt(0.5)))


def gelu_grad(v):
    return 0.5 * (1.0 + lax.erf(v * math.sqrt(0.5))) + v * (
        math.sqrt(0.5 / math.pi) * jnp.exp(-0.5 * v * v)
    )


def pick(items, t):
    low, high = (t & 1) == 1, (t & 2) == 2
    items = [jnp.where(low, items[i ^ 1], items[i]) for i in range(4)]
    return [jnp.where(high, items[i ^ 2], items[i]) for i in range(4)]


def regroup(x, dim, outer, inner):
    n = x.shape[dim] // 8
    shape = x.shape
    x = x.reshape(shape[:dim] + (outer, inner, n) + shape[dim + 1 :])
    return jnp.swapaxes(x, dim, dim + 1).reshape(shape)


def cost(us):
    return pl.CostEstimate(flops=int(us * 1.1e9), transcendentals=0, bytes_accessed=0)


CELL = 256
ALONG_Z = [[0, 2, 4, 6], [1, 3, 5, 7]]
VMEM_ROOM = 48 * 1024 * 1024


def bundle(shards):
    return jnp.concatenate(
        [s[:, i : i + CELL] for s in shards for i in range(0, s.shape[1], CELL)], axis=0
    )


def along_z(x):
    return lax.all_to_all(x, "seq", 0, 0, axis_index_groups=ALONG_Z, tiled=True)


def unpack_body(shapes, near_ref, far_ref, *outs):
    p = pl.program_id(0)

    def copy(ref):
        at = 0
        for (r, w), out in zip(shapes, outs):
            for i in range(0, w, CELL):
                out[:, i : i + CELL] = ref[0, at : at + r]
                at += r

    pl.when(p < 4)(lambda: copy(near_ref))
    pl.when(p >= 4)(lambda: copy(far_ref))


def unpack(near, far, shapes):
    block = (1,) + near.shape[1:]
    return pl.pallas_call(
        lambda *refs: unpack_body(shapes, *refs),
        out_shape=[jax.ShapeDtypeStruct((8 * r, w), near.dtype) for r, w in shapes],
        grid=(8,),
        in_specs=[
            pl.BlockSpec(block, lambda p: (jnp.minimum(p, 3), 0, 0)),
            pl.BlockSpec(block, lambda p: (jnp.maximum(p - 4, 0), 0, 0)),
        ],
        out_specs=[pl.BlockSpec((r, w), lambda p: (p, 0)) for r, w in shapes],
        compiler_params=pltpu.CompilerParams(vmem_limit_bytes=VMEM_ROOM),
        name="unpack",
        cost_estimate=cost(3),
    )(near, far)


def gather_plain(shards):
    return [regroup(lax.all_gather(s, "seq", axis=0, tiled=True), 0, 4, 2) for s in shards]


def pack_body(count, *refs):
    half, at = pl.program_id(0), 0
    for ref in refs[:count]:
        r, w = ref.shape
        for i in range(0, w, CELL):
            for k, out in enumerate(refs[count:]):

                @pl.when(half == k)
                def _(out=out, ref=ref, at=at, r=r, i=i):
                    out[0, at : at + r] = ref[:, i : i + CELL]

            at += r


def pack(grads):
    shapes = [(g.shape[0] // 8, g.shape[1]) for g in grads]
    rows = sum(r * w for r, w in shapes) // CELL
    shape = jax.ShapeDtypeStruct((4, rows, CELL), BF16)
    return pl.pallas_call(
        lambda *refs: pack_body(len(grads), *refs),
        out_shape=(shape, shape),
        grid=(2, 4),
        in_specs=[pl.BlockSpec((r, w), lambda h, p: (4 * h + p, 0)) for r, w in shapes],
        out_specs=(
            pl.BlockSpec((1, rows, CELL), lambda h, p: (jnp.where(h == 0, p, 3), 0, 0)),
            pl.BlockSpec((1, rows, CELL), lambda h, p: (jnp.where(h == 1, p, 0), 0, 0)),
        ),
        compiler_params=pltpu.CompilerParams(vmem_limit_bytes=VMEM_ROOM),
        name="pack",
        cost_estimate=cost(2),
    )(*grads)


def total_body(shapes, in_ref, *outs):
    at = 0
    for (r, w), out in zip(shapes, outs):
        for i in range(0, w, CELL):
            cells = [in_ref[k, at : at + r].astype(F32) for k in range(4)]
            out[:, i : i + CELL] = (cells[0] + cells[1]) + (cells[2] + cells[3])
            at += r


def total(parts, shapes):
    return pl.pallas_call(
        lambda *refs: total_body(shapes, *refs),
        out_shape=[jax.ShapeDtypeStruct(shape, F32) for shape in shapes],
        compiler_params=pltpu.CompilerParams(vmem_limit_bytes=VMEM_ROOM),
        name="total",
        cost_estimate=cost(1),
    )(parts)


def cross_x(grads):
    grads = [g.astype(BF16) for g in grads]
    if tuned():
        near, far = pack(grads)
        return near, hop(far, 1)
    return grads


def cross_z(started, shapes):
    if tuned():
        near, far = started
        return total(along_z((near.astype(F32) + far.astype(F32)).astype(BF16)), shapes)
    return [
        lax.psum_scatter(
            regroup(g, 0, 2, 4), "seq", scatter_dimension=0, tiled=True
        ).astype(F32)
        for g in started
    ]


class Line:
    def __init__(self):
        self.last = ()

    def send(self, *items):
        items = [(after(x, *self.last) if self.last else x, j) for x, j in items]
        self.last = [swap(x, j) for x, j in items]
        return self.last

    def spread(self, x):
        (y,) = self.send((x, 2))
        return [x, swap(x, 1), y, swap(y, 1)]

    def exchange(self, items):
        two, three = self.send((items[2], 2), (items[3], 3))
        return [items[0], swap(items[1], 1), two, three]


def same(x, j):
    return x


def fold_core(items, wire=BF16, fix=same):
    one = fix(swap(items[1].astype(wire), 1), 1).astype(F32)
    three = fix(swap(items[3].astype(wire), 1), 1).astype(F32)
    return items[0].astype(F32) + one, (items[2].astype(F32) + three).astype(wire)


def fold(line, items, wire=BF16, fix=same):
    zero, two = fold_core(items, wire, fix)
    return zero + fix(line.send((two, 2))[0], 2).astype(F32)


def lane_block(i):
    return pl.ds(pl.multiple_of(i * LANES, LANES), LANES)


def enter_body(from_up, to_layer, up_ref, q0, q1, q2, q3, out_ref, held, spaced):
    coarse = up_ref.shape[0]
    quarter = q0.shape[1]
    for j, ref in enumerate((q0, q1, q2, q3)):
        held[:, j * quarter : (j + 1) * quarter] = ref[...]
    for r in range(4):
        for p in range(8):
            spaced[p, pl.ds(r, coarse, stride=4), :] = up_ref[:, lane_block(from_up[r * 8 + p])]
    for p in range(8):
        out_ref[:, p * LANES : (p + 1) * LANES] = spaced[p] + held[
            :, lane_block(to_layer[p])
        ].astype(F32)


def enter(up_terms, quarters, from_up, to_layer):
    coarse, wide = up_terms.shape
    whole = lambda shape: pl.BlockSpec(shape, lambda i, a, b: (0, 0))
    tokens, quarter = quarters[0].shape
    return pl.pallas_call(
        enter_body,
        out_shape=jax.ShapeDtypeStruct((tokens, wide // 4), F32),
        grid_spec=pltpu.PrefetchScalarGridSpec(
            num_scalar_prefetch=2,
            grid=(1,),
            in_specs=[whole((coarse, wide))] + [whole((tokens, quarter))] * 4,
            out_specs=whole((tokens, wide // 4)),
            scratch_shapes=[
                pltpu.VMEM((tokens, wide // 4), BF16),
                pltpu.VMEM((8, tokens, LANES), F32),
            ],
        ),
        compiler_params=pltpu.CompilerParams(vmem_limit_bytes=VMEM_ROOM),
        name="enter",
        cost_estimate=cost(2),
    )(from_up, to_layer, up_terms, *quarters)


def leave_body(to_up, to_quarters, in_ref, rows_ref, q0, q1, q2, q3, spaced):
    coarse = rows_ref.shape[0]
    for p in range(8):
        spaced[p] = in_ref[:, p * LANES : (p + 1) * LANES]
    for i in range(32):
        source = to_up[i]
        rows_ref[:, i * LANES : (i + 1) * LANES] = spaced[
            source & 7, pl.ds(source >> 3, coarse, stride=4), :
        ].astype(BF16)
    for j, ref in enumerate((q0, q1, q2, q3)):
        for half in range(2):
            ref[:, half * LANES : (half + 1) * LANES] = in_ref[
                :, lane_block(to_quarters[2 * j + half])
            ].astype(BF16)


def leave(grad, to_up, to_quarters):
    tokens, width = grad.shape
    whole = lambda shape: pl.BlockSpec(shape, lambda i, a, b: (0, 0))
    shapes = [(tokens // 4, 4 * width)] + [(tokens, width // 4)] * 4
    return pl.pallas_call(
        leave_body,
        out_shape=[jax.ShapeDtypeStruct(shape, BF16) for shape in shapes],
        grid_spec=pltpu.PrefetchScalarGridSpec(
            num_scalar_prefetch=2,
            grid=(1,),
            in_specs=[whole((tokens, width))],
            out_specs=[whole(shape) for shape in shapes],
            scratch_shapes=[pltpu.VMEM((8, tokens, LANES), F32)],
        ),
        compiler_params=pltpu.CompilerParams(vmem_limit_bytes=VMEM_ROOM),
        name="leave",
        cost_estimate=cost(2),
    )(to_up, to_quarters, grad)


TILE = 128
SCALE = 1.0 / math.sqrt(HEAD)


def by_head(x):
    heads = x.shape[1] // HEAD
    feature = lax.broadcasted_iota(jnp.int32, x.shape, 1) // HEAD
    return jnp.concatenate(
        [jnp.where(feature == h, x, jnp.zeros_like(x)) for h in range(heads)], axis=0
    )


def of_heads(x):
    heads = x.shape[1] // HEAD
    feature = lax.broadcasted_iota(jnp.int32, (TILE, x.shape[1]), 1) // HEAD
    out = x[:TILE]
    for h in range(1, heads):
        out = jnp.where(feature == h, x[h * TILE : (h + 1) * TILE], out)
    return out


def visible(column, row):
    i = lax.broadcasted_iota(jnp.int32, (TILE, TILE), 0)
    j = lax.broadcasted_iota(jnp.int32, (TILE, TILE), 1)
    return (column == row) & (i >= j) & (i // ROW == j // ROW)


def soft(query, keys, allowed):
    scores = dot_t(query, keys) * SCALE
    probs = []
    for h in range(scores.shape[1] // TILE):
        part = jnp.where(allowed, scores[:, h * TILE : (h + 1) * TILE], NEG_FILL)
        exps = jnp.exp(part - jnp.max(part, axis=1, keepdims=True))
        probs.append(exps * (1.0 / jnp.sum(exps, axis=1, keepdims=True)))
    return probs


def attend_tile(qkv, allowed):
    n = qkv.shape[1] // 3
    probs = soft(qkv[:, :n], by_head(qkv[:, n : 2 * n]), allowed)
    low = jnp.concatenate([p.astype(BF16) for p in probs], axis=1)
    return dot(low, by_head(qkv[:, 2 * n :])).astype(BF16)


def attend_back_tile(qkv, grad, allowed):
    n = grad.shape[1]
    query = qkv[:, :n]
    keys = by_head(qkv[:, n : 2 * n])
    probs = soft(query, keys, allowed)
    grad_probs = dot_t(grad, by_head(qkv[:, 2 * n :]))
    grads = []
    for h, p in enumerate(probs):
        part = grad_probs[:, h * TILE : (h + 1) * TILE]
        inner = jnp.sum(p * part, axis=1, keepdims=True)
        grads.append((p * (part - inner)).astype(BF16))
    grads = jnp.concatenate(grads, axis=1)
    low = jnp.concatenate([p.astype(BF16) for p in probs], axis=1)
    return jnp.concatenate(
        [
            (dot(grads, keys) * SCALE).astype(BF16),
            (of_heads(gram(grads, query)) * SCALE).astype(BF16),
            of_heads(gram(low, grad)).astype(BF16),
        ],
        axis=1,
    )


def standard(stream):
    mean = jnp.mean(stream, axis=1, keepdims=True)
    centred = stream - mean
    rstd = lax.rsqrt(jnp.mean(centred * centred, axis=1, keepdims=True) + EPSILON)
    return centred * rstd, rstd


def standard_back(normed, rstd, gain, grad):
    scaled = grad * gain
    return rstd * (
        scaled
        - jnp.mean(scaled, axis=1, keepdims=True)
        - normed * jnp.mean(scaled * normed, axis=1, keepdims=True)
    )


LAYER_TILE = 256
SUBS = LAYER_TILE // TILE


def joined(ref, start, stop):
    return ref[:, :, :, start:stop].reshape(-1, stop - start)


def masks(column_ref, row_ref):
    return [
        visible(column_ref[i * TILE : (i + 1) * TILE], row_ref[i]) for i in range(SUBS)
    ]


def forward_body(*refs):
    column_ref, row_ref, stream_ref, vec_ref = refs[:4]
    weights = refs[4:8]
    norm_ref, out_ref, norm_two_ref = refs[8:11]
    qkvs, contexts = refs[11:15], refs[15:19]
    allowed = masks(column_ref, row_ref)
    stream = stream_ref[...]
    normed, _ = standard(stream)
    norm_ref[...] = (normed * vec_ref[0:1] + vec_ref[1:2]).astype(BF16)
    for weight, qkv_ref, context_ref in zip(weights, qkvs, contexts):
        n = context_ref.shape[1]
        qkv_ref[...] = dot(norm_ref[...], joined(weight, 0, 3 * n)).astype(BF16)
        for i in range(SUBS):
            at = slice(i * TILE, (i + 1) * TILE)
            context_ref[at] = attend_tile(qkv_ref[at], allowed[i])
        stream = stream + dot_t(context_ref[...], joined(weight, 3 * n, 4 * n))
    out_ref[...] = stream
    normed, _ = standard(stream)
    norm_two_ref[...] = (normed * vec_ref[2:3] + vec_ref[3:4]).astype(BF16)


def backward_body(*refs):
    column_ref, row_ref, zero_ref, one_ref, vec_ref, keep_ref, core_ref, y_ref, cot_ref = refs[:9]
    weights, qkvs = refs[9:13], refs[13:17]
    att_ref, input_ref, vec_grad_ref = refs[17:20]
    rows = refs[20:24]
    allowed = masks(column_ref, row_ref)
    grad = keep_ref[...] + core_ref[...].astype(F32) + y_ref[...].astype(F32)
    normed, rstd = standard(one_ref[...])
    sums = [jnp.sum(grad * normed, axis=0, keepdims=True), jnp.sum(grad, axis=0, keepdims=True)]
    stream = cot_ref[...].astype(F32) + standard_back(normed, rstd, vec_ref[2:3], grad)
    att_ref[...] = stream.astype(BF16)
    grad = None
    for weight, qkv_ref, row_grad_ref in zip(weights, qkvs, rows):
        n = qkv_ref.shape[1] // 3
        context = dot(att_ref[...], joined(weight, 3 * n, 4 * n)).astype(BF16)
        for i in range(SUBS):
            at = slice(i * TILE, (i + 1) * TILE)
            row_grad_ref[at] = attend_back_tile(qkv_ref[at], context[at], allowed[i])
        part = dot_t(row_grad_ref[...], joined(weight, 0, 3 * n))
        grad = part if grad is None else grad + part
    normed, rstd = standard(zero_ref[...])
    sums = [
        jnp.sum(grad * normed, axis=0, keepdims=True),
        jnp.sum(grad, axis=0, keepdims=True),
    ] + sums
    input_ref[...] = stream + standard_back(normed, rstd, vec_ref[0:1], grad)

    @pl.when(pl.program_id(0) == 0)
    def _():
        vec_grad_ref[...] = jnp.zeros_like(vec_grad_ref)

    for i, v in enumerate(sums):
        vec_grad_ref[i : i + 1] += v


def layer_call(body, segments, arrays, fixed, weights, more, outs, name, us):
    tokens = segments.shape[0]
    wide = lambda w: pl.BlockSpec((LAYER_TILE, w), lambda i: (i, 0))
    still = lambda shape: pl.BlockSpec(shape, lambda i: (0,) * len(shape))
    _, _, n, w = weights[0].shape
    tiles = tokens // TILE
    return pl.pallas_call(
        body,
        out_shape=[jax.ShapeDtypeStruct(shape, dtype) for shape, dtype in outs],
        grid=(tokens // LAYER_TILE,),
        in_specs=[wide(1), pl.BlockSpec((SUBS, 1, TILE), lambda i: (i, 0, 0))]
        + [wide(a.shape[1]) for a in arrays]
        + [still(fixed.shape)]
        + [wide(a.shape[1]) for a in more[0]]
        + [pl.BlockSpec((8, 1, n, w), lambda i, k=k: (0, k, 0, 0)) for k in (0, 0, 1, 1)]
        + [wide(a.shape[1]) for a in more[1]],
        out_specs=[
            wide(shape[1]) if shape[0] == tokens else still(shape) for shape, _ in outs
        ],
        compiler_params=pltpu.CompilerParams(vmem_limit_bytes=VMEM_ROOM),
        name=name,
        cost_estimate=cost(us),
    )(
        segments.reshape(tokens, 1),
        segments.reshape(tiles, 1, TILE),
        *arrays,
        fixed,
        *more[0],
        weights[0],
        weights[1],
        weights[0],
        weights[1],
        *more[1],
    )


def layer_forward(segments, stream, vectors, weights):
    tokens, width = stream.shape
    quarter = width // 4
    outs = (
        [((tokens, width), BF16), ((tokens, width), F32), ((tokens, width), BF16)]
        + [((tokens, 3 * quarter), BF16)] * 4
        + [((tokens, quarter), BF16)] * 4
    )
    norm_one, stream_one, norm_two, *rest = layer_call(
        forward_body, segments, [stream], vectors, weights, ([], []), outs, "layer_forward", 18
    )
    return norm_one, stream_one, norm_two, rest[:4], rest[4:]


def layer_backward(segments, streams, vectors, grads, cot, weights, qkv):
    tokens, width = cot.shape
    outs = [((tokens, width), BF16), ((tokens, width), F32), (vectors.shape, F32)]
    outs += [(q.shape, BF16) for q in qkv]
    return layer_call(
        backward_body, segments, streams, vectors, weights, ([*grads, cot], qkv), outs,
        "layer_backward",
        24,
    )


def layer_grads_body(norm_ref, att_ref, *refs):
    rows, contexts, outs = refs[:4], refs[4:8], refs[8:]
    blocks, _, n, _ = outs[0].shape
    for j in range(4):
        out, k = outs[j & 1], j >> 1
        w = rows[j].shape[1]
        left = gram(norm_ref[...], rows[j][...]).astype(BF16)
        right = gram(att_ref[...], contexts[j][...]).astype(BF16)
        for i in range(blocks):
            out[i, k, :, :w] = left[i * n : (i + 1) * n]
            out[i, k, :, w:] = right[i * n : (i + 1) * n]


def layer_grads(norm, att, rows, contexts):
    tokens, width = norm.shape
    n = width // 8
    part = pl.BlockSpec((tokens, 2 * n), lambda i: (0, i))
    whole = lambda a: pl.BlockSpec(a.shape, lambda i: (0, 0))
    shape = jax.ShapeDtypeStruct((8, 2, n, width), BF16)
    out = pl.BlockSpec((2, 2, n, width), lambda i: (i, 0, 0, 0))
    return pl.pallas_call(
        layer_grads_body,
        out_shape=(shape, shape),
        grid=(4,),
        in_specs=[part, part] + [whole(a) for a in (*rows, *contexts)],
        out_specs=(out, out),
        compiler_params=pltpu.CompilerParams(vmem_limit_bytes=VMEM_ROOM),
        name="layer_grads",
        cost_estimate=cost(8),
    )(norm, att, *rows, *contexts)


def vector_owner(c, x):
    i = jnp.arange(32)
    source = i & 7
    piece = ((i >> 3) ^ c) * 8 + ((((source & 1) ^ x) << 2) | (source >> 1))
    return piece[:, None] == jnp.arange(32)[None, :]


PAD = 16


def vector_rows(vectors):
    ends = [(0, 0)] * (vectors.ndim - 2)
    count, n = vectors.shape[-2:]
    return jnp.pad(vectors, ends + [(0, PAD - count), (0, CELL - n)])


def join_vectors(spreads, n, c, x):
    pieces = jnp.stack([s.reshape(8, -1, PAD, CELL)[:, :, :4, :n] for s in spreads])
    pieces = pieces.transpose(3, 0, 1, 2, 4).reshape(4, 32, -1)
    owner = vector_owner(c, x).astype(BF16)
    full = jnp.einsum("dp,vpn->vdn", owner, pieces, preferred_element_type=F32)
    return full.reshape(4, -1)


def split_vectors(full, n, c, x):
    owner = vector_owner(c, x).astype(F32)
    pieces = jnp.einsum(
        "dp,vdn->pvn",
        owner,
        full.reshape(4, 32, -1),
        precision=lax.Precision.HIGHEST,
        preferred_element_type=F32,
    )
    pieces = pieces.reshape(4, 8, 4, -1, n).swapaxes(2, 3)
    rows = vector_rows(pieces)
    return [rows[j].reshape(-1, CELL) for j in range(4)]


MLP_TILE = 256
TURNS = 8


def order_of(k):
    return ((k & 1) << 1) | (k >> 1)


def mlp_body(index, *refs):
    (n0, n1, n2, n3, q0, q1, q2, q3, in_ref, down_ref, stream_ref) = refs[:11]
    (act_ref, grad_ref, norm_ref, cot_ref, d0, d1, d2, d3, keep_ref, send_ref, mine_ref) = refs[11:22]
    (wide,) = refs[22:]
    tile = pl.program_id(0)
    k = tile // 2
    for at, ref in enumerate((n0, n2, n1, n3)):

        @pl.when(k == at)
        def _(ref=ref):
            norm_ref[...] = ref[...]

    quarters = [pl.ds(pl.multiple_of(index[j] * 256, 256), 256) for j in range(4)]
    for j, ref in enumerate((q0, q1, q2, q3)):
        cot_ref[:, quarters[j]] = ref[...]
    weight_in = in_ref[...].reshape(-1, in_ref.shape[-1])
    weight_down = down_ref[...].reshape(-1, down_ref.shape[-1])
    pre = dot(norm_ref[...], weight_in)
    half = 0.5 + 0.5 * lax.erf(pre * math.sqrt(0.5))
    act = (pre * half).astype(BF16)
    act_ref[...] = act
    slope = half + pre * (math.sqrt(0.5 / math.pi) * jnp.exp(-0.5 * pre * pre))
    grad = (slope * dot(cot_ref[...], weight_down)).astype(BF16)
    grad_ref[...] = grad
    wide[...] = dot_t(act, weight_down)

    @pl.when(tile < 2)
    def _():
        wide[...] = wide[...] + stream_ref[...]
        mine_ref[...] = cot_ref[...]

    for j, ref in enumerate((d0, d1, d2, d3)):
        ref[...] = wide[:, quarters[j]].astype(BF16)
    other = dot_t(grad, weight_in)

    @pl.when(tile < 4)
    def _():
        keep_ref[...] = other

    @pl.when(tile >= 4)
    def _():
        send_ref[...] = other.astype(BF16)


def mlp(norms, cots, weights, stream, index):
    tokens, width = norms[0].shape
    rows, quarter = cots[0].shape
    hidden = weights.shape[-1]
    n = weights.shape[2]
    tile = MLP_TILE
    per = tokens // tile
    assert per == 2
    held = lambda start, count: lambda i, index: (jnp.clip(i - start, 0, count - 1), 0)
    norm_specs = [
        pl.BlockSpec((tile, width), held(2 * order_of(m), 2)) for m in range(4)
    ]
    cot_specs = [
        pl.BlockSpec(
            (tile, quarter),
            lambda i, index, j=j: (
                jnp.bitwise_xor(order_of(i // 2), j) * 2 + lax.rem(i, 2),
                0,
            ),
        )
        for j in range(4)
    ]
    weight_specs = [
        pl.BlockSpec((8, 1, n, hidden), lambda i, index, k=k: (0, k, 0, 0)) for k in range(2)
    ]
    each = lambda w: pl.BlockSpec((tile, w), lambda i, index: (i, 0))
    shape = jax.ShapeDtypeStruct
    return pl.pallas_call(
        mlp_body,
        out_shape=[
            shape((rows, hidden), BF16),
            shape((rows, hidden), BF16),
            shape((rows, width), BF16),
            shape((rows, width), BF16),
            *[shape((rows, quarter), BF16)] * 4,
            shape((rows // 2, width), F32),
            shape((rows // 2, width), BF16),
            shape((tokens, width), BF16),
        ],
        grid_spec=pltpu.PrefetchScalarGridSpec(
            num_scalar_prefetch=1,
            grid=(TURNS,),
            in_specs=norm_specs
            + cot_specs
            + weight_specs
            + [pl.BlockSpec((tile, width), held(0, 2))],
            out_specs=[each(hidden), each(hidden), each(width), each(width)]
            + [each(quarter)] * 4
            + [
                pl.BlockSpec((tile, width), held(0, 4)),
                pl.BlockSpec((tile, width), held(4, 4)),
                pl.BlockSpec((tile, width), held(0, 2)),
            ],
            scratch_shapes=[pltpu.VMEM((tile, width), F32)],
        ),
        compiler_params=pltpu.CompilerParams(vmem_limit_bytes=VMEM_ROOM),
        name="mlp",
        cost_estimate=cost(30),
    )(index, *norms, *cots, weights, weights, stream)


def mlp_grads_body(norm_ref, cot_ref, act_ref, grad_ref, out_ref):
    for k, (left, right) in enumerate(((norm_ref, grad_ref), (cot_ref, act_ref))):
        block = gram(left[...], right[...]).astype(BF16)
        n = out_ref.shape[2]
        for i in range(out_ref.shape[0]):
            out_ref[i, k] = block[i * n : (i + 1) * n]


def mlp_grads(norm, cot, act, grad):
    rows, width = norm.shape
    hidden = act.shape[1]
    n = width // 8
    whole = pl.BlockSpec((rows, hidden), lambda i: (0, 0))
    part = pl.BlockSpec((rows, 2 * n), lambda i: (0, i))
    return pl.pallas_call(
        mlp_grads_body,
        out_shape=jax.ShapeDtypeStruct((8, 2, n, hidden), BF16),
        grid=(4,),
        in_specs=[part, part, whole, whole],
        out_specs=pl.BlockSpec((2, 2, n, hidden), lambda i: (i, 0, 0, 0)),
        compiler_params=pltpu.CompilerParams(vmem_limit_bytes=VMEM_ROOM),
        name="mlp_grads",
        cost_estimate=cost(14),
    )(norm, cot, act, grad)


def join_rows(packed):
    pieces, _, n, w = packed.shape
    return (
        packed.reshape(8, pieces // 8, 2, n, w).swapaxes(1, 2).reshape(8, 2, n * pieces // 8, w)
    )


def split_rows(packed):
    _, _, n, w = packed.shape
    share = lax.axis_size("seq") // 8
    return (
        packed.reshape(8, 2, share, n // share, w).swapaxes(1, 2).reshape(8 * share, 2, n // share, w)
    )


def edges(cells):
    count = lax.axis_size("seq")
    head, tail = cells
    return (
        lax.ppermute(tail, "seq", [(i, i + 1) for i in range(count - 1)]),
        lax.ppermute(head, "seq", [(i + 1, i) for i in range(count - 1)]),
    )


def on_device(
    inputs,
    coarse_ids,
    segment_ids,
    cotangent,
    embed_table,
    conv_weight,
    res_weight,
    up_weight,
    gain_one,
    shift_one,
    qkv_weight,
    out_weight,
    gain_two,
    shift_two,
    in_weight,
    down_weight,
):
    c, x = place()
    micros, tokens, quarter = inputs.shape
    width = 4 * quarter
    coarse = coarse_ids.shape[1]
    step = CONV_DILATION
    slot = jnp.arange(8, dtype=jnp.int32)
    quarters = (((slot >> 1) ^ c) << 1) | (slot & 1)

    line = Line()
    stream_in = line.exchange(pick([inputs[i] for i in range(4)], c))
    attn_shard = jnp.concatenate([qkv_weight.reshape(-1, 3 * quarter), out_weight.T], axis=1)
    attn_shard = jnp.stack([attn_shard, *line.send((attn_shard, 2))])
    mlp_shard = jnp.stack([in_weight, down_weight.T])
    cots = line.spread(jnp.concatenate(pick([cotangent[i] for i in range(4)], c), axis=0))

    lot = gain_one.shape[0]
    vectors = vector_rows(jnp.stack([gain_one, shift_one, gain_two, shift_two]))
    conv_shard = conv_weight.transpose(2, 0, 1).reshape(-1, 3 * quarter)
    groups = ((embed_table, conv_shard, vectors), (res_weight, up_weight.T))
    if tuned():
        first, second = (bundle(group) for group in groups)
        first = along_z(jnp.broadcast_to(first, (4,) + first.shape))
        second = after(second, first, *stream_in, attn_shard)
        second = along_z(jnp.broadcast_to(second, (4,) + second.shape))
        first_far = hop(first, 1)
        second_far = hop(after(second, first_far), 1)
        table, conv, vectors = unpack(first, after(first_far, *cots), [w.shape for w in groups[0]])
        attn_shard = after(attn_shard, second, table)
        res, up = unpack(second, second_far, [w.shape for w in groups[1]])
    else:
        (table, conv, vectors), (res, up) = (gather_plain(group) for group in groups)
    attn_w = lax.all_gather(attn_shard, "seq", axis=0)
    mlp_w = lax.all_gather(after(mlp_shard, attn_w), "seq", axis=0)
    vectors = jnp.pad(join_vectors(line.spread(vectors), lot, c, x), ((0, 4), (0, 0)))

    ids = jnp.concatenate(pick([coarse_ids[i] for i in range(4)], c))
    vocab = table.shape[0]
    code = jnp.arange(vocab, dtype=jnp.int32)
    block = vocab // 8
    slot_of = code // block
    code = (((slot_of & 3) << 1) | ((slot_of >> 2) ^ x)) * block + code % block
    onehot = (ids[:, None] == code[None, :]).astype(BF16)
    embed = dot(onehot, table)
    act = gelu(embed).astype(BF16).reshape(micros, coarse, quarter)
    prior, later = edges((act[:, :step], act[:, coarse - step :]))
    padded = jnp.concatenate([prior, act, later], axis=1)
    taps = jnp.concatenate(
        [padded[:, k * step : k * step + coarse] for k in range(3)], axis=2
    ).reshape(micros * coarse, 3 * quarter)
    conv_terms = dot_t(taps, conv).reshape(micros, coarse, width)
    conv_out = fold(line, [conv_terms[j] for j in range(4)])
    mixed = after(gelu(conv_out).astype(BF16), res, up)
    mixed_all = jnp.concatenate(line.spread(mixed), axis=0)
    hidden = (embed + dot(mixed_all, res)).astype(BF16)
    up_terms = dot_t(hidden, up).reshape(micros, coarse, 4 * width)
    up_terms = fold(line, [up_terms[j] for j in range(4)])
    i = jnp.arange(32, dtype=jnp.int32)
    from_up = (((i >> 2) & 1) ^ x) * 16 + (i >> 3) * 4 + (i & 3)
    to_up = ((i >> 2) & 3) * 8 + ((i >> 4) ^ x) * 4 + (i & 3)
    stream_zero = enter(up_terms, stream_in, from_up, quarters)
    segments = lax.dynamic_index_in_dim(segment_ids, c, 0, keepdims=False)
    attn_w = join_rows(attn_w)
    attn_w = (attn_w, swap(attn_w, 1))
    norm_one, stream_one, norm_two, qkv, context = layer_forward(
        segments, stream_zero, vectors, attn_w
    )

    norm_all = line.spread(norm_two)
    mlp_act, grad_pre, norm_rows, cot_rows, *outs, keep, send, cot_mine = mlp(
        norm_all, cots, join_rows(mlp_w), stream_one, jnp.arange(4, dtype=jnp.int32) ^ c
    )
    from_core = swap(send, 1)
    over_y = (keep[tokens:] + from_core[tokens:].astype(F32)).astype(BF16)
    (from_y,) = line.send((over_y, 2))
    grad_mlp = mlp_grads(after(norm_rows, over_y), cot_rows, mlp_act, grad_pre)
    turned = lambda v, j: jnp.stack([v[m ^ order_of(j)] for m in range(4)])
    result, over_y = fold_core(
        [d.reshape(micros, tokens, quarter) for d in outs], fix=turned
    )
    terms = lax.optimization_barrier((keep, from_core, from_y, grad_mlp, over_y))
    grads, over_y = terms[:3], terms[4]
    (from_y,) = line.send((over_y, 2))
    result = (result + turned(from_y, 2).astype(F32)).astype(BF16)
    act_done = from_y
    result = jnp.stack(pick([result[order_of(m)] for m in range(4)], c))
    grad_mlp = lax.psum_scatter(split_rows(terms[3]), "seq", scatter_dimension=0, tiled=False)
    grad_in, grad_down = grad_mlp[0].astype(F32), grad_mlp[1].astype(F32).T

    att, input_grad, grad_vectors, *grad_rows = layer_backward(
        segments, [stream_zero, stream_one], vectors, grads, cot_mine, attn_w, qkv
    )
    grad_vectors = split_vectors(grad_vectors[:4], lot, c, x)
    leave_rows, *grad_in_q = leave(input_grad, to_up, quarters)
    grad_rows[0] = after(grad_rows[0], leave_rows, act_done)
    grad_attn, send = layer_grads(norm_one, att, grad_rows, context)
    grad_up_rows = line.spread(leave_rows)
    grad_attn = grad_attn.astype(F32) + swap(send, 1).astype(F32)
    grad_attn = split_rows(grad_attn.astype(BF16))
    grad_up_rows = jnp.concatenate(grad_up_rows, axis=0)
    grad_hidden = dot(grad_up_rows, up)
    grad_low = grad_hidden.astype(BF16)
    grad_up = gram(grad_up_rows, hidden).astype(BF16)
    grad_res = gram(mixed_all, grad_low).astype(BF16)
    up_started = cross_x([grad_res, grad_up])
    grad_mixed = dot_t(after(grad_low, grad_up, grad_res), res).reshape(micros, coarse, width)
    grad_mixed, over_y = fold_core([grad_mixed[j] for j in range(4)])
    grad_attn = after(grad_attn, grad_mlp, over_y)
    grad_attn = lax.psum_scatter(grad_attn, "seq", scatter_dimension=0, tiled=False)
    grad_mixed = grad_mixed + line.send((over_y, 2))[0].astype(F32)
    grad_conv_low = after((gelu_grad(conv_out) * grad_mixed).astype(BF16), grad_mlp, up_started[1])

    grad_conv_all = jnp.concatenate(line.spread(grad_conv_low), axis=0)
    grad_taps = dot(grad_conv_all, conv).reshape(micros, coarse, 3 * quarter)
    tap = [grad_taps[:, :, k * quarter : (k + 1) * quarter] for k in range(3)]
    rims = tap[0][:, :step].astype(BF16), tap[2][:, coarse - step :].astype(BF16)
    prior, later = edges(rims)
    grad_conv = gram(grad_conv_all, taps).astype(BF16)
    grad_vectors = fold(line, grad_vectors)
    grad_act = (
        tap[1]
        + jnp.concatenate([tap[0][:, step:], later.astype(F32)], axis=1)
        + jnp.concatenate([prior.astype(F32), tap[2][:, : coarse - step]], axis=1)
    ).reshape(micros * coarse, quarter)
    grad_embed = (grad_hidden + gelu_grad(embed) * grad_act).astype(BF16)
    started = cross_x([gram(onehot, grad_embed), grad_conv, grad_vectors])
    up_started = after(up_started, started[0])
    grad_res, grad_up = cross_z(up_started, [w.shape for w in groups[1]])
    grad_table, grad_conv, grad_vectors = cross_z(started, [w.shape for w in groups[0]])
    grad_conv = grad_conv.reshape(-1, 3, quarter).transpose(1, 2, 0)
    input_grads = jnp.stack(pick(line.exchange(grad_in_q), c))
    grad_attn = grad_attn[0].astype(F32) + line.send((grad_attn[1], 2))[0].astype(F32)
    grad_qkv, grad_out = grad_attn[:, : 3 * quarter], grad_attn[:, 3 * quarter :]
    grad_vectors = [grad_vectors[i, :lot] for i in range(4)]
    return (
        result,
        input_grads,
        grad_table,
        grad_conv,
        grad_res,
        grad_up.T,
        grad_vectors[0],
        grad_vectors[1],
        grad_qkv.reshape(qkv_weight.shape),
        grad_out.T,
        grad_vectors[2],
        grad_vectors[3],
        grad_in,
        grad_down,
    )


def solution(mesh):
    wide = P(("cond", "seq"))
    acts = P(None, "seq", "cond")
    weights = (
        P("seq", "cond"),
        P(None, "cond", "seq"),
        P("seq", "cond"),
        P("cond", "seq"),
        wide,
        wide,
        P("seq", None, "cond"),
        P("cond", "seq"),
        wide,
        wide,
        P("seq", "cond"),
        P("cond", "seq"),
    )
    return jax.shard_map(
        on_device,
        mesh=mesh,
        in_specs=(acts, P(None, "seq"), P(None, "seq"), acts) + weights,
        out_specs=(acts, acts) + weights,
        check_vma=False,
    )
```

```python
import math

import jax
import jax.numpy as jnp
from jax import lax
from jax.experimental import pallas as pl
from jax.experimental.pallas import tpu as pltpu
from jax.sharding import PartitionSpec as P

HEAD = 64
ROW = 64
CONV_DILATION = 27
EPSILON = 1e-05
NEG_FILL = -1e30
LANES = 128
BF16 = jnp.bfloat16
F32 = jnp.float32


def tuned():
    return lax.axis_size("seq") == 8


def swap(x, j):
    return lax.ppermute(x, "cond", [(i, i ^ j) for i in range(4)])


def hop(x, k):
    return lax.ppermute(x, "seq", [(i, i ^ k) for i in range(8)])


def place():
    c = lax.axis_index("cond")
    return c, (lax.axis_index("seq") & 1 if tuned() else jnp.zeros((), jnp.int32))


def after(value, *before):
    return lax.optimization_barrier((value, *before))[0]


def dot(a, b, dims=((1,), (0,))):
    return lax.dot_general(a, b, (dims, ((), ())), preferred_element_type=F32)


def gram(a, b):
    return dot(a, b, ((0,), (0,)))


def dot_t(a, b):
    return dot(a, b, ((1,), (1,)))


def gelu(v):
    return 0.5 * v * (1.0 + lax.erf(v * math.sqrt(0.5)))


def gelu_grad(v):
    return 0.5 * (1.0 + lax.erf(v * math.sqrt(0.5))) + v * (
        math.sqrt(0.5 / math.pi) * jnp.exp(-0.5 * v * v)
    )


def pick(items, t):
    low, high = (t & 1) == 1, (t & 2) == 2
    items = [jnp.where(low, items[i ^ 1], items[i]) for i in range(4)]
    return [jnp.where(high, items[i ^ 2], items[i]) for i in range(4)]


def regroup(x, dim, outer, inner):
    n = x.shape[dim] // 8
    shape = x.shape
    x = x.reshape(shape[:dim] + (outer, inner, n) + shape[dim + 1 :])
    return jnp.swapaxes(x, dim, dim + 1).reshape(shape)


def cost(us):
    return pl.CostEstimate(flops=int(us * 1.1e9), transcendentals=0, bytes_accessed=0)


CELL = 256
ALONG_Z = [[0, 2, 4, 6], [1, 3, 5, 7]]
VMEM_ROOM = 48 * 1024 * 1024


def bundle(shards):
    return jnp.concatenate(
        [s[:, i : i + CELL] for s in shards for i in range(0, s.shape[1], CELL)], axis=0
    )


def along_z(x):
    return lax.all_to_all(x, "seq", 0, 0, axis_index_groups=ALONG_Z, tiled=True)


def unpack_body(shapes, near_ref, far_ref, *outs):
    p = pl.program_id(0)

    def copy(ref):
        at = 0
        for (r, w), out in zip(shapes, outs):
            for i in range(0, w, CELL):
                out[:, i : i + CELL] = ref[0, at : at + r]
                at += r

    pl.when(p < 4)(lambda: copy(near_ref))
    pl.when(p >= 4)(lambda: copy(far_ref))


def unpack(near, far, shapes):
    block = (1,) + near.shape[1:]
    return pl.pallas_call(
        lambda *refs: unpack_body(shapes, *refs),
        out_shape=[jax.ShapeDtypeStruct((8 * r, w), near.dtype) for r, w in shapes],
        grid=(8,),
        in_specs=[
            pl.BlockSpec(block, lambda p: (jnp.minimum(p, 3), 0, 0)),
            pl.BlockSpec(block, lambda p: (jnp.maximum(p - 4, 0), 0, 0)),
        ],
        out_specs=[pl.BlockSpec((r, w), lambda p: (p, 0)) for r, w in shapes],
        compiler_params=pltpu.CompilerParams(vmem_limit_bytes=VMEM_ROOM),
        name="unpack",
        cost_estimate=cost(3),
    )(near, far)


def gather_plain(shards):
    return [regroup(lax.all_gather(s, "seq", axis=0, tiled=True), 0, 4, 2) for s in shards]


def pack_body(count, *refs):
    half, at = pl.program_id(0), 0
    for ref in refs[:count]:
        r, w = ref.shape
        for i in range(0, w, CELL):
            for k, out in enumerate(refs[count:]):

                @pl.when(half == k)
                def _(out=out, ref=ref, at=at, r=r, i=i):
                    out[0, at : at + r] = ref[:, i : i + CELL]

            at += r


def pack(grads):
    shapes = [(g.shape[0] // 8, g.shape[1]) for g in grads]
    rows = sum(r * w for r, w in shapes) // CELL
    shape = jax.ShapeDtypeStruct((4, rows, CELL), BF16)
    return pl.pallas_call(
        lambda *refs: pack_body(len(grads), *refs),
        out_shape=(shape, shape),
        grid=(2, 4),
        in_specs=[pl.BlockSpec((r, w), lambda h, p: (4 * h + p, 0)) for r, w in shapes],
        out_specs=(
            pl.BlockSpec((1, rows, CELL), lambda h, p: (jnp.where(h == 0, p, 3), 0, 0)),
            pl.BlockSpec((1, rows, CELL), lambda h, p: (jnp.where(h == 1, p, 0), 0, 0)),
        ),
        compiler_params=pltpu.CompilerParams(vmem_limit_bytes=VMEM_ROOM),
        name="pack",
        cost_estimate=cost(2),
    )(*grads)


def total_body(shapes, in_ref, *outs):
    at = 0
    for (r, w), out in zip(shapes, outs):
        for i in range(0, w, CELL):
            cells = [in_ref[k, at : at + r].astype(F32) for k in range(4)]
            out[:, i : i + CELL] = (cells[0] + cells[1]) + (cells[2] + cells[3])
            at += r


def total(parts, shapes):
    return pl.pallas_call(
        lambda *refs: total_body(shapes, *refs),
        out_shape=[jax.ShapeDtypeStruct(shape, F32) for shape in shapes],
        compiler_params=pltpu.CompilerParams(vmem_limit_bytes=VMEM_ROOM),
        name="total",
        cost_estimate=cost(1),
    )(parts)


def cross_x(grads):
    grads = [g.astype(BF16) for g in grads]
    if tuned():
        near, far = pack(grads)
        return near, hop(far, 1)
    return grads


def cross_z(started, shapes):
    if tuned():
        near, far = started
        return total(along_z((near.astype(F32) + far.astype(F32)).astype(BF16)), shapes)
    return [
        lax.psum_scatter(
            regroup(g, 0, 2, 4), "seq", scatter_dimension=0, tiled=True
        ).astype(F32)
        for g in started
    ]


class Line:
    def __init__(self):
        self.last = ()

    def send(self, *items):
        items = [(after(x, *self.last) if self.last else x, j) for x, j in items]
        self.last = [swap(x, j) for x, j in items]
        return self.last

    def spread(self, x):
        (y,) = self.send((x, 2))
        return [x, swap(x, 1), y, swap(y, 1)]

    def exchange(self, items):
        two, three = self.send((items[2], 2), (items[3], 3))
        return [items[0], swap(items[1], 1), two, three]


def same(x, j):
    return x


def fold_core(items, wire=BF16, fix=same):
    one = fix(swap(items[1].astype(wire), 1), 1).astype(F32)
    three = fix(swap(items[3].astype(wire), 1), 1).astype(F32)
    return items[0].astype(F32) + one, (items[2].astype(F32) + three).astype(wire)


def fold(line, items, wire=BF16, fix=same):
    zero, two = fold_core(items, wire, fix)
    return zero + fix(line.send((two, 2))[0], 2).astype(F32)


def lane_block(i):
    return pl.ds(pl.multiple_of(i * LANES, LANES), LANES)


def enter_body(from_up, to_layer, up_ref, q0, q1, q2, q3, out_ref, held, spaced):
    coarse = up_ref.shape[0]
    quarter = q0.shape[1]
    for j, ref in enumerate((q0, q1, q2, q3)):
        held[:, j * quarter : (j + 1) * quarter] = ref[...]
    for r in range(4):
        for p in range(8):
            spaced[p, pl.ds(r, coarse, stride=4), :] = up_ref[:, lane_block(from_up[r * 8 + p])]
    for p in range(8):
        out_ref[:, p * LANES : (p + 1) * LANES] = spaced[p] + held[
            :, lane_block(to_layer[p])
        ].astype(F32)


def enter(up_terms, quarters, from_up, to_layer):
    coarse, wide = up_terms.shape
    whole = lambda shape: pl.BlockSpec(shape, lambda i, a, b: (0, 0))
    tokens, quarter = quarters[0].shape
    return pl.pallas_call(
        enter_body,
        out_shape=jax.ShapeDtypeStruct((tokens, wide // 4), F32),
        grid_spec=pltpu.PrefetchScalarGridSpec(
            num_scalar_prefetch=2,
            grid=(1,),
            in_specs=[whole((coarse, wide))] + [whole((tokens, quarter))] * 4,
            out_specs=whole((tokens, wide // 4)),
            scratch_shapes=[
                pltpu.VMEM((tokens, wide // 4), BF16),
                pltpu.VMEM((8, tokens, LANES), F32),
            ],
        ),
        compiler_params=pltpu.CompilerParams(vmem_limit_bytes=VMEM_ROOM),
        name="enter",
        cost_estimate=cost(2),
    )(from_up, to_layer, up_terms, *quarters)


def leave_body(to_up, to_quarters, in_ref, rows_ref, q0, q1, q2, q3, spaced):
    coarse = rows_ref.shape[0]
    for p in range(8):
        spaced[p] = in_ref[:, p * LANES : (p + 1) * LANES]
    for i in range(32):
        source = to_up[i]
        rows_ref[:, i * LANES : (i + 1) * LANES] = spaced[
            source & 7, pl.ds(source >> 3, coarse, stride=4), :
        ].astype(BF16)
    for j, ref in enumerate((q0, q1, q2, q3)):
        for half in range(2):
            ref[:, half * LANES : (half + 1) * LANES] = in_ref[
                :, lane_block(to_quarters[2 * j + half])
            ].astype(BF16)


def leave(grad, to_up, to_quarters):
    tokens, width = grad.shape
    whole = lambda shape: pl.BlockSpec(shape, lambda i, a, b: (0, 0))
    shapes = [(tokens // 4, 4 * width)] + [(tokens, width // 4)] * 4
    return pl.pallas_call(
        leave_body,
        out_shape=[jax.ShapeDtypeStruct(shape, BF16) for shape in shapes],
        grid_spec=pltpu.PrefetchScalarGridSpec(
            num_scalar_prefetch=2,
            grid=(1,),
            in_specs=[whole((tokens, width))],
            out_specs=[whole(shape) for shape in shapes],
            scratch_shapes=[pltpu.VMEM((8, tokens, LANES), F32)],
        ),
        compiler_params=pltpu.CompilerParams(vmem_limit_bytes=VMEM_ROOM),
        name="leave",
        cost_estimate=cost(2),
    )(to_up, to_quarters, grad)


TILE = 128
SCALE = 1.0 / math.sqrt(HEAD)


def by_head(x):
    heads = x.shape[1] // HEAD
    feature = lax.broadcasted_iota(jnp.int32, x.shape, 1) // HEAD
    return jnp.concatenate(
        [jnp.where(feature == h, x, jnp.zeros_like(x)) for h in range(heads)], axis=0
    )


def of_heads(x):
    heads = x.shape[1] // HEAD
    feature = lax.broadcasted_iota(jnp.int32, (TILE, x.shape[1]), 1) // HEAD
    out = x[:TILE]
    for h in range(1, heads):
        out = jnp.where(feature == h, x[h * TILE : (h + 1) * TILE], out)
    return out


def visible(column, row):
    i = lax.broadcasted_iota(jnp.int32, (TILE, TILE), 0)
    j = lax.broadcasted_iota(jnp.int32, (TILE, TILE), 1)
    return (column == row) & (i >= j) & (i // ROW == j // ROW)


def soft(query, keys, allowed):
    scores = dot_t(query, keys) * SCALE
    probs = []
    for h in range(scores.shape[1] // TILE):
        part = jnp.where(allowed, scores[:, h * TILE : (h + 1) * TILE], NEG_FILL)
        exps = jnp.exp(part - jnp.max(part, axis=1, keepdims=True))
        probs.append(exps * (1.0 / jnp.sum(exps, axis=1, keepdims=True)))
    return probs


def attend_tile(qkv, allowed):
    n = qkv.shape[1] // 3
    probs = soft(qkv[:, :n], by_head(qkv[:, n : 2 * n]), allowed)
    low = jnp.concatenate([p.astype(BF16) for p in probs], axis=1)
    return dot(low, by_head(qkv[:, 2 * n :])).astype(BF16)


def attend_back_tile(qkv, grad, allowed):
    n = grad.shape[1]
    query = qkv[:, :n]
    keys = by_head(qkv[:, n : 2 * n])
    probs = soft(query, keys, allowed)
    grad_probs = dot_t(grad, by_head(qkv[:, 2 * n :]))
    grads = []
    for h, p in enumerate(probs):
        part = grad_probs[:, h * TILE : (h + 1) * TILE]
        inner = jnp.sum(p * part, axis=1, keepdims=True)
        grads.append((p * (part - inner)).astype(BF16))
    grads = jnp.concatenate(grads, axis=1)
    low = jnp.concatenate([p.astype(BF16) for p in probs], axis=1)
    return jnp.concatenate(
        [
            (dot(grads, keys) * SCALE).astype(BF16),
            (of_heads(gram(grads, query)) * SCALE).astype(BF16),
            of_heads(gram(low, grad)).astype(BF16),
        ],
        axis=1,
    )


def standard(stream):
    mean = jnp.mean(stream, axis=1, keepdims=True)
    centred = stream - mean
    rstd = lax.rsqrt(jnp.mean(centred * centred, axis=1, keepdims=True) + EPSILON)
    return centred * rstd, rstd


def standard_back(normed, rstd, gain, grad):
    scaled = grad * gain
    return rstd * (
        scaled
        - jnp.mean(scaled, axis=1, keepdims=True)
        - normed * jnp.mean(scaled * normed, axis=1, keepdims=True)
    )


ANYWHERE = jax.ShapeDtypeStruct
LAYER_TILE = 256
SUBS = LAYER_TILE // TILE


def joined(ref, start, stop):
    return ref[:, :, :, start:stop].reshape(-1, stop - start)


def masks(column_ref, row_ref):
    return [
        visible(column_ref[i * TILE : (i + 1) * TILE], row_ref[i]) for i in range(SUBS)
    ]


def forward_body(*refs):
    column_ref, row_ref, stream_ref, vec_ref = refs[:4]
    weights = refs[4:8]
    norm_ref, out_ref, norm_two_ref = refs[8:11]
    qkvs, contexts = refs[11:15], refs[15:19]
    allowed = masks(column_ref, row_ref)
    stream = stream_ref[...]
    normed, _ = standard(stream)
    norm_ref[...] = (normed * vec_ref[0:1] + vec_ref[1:2]).astype(BF16)
    for weight, qkv_ref, context_ref in zip(weights, qkvs, contexts):
        n = context_ref.shape[1]
        qkv_ref[...] = dot(norm_ref[...], joined(weight, 0, 3 * n)).astype(BF16)
        for i in range(SUBS):
            at = slice(i * TILE, (i + 1) * TILE)
            context_ref[at] = attend_tile(qkv_ref[at], allowed[i])
        stream = stream + dot_t(context_ref[...], joined(weight, 3 * n, 4 * n))
    out_ref[...] = stream
    normed, _ = standard(stream)
    norm_two_ref[...] = (normed * vec_ref[2:3] + vec_ref[3:4]).astype(BF16)


def backward_body(*refs):
    column_ref, row_ref, zero_ref, one_ref, vec_ref, keep_ref, core_ref, y_ref, cot_ref = refs[:9]
    weights, qkvs = refs[9:13], refs[13:17]
    att_ref, input_ref, vec_grad_ref = refs[17:20]
    rows = refs[20:24]
    allowed = masks(column_ref, row_ref)
    grad = keep_ref[...] + core_ref[...].astype(F32) + y_ref[...].astype(F32)
    normed, rstd = standard(one_ref[...])
    sums = [jnp.sum(grad * normed, axis=0, keepdims=True), jnp.sum(grad, axis=0, keepdims=True)]
    stream = cot_ref[...].astype(F32) + standard_back(normed, rstd, vec_ref[2:3], grad)
    att_ref[...] = stream.astype(BF16)
    grad = None
    for weight, qkv_ref, row_grad_ref in zip(weights, qkvs, rows):
        n = qkv_ref.shape[1] // 3
        context = dot(att_ref[...], joined(weight, 3 * n, 4 * n)).astype(BF16)
        for i in range(SUBS):
            at = slice(i * TILE, (i + 1) * TILE)
            row_grad_ref[at] = attend_back_tile(qkv_ref[at], context[at], allowed[i])
        part = dot_t(row_grad_ref[...], joined(weight, 0, 3 * n))
        grad = part if grad is None else grad + part
    normed, rstd = standard(zero_ref[...])
    sums = [
        jnp.sum(grad * normed, axis=0, keepdims=True),
        jnp.sum(grad, axis=0, keepdims=True),
    ] + sums
    input_ref[...] = stream + standard_back(normed, rstd, vec_ref[0:1], grad)

    @pl.when(pl.program_id(0) == 0)
    def _():
        vec_grad_ref[...] = jnp.zeros_like(vec_grad_ref)

    for i, v in enumerate(sums):
        vec_grad_ref[i : i + 1] += v


def layer_call(body, segments, arrays, fixed, weights, more, outs, name, us):
    tokens = segments.shape[0]
    wide = lambda w: pl.BlockSpec((LAYER_TILE, w), lambda i: (i, 0))
    still = lambda shape: pl.BlockSpec(shape, lambda i: (0,) * len(shape))
    _, _, n, w = weights[0].shape
    tiles = tokens // TILE
    return pl.pallas_call(
        body,
        out_shape=[space(shape, dtype) for space, shape, dtype in outs],
        grid=(tokens // LAYER_TILE,),
        in_specs=[wide(1), pl.BlockSpec((SUBS, 1, TILE), lambda i: (i, 0, 0))]
        + [wide(a.shape[1]) for a in arrays]
        + [still(fixed.shape)]
        + [wide(a.shape[1]) for a in more[0]]
        + [pl.BlockSpec((8, 1, n, w), lambda i, k=k: (0, k, 0, 0)) for k in (0, 0, 1, 1)]
        + [wide(a.shape[1]) for a in more[1]],
        out_specs=[
            wide(shape[1]) if shape[0] == tokens else still(shape) for _, shape, _ in outs
        ],
        compiler_params=pltpu.CompilerParams(vmem_limit_bytes=VMEM_ROOM),
        name=name,
        cost_estimate=cost(us),
    )(
        segments.reshape(tokens, 1),
        segments.reshape(tiles, 1, TILE),
        *arrays,
        fixed,
        *more[0],
        weights[0],
        weights[1],
        weights[0],
        weights[1],
        *more[1],
    )


def layer_forward(segments, stream, vectors, weights):
    tokens, width = stream.shape
    quarter = width // 4
    outs = (
        [
            (pltpu.HBM, (tokens, width), BF16),
            (ANYWHERE, (tokens, width), F32),
            (ANYWHERE, (tokens, width), BF16),
        ]
        + [(pltpu.HBM, (tokens, 3 * quarter), BF16)] * 4
        + [(pltpu.HBM, (tokens, quarter), BF16)] * 4
    )
    norm_one, stream_one, norm_two, *rest = layer_call(
        forward_body, segments, [stream], vectors, weights, ([], []), outs, "layer_forward", 18
    )
    return norm_one, stream_one, norm_two, rest[:4], rest[4:]


def layer_backward(segments, streams, vectors, grads, cot, weights, qkv):
    tokens, width = cot.shape
    outs = [
        (ANYWHERE, (tokens, width), BF16),
        (ANYWHERE, (tokens, width), F32),
        (ANYWHERE, vectors.shape, F32),
    ]
    outs += [(ANYWHERE, q.shape, BF16) for q in qkv]
    return layer_call(
        backward_body, segments, streams, vectors, weights, ([*grads, cot], qkv), outs,
        "layer_backward",
        24,
    )


def layer_grads_body(norm_ref, att_ref, *refs):
    rows, contexts, outs = refs[:4], refs[4:8], refs[8:]
    blocks, _, n, _ = outs[0].shape
    for j in range(4):
        out, k = outs[j & 1], j >> 1
        w = rows[j].shape[1]
        left = gram(norm_ref[...], rows[j][...]).astype(BF16)
        right = gram(att_ref[...], contexts[j][...]).astype(BF16)
        for i in range(blocks):
            out[i, k, :, :w] = left[i * n : (i + 1) * n]
            out[i, k, :, w:] = right[i * n : (i + 1) * n]


def layer_grads(norm, att, rows, contexts):
    tokens, width = norm.shape
    n = width // 8
    part = pl.BlockSpec((tokens, 2 * n), lambda i: (0, i))
    whole = lambda a: pl.BlockSpec(a.shape, lambda i: (0, 0))
    shape = jax.ShapeDtypeStruct((8, 2, n, width), BF16)
    out = pl.BlockSpec((2, 2, n, width), lambda i: (i, 0, 0, 0))
    return pl.pallas_call(
        layer_grads_body,
        out_shape=(shape, shape),
        grid=(4,),
        in_specs=[part, part] + [whole(a) for a in (*rows, *contexts)],
        out_specs=(out, out),
        compiler_params=pltpu.CompilerParams(vmem_limit_bytes=VMEM_ROOM),
        name="layer_grads",
        cost_estimate=cost(8),
    )(norm, att, *rows, *contexts)


def vector_owner(c, x):
    i = jnp.arange(32)
    source = i & 7
    piece = ((i >> 3) ^ c) * 8 + ((((source & 1) ^ x) << 2) | (source >> 1))
    return piece[:, None] == jnp.arange(32)[None, :]


PAD = 16


def vector_rows(vectors):
    ends = [(0, 0)] * (vectors.ndim - 2)
    count, n = vectors.shape[-2:]
    return jnp.pad(vectors, ends + [(0, PAD - count), (0, CELL - n)])


def join_vectors(spreads, n, c, x):
    pieces = jnp.stack([s.reshape(8, -1, PAD, CELL)[:, :, :4, :n] for s in spreads])
    pieces = pieces.transpose(3, 0, 1, 2, 4).reshape(4, 32, -1)
    owner = vector_owner(c, x).astype(BF16)
    full = jnp.einsum("dp,vpn->vdn", owner, pieces, preferred_element_type=F32)
    return full.reshape(4, -1)


def split_vectors(full, n, c, x):
    owner = vector_owner(c, x).astype(F32)
    pieces = jnp.einsum(
        "dp,vdn->pvn",
        owner,
        full.reshape(4, 32, -1),
        precision=lax.Precision.HIGHEST,
        preferred_element_type=F32,
    )
    pieces = pieces.reshape(4, 8, 4, -1, n).swapaxes(2, 3)
    rows = vector_rows(pieces)
    return [rows[j].reshape(-1, CELL) for j in range(4)]


MLP_TILE = 256
TURNS = 8


def order_of(k):
    return ((k & 1) << 1) | (k >> 1)


def mlp_body(index, *refs):
    (n0, n1, n2, n3, q0, q1, q2, q3, in_ref, down_ref, stream_ref) = refs[:11]
    (act_ref, grad_ref, norm_ref, cot_ref, d0, d1, d2, d3, keep_ref, send_ref, mine_ref) = refs[11:22]
    (wide,) = refs[22:]
    tile = pl.program_id(0)
    k = tile // 2
    for at, ref in enumerate((n0, n2, n1, n3)):

        @pl.when(k == at)
        def _(ref=ref):
            norm_ref[...] = ref[...]

    quarters = [pl.ds(pl.multiple_of(index[j] * 256, 256), 256) for j in range(4)]
    for j, ref in enumerate((q0, q1, q2, q3)):
        cot_ref[:, quarters[j]] = ref[...]
    weight_in = in_ref[...].reshape(-1, in_ref.shape[-1])
    weight_down = down_ref[...].reshape(-1, down_ref.shape[-1])
    pre = dot(norm_ref[...], weight_in)
    half = 0.5 + 0.5 * lax.erf(pre * math.sqrt(0.5))
    act = (pre * half).astype(BF16)
    act_ref[...] = act
    slope = half + pre * (math.sqrt(0.5 / math.pi) * jnp.exp(-0.5 * pre * pre))
    grad = (slope * dot(cot_ref[...], weight_down)).astype(BF16)
    grad_ref[...] = grad
    wide[...] = dot_t(act, weight_down)

    @pl.when(tile < 2)
    def _():
        wide[...] = wide[...] + stream_ref[...]
        mine_ref[...] = cot_ref[...]

    for j, ref in enumerate((d0, d1, d2, d3)):
        ref[...] = wide[:, quarters[j]].astype(BF16)
    other = dot_t(grad, weight_in)

    @pl.when(tile < 4)
    def _():
        keep_ref[...] = other

    @pl.when(tile >= 4)
    def _():
        send_ref[...] = other.astype(BF16)


def mlp(norms, cots, weights, stream, index):
    tokens, width = norms[0].shape
    rows, quarter = cots[0].shape
    hidden = weights.shape[-1]
    n = weights.shape[2]
    tile = MLP_TILE
    per = tokens // tile
    assert per == 2
    held = lambda start, count: lambda i, index: (jnp.clip(i - start, 0, count - 1), 0)
    norm_specs = [
        pl.BlockSpec((tile, width), held(2 * order_of(m), 2)) for m in range(4)
    ]
    cot_specs = [
        pl.BlockSpec(
            (tile, quarter),
            lambda i, index, j=j: (
                jnp.bitwise_xor(order_of(i // 2), j) * 2 + lax.rem(i, 2),
                0,
            ),
        )
        for j in range(4)
    ]
    weight_specs = [
        pl.BlockSpec((8, 1, n, hidden), lambda i, index, k=k: (0, k, 0, 0)) for k in range(2)
    ]
    each = lambda w: pl.BlockSpec((tile, w), lambda i, index: (i, 0))
    shape = jax.ShapeDtypeStruct
    return pl.pallas_call(
        mlp_body,
        out_shape=[
            shape((rows, hidden), BF16),
            shape((rows, hidden), BF16),
            shape((rows, width), BF16),
            shape((rows, width), BF16),
            *[shape((rows, quarter), BF16)] * 4,
            shape((rows // 2, width), F32),
            shape((rows // 2, width), BF16),
            shape((tokens, width), BF16),
        ],
        grid_spec=pltpu.PrefetchScalarGridSpec(
            num_scalar_prefetch=1,
            grid=(TURNS,),
            in_specs=norm_specs
            + cot_specs
            + weight_specs
            + [pl.BlockSpec((tile, width), held(0, 2))],
            out_specs=[each(hidden), each(hidden), each(width), each(width)]
            + [each(quarter)] * 4
            + [
                pl.BlockSpec((tile, width), held(0, 4)),
                pl.BlockSpec((tile, width), held(4, 4)),
                pl.BlockSpec((tile, width), held(0, 2)),
            ],
            scratch_shapes=[pltpu.VMEM((tile, width), F32)],
        ),
        compiler_params=pltpu.CompilerParams(vmem_limit_bytes=VMEM_ROOM),
        name="mlp",
        cost_estimate=cost(30),
    )(index, *norms, *cots, weights, weights, stream)


def mlp_grads_body(norm_ref, cot_ref, act_ref, grad_ref, out_ref):
    for k, (left, right) in enumerate(((norm_ref, grad_ref), (cot_ref, act_ref))):
        block = gram(left[...], right[...]).astype(BF16)
        n = out_ref.shape[2]
        for i in range(out_ref.shape[0]):
            out_ref[i, k] = block[i * n : (i + 1) * n]


def mlp_grads(norm, cot, act, grad):
    rows, width = norm.shape
    hidden = act.shape[1]
    n = width // 8
    whole = pl.BlockSpec((rows, hidden), lambda i: (0, 0))
    part = pl.BlockSpec((rows, 2 * n), lambda i: (0, i))
    return pl.pallas_call(
        mlp_grads_body,
        out_shape=pltpu.HBM((8, 2, n, hidden), BF16),
        grid=(4,),
        in_specs=[part, part, whole, whole],
        out_specs=pl.BlockSpec((2, 2, n, hidden), lambda i: (i, 0, 0, 0)),
        compiler_params=pltpu.CompilerParams(vmem_limit_bytes=VMEM_ROOM),
        name="mlp_grads",
        cost_estimate=cost(14),
    )(norm, cot, act, grad)


def join_rows(packed):
    pieces, _, n, w = packed.shape
    return (
        packed.reshape(8, pieces // 8, 2, n, w).swapaxes(1, 2).reshape(8, 2, n * pieces // 8, w)
    )


def split_rows(packed):
    _, _, n, w = packed.shape
    share = lax.axis_size("seq") // 8
    return (
        packed.reshape(8, 2, share, n // share, w).swapaxes(1, 2).reshape(8 * share, 2, n // share, w)
    )


def edges(cells):
    count = lax.axis_size("seq")
    head, tail = cells
    return (
        lax.ppermute(tail, "seq", [(i, i + 1) for i in range(count - 1)]),
        lax.ppermute(head, "seq", [(i + 1, i) for i in range(count - 1)]),
    )


def on_device(
    inputs,
    coarse_ids,
    segment_ids,
    cotangent,
    embed_table,
    conv_weight,
    res_weight,
    up_weight,
    gain_one,
    shift_one,
    qkv_weight,
    out_weight,
    gain_two,
    shift_two,
    in_weight,
    down_weight,
):
    c, x = place()
    micros, tokens, quarter = inputs.shape
    width = 4 * quarter
    coarse = coarse_ids.shape[1]
    step = CONV_DILATION
    slot = jnp.arange(8, dtype=jnp.int32)
    quarters = (((slot >> 1) ^ c) << 1) | (slot & 1)

    line = Line()
    stream_in = line.exchange(pick([inputs[i] for i in range(4)], c))
    attn_shard = jnp.concatenate([qkv_weight.reshape(-1, 3 * quarter), out_weight.T], axis=1)
    attn_shard = jnp.stack([attn_shard, *line.send((attn_shard, 2))])
    mlp_shard = jnp.stack([in_weight, down_weight.T])
    cots = line.spread(jnp.concatenate(pick([cotangent[i] for i in range(4)], c), axis=0))

    lot = gain_one.shape[0]
    vectors = vector_rows(jnp.stack([gain_one, shift_one, gain_two, shift_two]))
    conv_shard = conv_weight.transpose(2, 0, 1).reshape(-1, 3 * quarter)
    groups = ((embed_table, conv_shard, vectors), (res_weight, up_weight.T))
    if tuned():
        first, second = (bundle(group) for group in groups)
        first = along_z(jnp.broadcast_to(first, (4,) + first.shape))
        second = after(second, first, *stream_in, attn_shard)
        second = along_z(jnp.broadcast_to(second, (4,) + second.shape))
        first_far = hop(first, 1)
        second_far = hop(after(second, first_far), 1)
        table, conv, vectors = unpack(first, after(first_far, *cots), [w.shape for w in groups[0]])
        attn_shard = after(attn_shard, second, table)
        res, up = unpack(second, second_far, [w.shape for w in groups[1]])
    else:
        (table, conv, vectors), (res, up) = (gather_plain(group) for group in groups)
    attn_w = lax.all_gather(attn_shard, "seq", axis=0)
    mlp_w = lax.all_gather(after(mlp_shard, attn_w), "seq", axis=0)
    vectors = jnp.pad(join_vectors(line.spread(vectors), lot, c, x), ((0, 4), (0, 0)))

    ids = jnp.concatenate(pick([coarse_ids[i] for i in range(4)], c))
    vocab = table.shape[0]
    code = jnp.arange(vocab, dtype=jnp.int32)
    block = vocab // 8
    slot_of = code // block
    code = (((slot_of & 3) << 1) | ((slot_of >> 2) ^ x)) * block + code % block
    onehot = (ids[:, None] == code[None, :]).astype(BF16)
    embed = dot(onehot, table)
    act = gelu(embed).astype(BF16).reshape(micros, coarse, quarter)
    prior, later = edges((act[:, :step], act[:, coarse - step :]))
    padded = jnp.concatenate([prior, act, later], axis=1)
    taps = jnp.concatenate(
        [padded[:, k * step : k * step + coarse] for k in range(3)], axis=2
    ).reshape(micros * coarse, 3 * quarter)
    conv_terms = dot_t(taps, conv).reshape(micros, coarse, width)
    conv_out = fold(line, [conv_terms[j] for j in range(4)])
    mixed = after(gelu(conv_out).astype(BF16), res, up)
    mixed_all = jnp.concatenate(line.spread(mixed), axis=0)
    hidden = (embed + dot(mixed_all, res)).astype(BF16)
    up_terms = dot_t(hidden, up).reshape(micros, coarse, 4 * width)
    up_terms = fold(line, [up_terms[j] for j in range(4)])
    i = jnp.arange(32, dtype=jnp.int32)
    from_up = (((i >> 2) & 1) ^ x) * 16 + (i >> 3) * 4 + (i & 3)
    to_up = ((i >> 2) & 3) * 8 + ((i >> 4) ^ x) * 4 + (i & 3)
    stream_zero = enter(up_terms, stream_in, from_up, quarters)
    segments = lax.dynamic_index_in_dim(segment_ids, c, 0, keepdims=False)
    attn_w = join_rows(attn_w)
    attn_w = (attn_w, swap(attn_w, 1))
    norm_one, stream_one, norm_two, qkv, context = layer_forward(
        segments, stream_zero, vectors, attn_w
    )

    norm_all = line.spread(norm_two)
    mlp_act, grad_pre, norm_rows, cot_rows, *outs, keep, send, cot_mine = mlp(
        norm_all, cots, join_rows(mlp_w), stream_one, jnp.arange(4, dtype=jnp.int32) ^ c
    )
    from_core = swap(send, 1)
    over_y = (keep[tokens:] + from_core[tokens:].astype(F32)).astype(BF16)
    (from_y,) = line.send((over_y, 2))
    grad_mlp = mlp_grads(after(norm_rows, over_y), cot_rows, mlp_act, grad_pre)
    turned = lambda v, j: jnp.stack([v[m ^ order_of(j)] for m in range(4)])
    result, over_y = fold_core(
        [d.reshape(micros, tokens, quarter) for d in outs], fix=turned
    )
    terms = lax.optimization_barrier((keep, from_core, from_y, grad_mlp, over_y))
    grads, over_y = terms[:3], terms[4]
    (from_y,) = line.send((over_y, 2))
    result = (result + turned(from_y, 2).astype(F32)).astype(BF16)
    act_done = from_y
    result = jnp.stack(pick([result[order_of(m)] for m in range(4)], c))
    grad_mlp = lax.psum_scatter(split_rows(terms[3]), "seq", scatter_dimension=0, tiled=False)
    grad_in, grad_down = grad_mlp[0].astype(F32), grad_mlp[1].astype(F32).T

    att, input_grad, grad_vectors, *grad_rows = layer_backward(
        segments, [stream_zero, stream_one], vectors, grads, cot_mine, attn_w, qkv
    )
    grad_vectors = split_vectors(grad_vectors[:4], lot, c, x)
    leave_rows, *grad_in_q = leave(input_grad, to_up, quarters)
    grad_rows[0] = after(grad_rows[0], leave_rows, act_done)
    grad_attn, send = layer_grads(norm_one, att, grad_rows, context)
    leave_rows, from_y, send = lax.optimization_barrier(
        (leave_rows, *line.send((leave_rows, 2)), send)
    )
    grad_up_rows = [leave_rows, swap(leave_rows, 1), from_y, swap(from_y, 1)]
    grad_attn = grad_attn.astype(F32) + swap(send, 1).astype(F32)
    grad_attn = split_rows(grad_attn.astype(BF16))
    grad_attn = after(grad_attn, grad_up_rows[2])
    grad_attn = lax.psum_scatter(grad_attn, "seq", scatter_dimension=0, tiled=False)
    grad_up_rows = jnp.concatenate(grad_up_rows, axis=0)
    grad_hidden = dot(grad_up_rows, up)
    grad_low = grad_hidden.astype(BF16)
    grad_up = gram(grad_up_rows, hidden).astype(BF16)
    grad_res = gram(mixed_all, grad_low).astype(BF16)
    up_started = cross_x([grad_res, grad_up])
    grad_mixed = dot_t(after(grad_low, grad_up, grad_res), res).reshape(micros, coarse, width)
    grad_mixed, over_y = fold_core([grad_mixed[j] for j in range(4)])
    grad_mixed = grad_mixed + line.send((over_y, 2))[0].astype(F32)
    grad_conv_low = after((gelu_grad(conv_out) * grad_mixed).astype(BF16), grad_mlp, up_started[1])

    grad_conv_all = jnp.concatenate(line.spread(grad_conv_low), axis=0)
    grad_taps = dot(grad_conv_all, conv).reshape(micros, coarse, 3 * quarter)
    tap = [grad_taps[:, :, k * quarter : (k + 1) * quarter] for k in range(3)]
    rims = tap[0][:, :step].astype(BF16), tap[2][:, coarse - step :].astype(BF16)
    prior, later = edges(rims)
    grad_conv = gram(grad_conv_all, taps).astype(BF16)
    grad_vectors = fold(line, grad_vectors)
    grad_act = (
        tap[1]
        + jnp.concatenate([tap[0][:, step:], later.astype(F32)], axis=1)
        + jnp.concatenate([prior.astype(F32), tap[2][:, : coarse - step]], axis=1)
    ).reshape(micros * coarse, quarter)
    grad_embed = (grad_hidden + gelu_grad(embed) * grad_act).astype(BF16)
    started = cross_x([gram(onehot, grad_embed), grad_conv, grad_vectors])
    up_started = after(up_started, started[0])
    grad_res, grad_up = cross_z(up_started, [w.shape for w in groups[1]])
    grad_table, grad_conv, grad_vectors = cross_z(started, [w.shape for w in groups[0]])
    grad_conv = grad_conv.reshape(-1, 3, quarter).transpose(1, 2, 0)
    input_grads = jnp.stack(pick(line.exchange(grad_in_q), c))
    grad_attn = grad_attn[0].astype(F32) + line.send((grad_attn[1], 2))[0].astype(F32)
    grad_qkv, grad_out = grad_attn[:, : 3 * quarter], grad_attn[:, 3 * quarter :]
    grad_vectors = [grad_vectors[i, :lot] for i in range(4)]
    return (
        result,
        input_grads,
        grad_table,
        grad_conv,
        grad_res,
        grad_up.T,
        grad_vectors[0],
        grad_vectors[1],
        grad_qkv.reshape(qkv_weight.shape),
        grad_out.T,
        grad_vectors[2],
        grad_vectors[3],
        grad_in,
        grad_down,
    )


def solution(mesh):
    wide = P(("cond", "seq"))
    acts = P(None, "seq", "cond")
    weights = (
        P("seq", "cond"),
        P(None, "cond", "seq"),
        P("seq", "cond"),
        P("cond", "seq"),
        wide,
        wide,
        P("seq", None, "cond"),
        P("cond", "seq"),
        wide,
        wide,
        P("seq", "cond"),
        P("cond", "seq"),
    )
    return jax.shard_map(
        on_device,
        mesh=mesh,
        in_specs=(acts, P(None, "seq"), P(None, "seq"), acts) + weights,
        out_specs=(acts, acts) + weights,
        check_vma=False,
    )
```

```python
import math

import jax
import jax.numpy as jnp
from jax import lax
from jax.experimental import pallas as pl
from jax.experimental.pallas import tpu as pltpu
from jax.sharding import PartitionSpec as P

HEAD = 64
ROW = 64
CONV_DILATION = 27
EPSILON = 1e-05
NEG_FILL = -1e30
LANES = 128
BF16 = jnp.bfloat16
F32 = jnp.float32


def tuned():
    return lax.axis_size("seq") == 8


def swap(x, j):
    return lax.ppermute(x, "cond", [(i, i ^ j) for i in range(4)])


def hop(x, k):
    return lax.ppermute(x, "seq", [(i, i ^ k) for i in range(8)])


def place():
    c = lax.axis_index("cond")
    return c, (lax.axis_index("seq") & 1 if tuned() else jnp.zeros((), jnp.int32))


def after(value, *before):
    return lax.optimization_barrier((value, *before))[0]


def dot(a, b, dims=((1,), (0,))):
    return lax.dot_general(a, b, (dims, ((), ())), preferred_element_type=F32)


def gram(a, b):
    return dot(a, b, ((0,), (0,)))


def dot_t(a, b):
    return dot(a, b, ((1,), (1,)))


def gelu(v):
    return 0.5 * v * (1.0 + lax.erf(v * math.sqrt(0.5)))


def gelu_grad(v):
    return 0.5 * (1.0 + lax.erf(v * math.sqrt(0.5))) + v * (
        math.sqrt(0.5 / math.pi) * jnp.exp(-0.5 * v * v)
    )


def pick(items, t):
    low, high = (t & 1) == 1, (t & 2) == 2
    items = [jnp.where(low, items[i ^ 1], items[i]) for i in range(4)]
    return [jnp.where(high, items[i ^ 2], items[i]) for i in range(4)]


def regroup(x, dim, outer, inner):
    n = x.shape[dim] // 8
    shape = x.shape
    x = x.reshape(shape[:dim] + (outer, inner, n) + shape[dim + 1 :])
    return jnp.swapaxes(x, dim, dim + 1).reshape(shape)


def cost(us):
    return pl.CostEstimate(flops=int(us * 1.76e9), transcendentals=0, bytes_accessed=0)


CELL = 256
ALONG_Z = [[0, 2, 4, 6], [1, 3, 5, 7]]
VMEM_ROOM = 48 * 1024 * 1024


def bundle(shards):
    return jnp.concatenate(
        [s[:, i : i + CELL] for s in shards for i in range(0, s.shape[1], CELL)], axis=0
    )


def along_z(x):
    return lax.all_to_all(x, "seq", 0, 0, axis_index_groups=ALONG_Z, tiled=True)


def unpack_body(shapes, near_ref, far_ref, *outs):
    p = pl.program_id(0)

    def copy(ref):
        at = 0
        for (r, w), out in zip(shapes, outs):
            for i in range(0, w, CELL):
                out[:, i : i + CELL] = ref[0, at : at + r]
                at += r

    pl.when(p < 4)(lambda: copy(near_ref))
    pl.when(p >= 4)(lambda: copy(far_ref))


def unpack(near, far, shapes):
    block = (1,) + near.shape[1:]
    return pl.pallas_call(
        lambda *refs: unpack_body(shapes, *refs),
        out_shape=[jax.ShapeDtypeStruct((8 * r, w), near.dtype) for r, w in shapes],
        grid=(8,),
        in_specs=[
            pl.BlockSpec(block, lambda p: (jnp.minimum(p, 3), 0, 0)),
            pl.BlockSpec(block, lambda p: (jnp.maximum(p - 4, 0), 0, 0)),
        ],
        out_specs=[pl.BlockSpec((r, w), lambda p: (p, 0)) for r, w in shapes],
        compiler_params=pltpu.CompilerParams(vmem_limit_bytes=VMEM_ROOM),
        name="unpack",
        cost_estimate=cost(3),
    )(near, far)


def gather_plain(shards):
    return [regroup(lax.all_gather(s, "seq", axis=0, tiled=True), 0, 4, 2) for s in shards]


def pack_body(count, *refs):
    half, at = pl.program_id(0), 0
    for ref in refs[:count]:
        r, w = ref.shape
        for i in range(0, w, CELL):
            for k, out in enumerate(refs[count:]):

                @pl.when(half == k)
                def _(out=out, ref=ref, at=at, r=r, i=i):
                    out[0, at : at + r] = ref[:, i : i + CELL]

            at += r


def pack(grads):
    shapes = [(g.shape[0] // 8, g.shape[1]) for g in grads]
    rows = sum(r * w for r, w in shapes) // CELL
    shape = jax.ShapeDtypeStruct((4, rows, CELL), BF16)
    return pl.pallas_call(
        lambda *refs: pack_body(len(grads), *refs),
        out_shape=(shape, shape),
        grid=(2, 4),
        in_specs=[pl.BlockSpec((r, w), lambda h, p: (4 * h + p, 0)) for r, w in shapes],
        out_specs=(
            pl.BlockSpec((1, rows, CELL), lambda h, p: (jnp.where(h == 0, p, 3), 0, 0)),
            pl.BlockSpec((1, rows, CELL), lambda h, p: (jnp.where(h == 1, p, 0), 0, 0)),
        ),
        compiler_params=pltpu.CompilerParams(vmem_limit_bytes=VMEM_ROOM),
        name="pack",
        cost_estimate=cost(2),
    )(*grads)


def total_body(shapes, in_ref, *outs):
    at = 0
    for (r, w), out in zip(shapes, outs):
        for i in range(0, w, CELL):
            cells = [in_ref[k, at : at + r].astype(F32) for k in range(4)]
            out[:, i : i + CELL] = (cells[0] + cells[1]) + (cells[2] + cells[3])
            at += r


def total(parts, shapes):
    return pl.pallas_call(
        lambda *refs: total_body(shapes, *refs),
        out_shape=[jax.ShapeDtypeStruct(shape, F32) for shape in shapes],
        compiler_params=pltpu.CompilerParams(vmem_limit_bytes=VMEM_ROOM),
        name="total",
        cost_estimate=cost(1),
    )(parts)


def cross_x(grads):
    grads = [g.astype(BF16) for g in grads]
    if tuned():
        near, far = pack(grads)
        return near, hop(far, 1)
    return grads


def cross_z(started, shapes):
    if tuned():
        near, far = started
        return total(along_z((near.astype(F32) + far.astype(F32)).astype(BF16)), shapes)
    return [
        lax.psum_scatter(
            regroup(g, 0, 2, 4), "seq", scatter_dimension=0, tiled=True
        ).astype(F32)
        for g in started
    ]


class Line:
    def __init__(self):
        self.last = ()

    def send(self, *items):
        items = [(after(x, *self.last) if self.last else x, j) for x, j in items]
        self.last = [swap(x, j) for x, j in items]
        return self.last

    def spread(self, x):
        (y,) = self.send((x, 2))
        return [x, swap(x, 1), y, swap(y, 1)]

    def exchange(self, items):
        two, three = self.send((items[2], 2), (items[3], 3))
        return [items[0], swap(items[1], 1), two, three]


def same(x, j):
    return x


def fold_core(items, wire=BF16, fix=same):
    one = fix(swap(items[1].astype(wire), 1), 1).astype(F32)
    three = fix(swap(items[3].astype(wire), 1), 1).astype(F32)
    return items[0].astype(F32) + one, (items[2].astype(F32) + three).astype(wire)


def fold(line, items, wire=BF16, fix=same):
    zero, two = fold_core(items, wire, fix)
    return zero + fix(line.send((two, 2))[0], 2).astype(F32)


def lane_block(i):
    return pl.ds(pl.multiple_of(i * LANES, LANES), LANES)


def enter_body(from_up, to_layer, up_ref, q0, q1, q2, q3, out_ref, held, spaced):
    coarse = up_ref.shape[0]
    quarter = q0.shape[1]
    for j, ref in enumerate((q0, q1, q2, q3)):
        held[:, j * quarter : (j + 1) * quarter] = ref[...]
    for r in range(4):
        for p in range(8):
            spaced[p, pl.ds(r, coarse, stride=4), :] = up_ref[:, lane_block(from_up[r * 8 + p])]
    for p in range(8):
        out_ref[:, p * LANES : (p + 1) * LANES] = spaced[p] + held[
            :, lane_block(to_layer[p])
        ].astype(F32)


def enter(up_terms, quarters, from_up, to_layer):
    coarse, wide = up_terms.shape
    whole = lambda shape: pl.BlockSpec(shape, lambda i, a, b: (0, 0))
    tokens, quarter = quarters[0].shape
    return pl.pallas_call(
        enter_body,
        out_shape=jax.ShapeDtypeStruct((tokens, wide // 4), F32),
        grid_spec=pltpu.PrefetchScalarGridSpec(
            num_scalar_prefetch=2,
            grid=(1,),
            in_specs=[whole((coarse, wide))] + [whole((tokens, quarter))] * 4,
            out_specs=whole((tokens, wide // 4)),
            scratch_shapes=[
                pltpu.VMEM((tokens, wide // 4), BF16),
                pltpu.VMEM((8, tokens, LANES), F32),
            ],
        ),
        compiler_params=pltpu.CompilerParams(vmem_limit_bytes=VMEM_ROOM),
        name="enter",
        cost_estimate=cost(2),
    )(from_up, to_layer, up_terms, *quarters)


def leave_body(to_up, to_quarters, in_ref, rows_ref, q0, q1, q2, q3, spaced):
    coarse = rows_ref.shape[0]
    for p in range(8):
        spaced[p] = in_ref[:, p * LANES : (p + 1) * LANES]
    for i in range(32):
        source = to_up[i]
        rows_ref[:, i * LANES : (i + 1) * LANES] = spaced[
            source & 7, pl.ds(source >> 3, coarse, stride=4), :
        ].astype(BF16)
    for j, ref in enumerate((q0, q1, q2, q3)):
        for half in range(2):
            ref[:, half * LANES : (half + 1) * LANES] = in_ref[
                :, lane_block(to_quarters[2 * j + half])
            ].astype(BF16)


def leave(grad, to_up, to_quarters):
    tokens, width = grad.shape
    whole = lambda shape: pl.BlockSpec(shape, lambda i, a, b: (0, 0))
    shapes = [(tokens // 4, 4 * width)] + [(tokens, width // 4)] * 4
    return pl.pallas_call(
        leave_body,
        out_shape=[jax.ShapeDtypeStruct(shape, BF16) for shape in shapes],
        grid_spec=pltpu.PrefetchScalarGridSpec(
            num_scalar_prefetch=2,
            grid=(1,),
            in_specs=[whole((tokens, width))],
            out_specs=[whole(shape) for shape in shapes],
            scratch_shapes=[pltpu.VMEM((8, tokens, LANES), F32)],
        ),
        compiler_params=pltpu.CompilerParams(vmem_limit_bytes=VMEM_ROOM),
        name="leave",
        cost_estimate=cost(2),
    )(to_up, to_quarters, grad)


TILE = 128
SCALE = 1.0 / math.sqrt(HEAD)


def by_head(x):
    heads = x.shape[1] // HEAD
    feature = lax.broadcasted_iota(jnp.int32, x.shape, 1) // HEAD
    return jnp.concatenate(
        [jnp.where(feature == h, x, jnp.zeros_like(x)) for h in range(heads)], axis=0
    )


def of_heads(x):
    heads = x.shape[1] // HEAD
    feature = lax.broadcasted_iota(jnp.int32, (TILE, x.shape[1]), 1) // HEAD
    out = x[:TILE]
    for h in range(1, heads):
        out = jnp.where(feature == h, x[h * TILE : (h + 1) * TILE], out)
    return out


def visible(column, row):
    i = lax.broadcasted_iota(jnp.int32, (TILE, TILE), 0)
    j = lax.broadcasted_iota(jnp.int32, (TILE, TILE), 1)
    return (column == row) & (i >= j) & (i // ROW == j // ROW)


def soft(query, keys, allowed):
    scores = dot_t(query, keys) * SCALE
    probs = []
    for h in range(scores.shape[1] // TILE):
        part = jnp.where(allowed, scores[:, h * TILE : (h + 1) * TILE], NEG_FILL)
        exps = jnp.exp(part - jnp.max(part, axis=1, keepdims=True))
        probs.append(exps * (1.0 / jnp.sum(exps, axis=1, keepdims=True)))
    return probs


def attend_tile(qkv, allowed):
    n = qkv.shape[1] // 3
    probs = soft(qkv[:, :n], by_head(qkv[:, n : 2 * n]), allowed)
    low = jnp.concatenate([p.astype(BF16) for p in probs], axis=1)
    return dot(low, by_head(qkv[:, 2 * n :])).astype(BF16)


def attend_back_tile(qkv, grad, allowed):
    n = grad.shape[1]
    query = qkv[:, :n]
    keys = by_head(qkv[:, n : 2 * n])
    probs = soft(query, keys, allowed)
    grad_probs = dot_t(grad, by_head(qkv[:, 2 * n :]))
    grads = []
    for h, p in enumerate(probs):
        part = grad_probs[:, h * TILE : (h + 1) * TILE]
        inner = jnp.sum(p * part, axis=1, keepdims=True)
        grads.append((p * (part - inner)).astype(BF16))
    grads = jnp.concatenate(grads, axis=1)
    low = jnp.concatenate([p.astype(BF16) for p in probs], axis=1)
    return jnp.concatenate(
        [
            (dot(grads, keys) * SCALE).astype(BF16),
            (of_heads(gram(grads, query)) * SCALE).astype(BF16),
            of_heads(gram(low, grad)).astype(BF16),
        ],
        axis=1,
    )


def standard(stream):
    mean = jnp.mean(stream, axis=1, keepdims=True)
    centred = stream - mean
    rstd = lax.rsqrt(jnp.mean(centred * centred, axis=1, keepdims=True) + EPSILON)
    return centred * rstd, rstd


def standard_back(normed, rstd, gain, grad):
    scaled = grad * gain
    return rstd * (
        scaled
        - jnp.mean(scaled, axis=1, keepdims=True)
        - normed * jnp.mean(scaled * normed, axis=1, keepdims=True)
    )


ANYWHERE = jax.ShapeDtypeStruct
LAYER_TILE = 256
SUBS = LAYER_TILE // TILE


def joined(ref, start, stop):
    return ref[:, :, :, start:stop].reshape(-1, stop - start)


def masks(column_ref, row_ref):
    return [
        visible(column_ref[i * TILE : (i + 1) * TILE], row_ref[i]) for i in range(SUBS)
    ]


def forward_body(*refs):
    column_ref, row_ref, stream_ref, vec_ref = refs[:4]
    weights = refs[4:8]
    norm_ref, out_ref, norm_two_ref = refs[8:11]
    qkvs, contexts = refs[11:15], refs[15:19]
    allowed = masks(column_ref, row_ref)
    stream = stream_ref[...]
    normed, _ = standard(stream)
    norm_ref[...] = (normed * vec_ref[0:1] + vec_ref[1:2]).astype(BF16)
    for weight, qkv_ref, context_ref in zip(weights, qkvs, contexts):
        n = context_ref.shape[1]
        qkv_ref[...] = dot(norm_ref[...], joined(weight, 0, 3 * n)).astype(BF16)
        for i in range(SUBS):
            at = slice(i * TILE, (i + 1) * TILE)
            context_ref[at] = attend_tile(qkv_ref[at], allowed[i])
        stream = stream + dot_t(context_ref[...], joined(weight, 3 * n, 4 * n))
    out_ref[...] = stream
    normed, _ = standard(stream)
    norm_two_ref[...] = (normed * vec_ref[2:3] + vec_ref[3:4]).astype(BF16)


def backward_body(*refs):
    column_ref, row_ref, zero_ref, one_ref, vec_ref, keep_ref, core_ref, y_ref, cot_ref = refs[:9]
    weights, qkvs = refs[9:13], refs[13:17]
    att_ref, input_ref, vec_grad_ref = refs[17:20]
    rows = refs[20:24]
    allowed = masks(column_ref, row_ref)
    grad = keep_ref[...] + core_ref[...].astype(F32) + y_ref[...].astype(F32)
    normed, rstd = standard(one_ref[...])
    sums = [jnp.sum(grad * normed, axis=0, keepdims=True), jnp.sum(grad, axis=0, keepdims=True)]
    stream = cot_ref[...].astype(F32) + standard_back(normed, rstd, vec_ref[2:3], grad)
    att_ref[...] = stream.astype(BF16)
    grad = None
    for weight, qkv_ref, row_grad_ref in zip(weights, qkvs, rows):
        n = qkv_ref.shape[1] // 3
        context = dot(att_ref[...], joined(weight, 3 * n, 4 * n)).astype(BF16)
        for i in range(SUBS):
            at = slice(i * TILE, (i + 1) * TILE)
            row_grad_ref[at] = attend_back_tile(qkv_ref[at], context[at], allowed[i])
        part = dot_t(row_grad_ref[...], joined(weight, 0, 3 * n))
        grad = part if grad is None else grad + part
    normed, rstd = standard(zero_ref[...])
    sums = [
        jnp.sum(grad * normed, axis=0, keepdims=True),
        jnp.sum(grad, axis=0, keepdims=True),
    ] + sums
    input_ref[...] = stream + standard_back(normed, rstd, vec_ref[0:1], grad)

    @pl.when(pl.program_id(0) == 0)
    def _():
        vec_grad_ref[...] = jnp.zeros_like(vec_grad_ref)

    for i, v in enumerate(sums):
        vec_grad_ref[i : i + 1] += v


def layer_call(body, segments, arrays, fixed, weights, more, outs, name, us):
    tokens = segments.shape[0]
    wide = lambda w: pl.BlockSpec((LAYER_TILE, w), lambda i: (i, 0))
    still = lambda shape: pl.BlockSpec(shape, lambda i: (0,) * len(shape))
    _, _, n, w = weights[0].shape
    tiles = tokens // TILE
    return pl.pallas_call(
        body,
        out_shape=[space(shape, dtype) for space, shape, dtype in outs],
        grid=(tokens // LAYER_TILE,),
        in_specs=[wide(1), pl.BlockSpec((SUBS, 1, TILE), lambda i: (i, 0, 0))]
        + [wide(a.shape[1]) for a in arrays]
        + [still(fixed.shape)]
        + [wide(a.shape[1]) for a in more[0]]
        + [pl.BlockSpec((8, 1, n, w), lambda i, k=k: (0, k, 0, 0)) for k in (0, 0, 1, 1)]
        + [wide(a.shape[1]) for a in more[1]],
        out_specs=[
            wide(shape[1]) if shape[0] == tokens else still(shape) for _, shape, _ in outs
        ],
        compiler_params=pltpu.CompilerParams(vmem_limit_bytes=VMEM_ROOM),
        name=name,
        cost_estimate=cost(us),
    )(
        segments.reshape(tokens, 1),
        segments.reshape(tiles, 1, TILE),
        *arrays,
        fixed,
        *more[0],
        weights[0],
        weights[1],
        weights[0],
        weights[1],
        *more[1],
    )


def layer_forward(segments, stream, vectors, weights):
    tokens, width = stream.shape
    quarter = width // 4
    outs = (
        [
            (pltpu.HBM, (tokens, width), BF16),
            (ANYWHERE, (tokens, width), F32),
            (ANYWHERE, (tokens, width), BF16),
        ]
        + [(pltpu.HBM, (tokens, 3 * quarter), BF16)] * 4
        + [(pltpu.HBM, (tokens, quarter), BF16)] * 4
    )
    norm_one, stream_one, norm_two, *rest = layer_call(
        forward_body, segments, [stream], vectors, weights, ([], []), outs, "layer_forward", 18
    )
    return norm_one, stream_one, norm_two, rest[:4], rest[4:]


def layer_backward(segments, streams, vectors, grads, cot, weights, qkv):
    tokens, width = cot.shape
    outs = [
        (ANYWHERE, (tokens, width), BF16),
        (ANYWHERE, (tokens, width), F32),
        (ANYWHERE, vectors.shape, F32),
    ]
    outs += [(ANYWHERE, q.shape, BF16) for q in qkv]
    return layer_call(
        backward_body, segments, streams, vectors, weights, ([*grads, cot], qkv), outs,
        "layer_backward",
        24,
    )


def layer_grads_body(norm_ref, att_ref, *refs):
    rows, contexts, outs = refs[:4], refs[4:8], refs[8:]
    blocks, _, n, _ = outs[0].shape
    for j in range(4):
        out, k = outs[j & 1], j >> 1
        w = rows[j].shape[1]
        left = gram(norm_ref[...], rows[j][...]).astype(BF16)
        right = gram(att_ref[...], contexts[j][...]).astype(BF16)
        for i in range(blocks):
            out[i, k, :, :w] = left[i * n : (i + 1) * n]
            out[i, k, :, w:] = right[i * n : (i + 1) * n]


def layer_grads(norm, att, rows, contexts):
    tokens, width = norm.shape
    n = width // 8
    part = pl.BlockSpec((tokens, 2 * n), lambda i: (0, i))
    whole = lambda a: pl.BlockSpec(a.shape, lambda i: (0, 0))
    shape = jax.ShapeDtypeStruct((8, 2, n, width), BF16)
    out = pl.BlockSpec((2, 2, n, width), lambda i: (i, 0, 0, 0))
    return pl.pallas_call(
        layer_grads_body,
        out_shape=(shape, shape),
        grid=(4,),
        in_specs=[part, part] + [whole(a) for a in (*rows, *contexts)],
        out_specs=(out, out),
        compiler_params=pltpu.CompilerParams(vmem_limit_bytes=VMEM_ROOM),
        name="layer_grads",
        cost_estimate=cost(8),
    )(norm, att, *rows, *contexts)


def vector_owner(c, x):
    i = jnp.arange(32)
    source = i & 7
    piece = ((i >> 3) ^ c) * 8 + ((((source & 1) ^ x) << 2) | (source >> 1))
    return piece[:, None] == jnp.arange(32)[None, :]


PAD = 16


def vector_rows(vectors):
    ends = [(0, 0)] * (vectors.ndim - 2)
    count, n = vectors.shape[-2:]
    return jnp.pad(vectors, ends + [(0, PAD - count), (0, CELL - n)])


def join_vectors(spreads, n, c, x):
    pieces = jnp.stack([s.reshape(8, -1, PAD, CELL)[:, :, :4, :n] for s in spreads])
    pieces = pieces.transpose(3, 0, 1, 2, 4).reshape(4, 32, -1)
    owner = vector_owner(c, x).astype(BF16)
    full = jnp.einsum("dp,vpn->vdn", owner, pieces, preferred_element_type=F32)
    return full.reshape(4, -1)


def split_vectors(full, n, c, x):
    owner = vector_owner(c, x).astype(F32)
    pieces = jnp.einsum(
        "dp,vdn->pvn",
        owner,
        full.reshape(4, 32, -1),
        precision=lax.Precision.HIGHEST,
        preferred_element_type=F32,
    )
    pieces = pieces.reshape(4, 8, 4, -1, n).swapaxes(2, 3)
    rows = vector_rows(pieces)
    return [rows[j].reshape(-1, CELL) for j in range(4)]


MLP_TILE = 256
TURNS = 8


def order_of(k):
    return ((k & 1) << 1) | (k >> 1)


def mlp_body(index, *refs):
    (n0, n1, n2, n3, q0, q1, q2, q3, in_ref, down_ref, stream_ref) = refs[:11]
    (act_ref, grad_ref, norm_ref, cot_ref, d0, d1, d2, d3, keep_ref, send_ref, mine_ref) = refs[11:22]
    (wide,) = refs[22:]
    tile = pl.program_id(0)
    k = tile // 2
    for at, ref in enumerate((n0, n2, n1, n3)):

        @pl.when(k == at)
        def _(ref=ref):
            norm_ref[...] = ref[...]

    quarters = [pl.ds(pl.multiple_of(index[j] * 256, 256), 256) for j in range(4)]
    for j, ref in enumerate((q0, q1, q2, q3)):
        cot_ref[:, quarters[j]] = ref[...]
    weight_in = in_ref[...].reshape(-1, in_ref.shape[-1])
    weight_down = down_ref[...].reshape(-1, down_ref.shape[-1])
    pre = dot(norm_ref[...], weight_in)
    half = 0.5 + 0.5 * lax.erf(pre * math.sqrt(0.5))
    act = (pre * half).astype(BF16)
    act_ref[...] = act
    slope = half + pre * (math.sqrt(0.5 / math.pi) * jnp.exp(-0.5 * pre * pre))
    grad = (slope * dot(cot_ref[...], weight_down)).astype(BF16)
    grad_ref[...] = grad
    wide[...] = dot_t(act, weight_down)

    @pl.when(tile < 2)
    def _():
        wide[...] = wide[...] + stream_ref[...]
        mine_ref[...] = cot_ref[...]

    for j, ref in enumerate((d0, d1, d2, d3)):
        ref[...] = wide[:, quarters[j]].astype(BF16)
    other = dot_t(grad, weight_in)

    @pl.when(tile < 4)
    def _():
        keep_ref[...] = other

    @pl.when(tile >= 4)
    def _():
        send_ref[...] = other.astype(BF16)


def mlp(norms, cots, weights, stream, index):
    tokens, width = norms[0].shape
    rows, quarter = cots[0].shape
    hidden = weights.shape[-1]
    n = weights.shape[2]
    tile = MLP_TILE
    per = tokens // tile
    assert per == 2
    held = lambda start, count: lambda i, index: (jnp.clip(i - start, 0, count - 1), 0)
    norm_specs = [
        pl.BlockSpec((tile, width), held(2 * order_of(m), 2)) for m in range(4)
    ]
    cot_specs = [
        pl.BlockSpec(
            (tile, quarter),
            lambda i, index, j=j: (
                jnp.bitwise_xor(order_of(i // 2), j) * 2 + lax.rem(i, 2),
                0,
            ),
        )
        for j in range(4)
    ]
    weight_specs = [
        pl.BlockSpec((8, 1, n, hidden), lambda i, index, k=k: (0, k, 0, 0)) for k in range(2)
    ]
    each = lambda w: pl.BlockSpec((tile, w), lambda i, index: (i, 0))
    shape = jax.ShapeDtypeStruct
    return pl.pallas_call(
        mlp_body,
        out_shape=[
            shape((rows, hidden), BF16),
            shape((rows, hidden), BF16),
            shape((rows, width), BF16),
            shape((rows, width), BF16),
            *[shape((rows, quarter), BF16)] * 4,
            shape((rows // 2, width), F32),
            shape((rows // 2, width), BF16),
            shape((tokens, width), BF16),
        ],
        grid_spec=pltpu.PrefetchScalarGridSpec(
            num_scalar_prefetch=1,
            grid=(TURNS,),
            in_specs=norm_specs
            + cot_specs
            + weight_specs
            + [pl.BlockSpec((tile, width), held(0, 2))],
            out_specs=[each(hidden), each(hidden), each(width), each(width)]
            + [each(quarter)] * 4
            + [
                pl.BlockSpec((tile, width), held(0, 4)),
                pl.BlockSpec((tile, width), held(4, 4)),
                pl.BlockSpec((tile, width), held(0, 2)),
            ],
            scratch_shapes=[pltpu.VMEM((tile, width), F32)],
        ),
        compiler_params=pltpu.CompilerParams(vmem_limit_bytes=VMEM_ROOM),
        name="mlp",
        cost_estimate=cost(30),
    )(index, *norms, *cots, weights, weights, stream)


def mlp_grads_body(norm_ref, cot_ref, act_ref, grad_ref, out_ref):
    for k, (left, right) in enumerate(((norm_ref, grad_ref), (cot_ref, act_ref))):
        block = gram(left[...], right[...]).astype(BF16)
        n = out_ref.shape[2]
        for i in range(out_ref.shape[0]):
            out_ref[i, k] = block[i * n : (i + 1) * n]


def mlp_grads(norm, cot, act, grad):
    rows, width = norm.shape
    hidden = act.shape[1]
    n = width // 8
    whole = pl.BlockSpec((rows, hidden), lambda i: (0, 0))
    part = pl.BlockSpec((rows, 2 * n), lambda i: (0, i))
    return pl.pallas_call(
        mlp_grads_body,
        out_shape=pltpu.HBM((8, 2, n, hidden), BF16),
        grid=(4,),
        in_specs=[part, part, whole, whole],
        out_specs=pl.BlockSpec((2, 2, n, hidden), lambda i: (i, 0, 0, 0)),
        compiler_params=pltpu.CompilerParams(vmem_limit_bytes=VMEM_ROOM),
        name="mlp_grads",
        cost_estimate=cost(14),
    )(norm, cot, act, grad)


def join_rows(packed):
    pieces, _, n, w = packed.shape
    return (
        packed.reshape(8, pieces // 8, 2, n, w).swapaxes(1, 2).reshape(8, 2, n * pieces // 8, w)
    )


def split_rows(packed):
    _, _, n, w = packed.shape
    share = lax.axis_size("seq") // 8
    return (
        packed.reshape(8, 2, share, n // share, w).swapaxes(1, 2).reshape(8 * share, 2, n // share, w)
    )


def edges(cells):
    count = lax.axis_size("seq")
    head, tail = cells
    return (
        lax.ppermute(tail, "seq", [(i, i + 1) for i in range(count - 1)]),
        lax.ppermute(head, "seq", [(i + 1, i) for i in range(count - 1)]),
    )


def on_device(
    inputs,
    coarse_ids,
    segment_ids,
    cotangent,
    embed_table,
    conv_weight,
    res_weight,
    up_weight,
    gain_one,
    shift_one,
    qkv_weight,
    out_weight,
    gain_two,
    shift_two,
    in_weight,
    down_weight,
):
    c, x = place()
    micros, tokens, quarter = inputs.shape
    width = 4 * quarter
    coarse = coarse_ids.shape[1]
    step = CONV_DILATION
    slot = jnp.arange(8, dtype=jnp.int32)
    quarters = (((slot >> 1) ^ c) << 1) | (slot & 1)

    line = Line()
    stream_in = line.exchange(pick([inputs[i] for i in range(4)], c))
    attn_shard = jnp.concatenate([qkv_weight.reshape(-1, 3 * quarter), out_weight.T], axis=1)
    attn_shard = jnp.stack([attn_shard, *line.send((attn_shard, 2))])
    mlp_shard = jnp.stack([in_weight, down_weight.T])
    cots = line.spread(jnp.concatenate(pick([cotangent[i] for i in range(4)], c), axis=0))

    lot = gain_one.shape[0]
    vectors = vector_rows(jnp.stack([gain_one, shift_one, gain_two, shift_two]))
    conv_shard = conv_weight.transpose(2, 0, 1).reshape(-1, 3 * quarter)
    groups = ((embed_table, conv_shard, vectors), (res_weight, up_weight.T))
    if tuned():
        first, second = (bundle(group) for group in groups)
        first = along_z(jnp.broadcast_to(first, (4,) + first.shape))
        second = after(second, first, *stream_in, attn_shard)
        second = along_z(jnp.broadcast_to(second, (4,) + second.shape))
        first_far = hop(first, 1)
        second_far = hop(after(second, first_far), 1)
        table, conv, vectors = unpack(first, after(first_far, *cots), [w.shape for w in groups[0]])
        attn_shard = after(attn_shard, second, table)
        res, up = unpack(second, second_far, [w.shape for w in groups[1]])
    else:
        (table, conv, vectors), (res, up) = (gather_plain(group) for group in groups)
    attn_w = lax.all_gather(attn_shard, "seq", axis=0)
    mlp_w = lax.all_gather(after(mlp_shard, attn_w), "seq", axis=0)
    vectors = jnp.pad(join_vectors(line.spread(vectors), lot, c, x), ((0, 4), (0, 0)))

    ids = jnp.concatenate(pick([coarse_ids[i] for i in range(4)], c))
    vocab = table.shape[0]
    code = jnp.arange(vocab, dtype=jnp.int32)
    block = vocab // 8
    slot_of = code // block
    code = (((slot_of & 3) << 1) | ((slot_of >> 2) ^ x)) * block + code % block
    onehot = (ids[:, None] == code[None, :]).astype(BF16)
    embed = dot(onehot, table)
    act = gelu(embed).astype(BF16).reshape(micros, coarse, quarter)
    prior, later = edges((act[:, :step], act[:, coarse - step :]))
    padded = jnp.concatenate([prior, act, later], axis=1)
    taps = jnp.concatenate(
        [padded[:, k * step : k * step + coarse] for k in range(3)], axis=2
    ).reshape(micros * coarse, 3 * quarter)
    conv_terms = dot_t(taps, conv).reshape(micros, coarse, width)
    conv_out = fold(line, [conv_terms[j] for j in range(4)])
    mixed = after(gelu(conv_out).astype(BF16), res, up)
    mixed_all = jnp.concatenate(line.spread(mixed), axis=0)
    hidden = (embed + dot(mixed_all, res)).astype(BF16)
    up_terms = dot_t(hidden, up).reshape(micros, coarse, 4 * width)
    up_terms = fold(line, [up_terms[j] for j in range(4)])
    i = jnp.arange(32, dtype=jnp.int32)
    from_up = (((i >> 2) & 1) ^ x) * 16 + (i >> 3) * 4 + (i & 3)
    to_up = ((i >> 2) & 3) * 8 + ((i >> 4) ^ x) * 4 + (i & 3)
    stream_zero = enter(up_terms, stream_in, from_up, quarters)
    segments = lax.dynamic_index_in_dim(segment_ids, c, 0, keepdims=False)
    attn_w = join_rows(attn_w)
    attn_w = (attn_w, swap(attn_w, 1))
    norm_one, stream_one, norm_two, qkv, context = layer_forward(
        segments, stream_zero, vectors, attn_w
    )

    norm_all = line.spread(norm_two)
    mlp_act, grad_pre, norm_rows, cot_rows, *outs, keep, send, cot_mine = mlp(
        norm_all, cots, join_rows(mlp_w), stream_one, jnp.arange(4, dtype=jnp.int32) ^ c
    )
    from_core = swap(send, 1)
    over_y = (keep[tokens:] + from_core[tokens:].astype(F32)).astype(BF16)
    (from_y,) = line.send((over_y, 2))
    grad_mlp = mlp_grads(after(norm_rows, over_y), cot_rows, mlp_act, grad_pre)
    turned = lambda v, j: jnp.stack([v[m ^ order_of(j)] for m in range(4)])
    result, over_y = fold_core(
        [d.reshape(micros, tokens, quarter) for d in outs], fix=turned
    )
    terms = lax.optimization_barrier((keep, from_core, from_y, grad_mlp, over_y))
    grads, over_y = terms[:3], terms[4]
    (from_y,) = line.send((over_y, 2))
    result = (result + turned(from_y, 2).astype(F32)).astype(BF16)
    act_done = from_y
    result = jnp.stack(pick([result[order_of(m)] for m in range(4)], c))
    grad_mlp = lax.psum_scatter(split_rows(terms[3]), "seq", scatter_dimension=0, tiled=False)

    att, input_grad, grad_vectors, *grad_rows = layer_backward(
        segments, [stream_zero, stream_one], vectors, grads, cot_mine, attn_w, qkv
    )
    grad_vectors = split_vectors(grad_vectors[:4], lot, c, x)
    leave_rows, *grad_in_q = leave(input_grad, to_up, quarters)
    grad_rows[0] = after(grad_rows[0], leave_rows, act_done)
    grad_attn, send = layer_grads(norm_one, att, grad_rows, context)
    leave_rows, from_y, send = lax.optimization_barrier(
        (leave_rows, *line.send((leave_rows, 2)), send)
    )
    grad_up_rows = [leave_rows, swap(leave_rows, 1), from_y, swap(from_y, 1)]
    grad_up_rows = jnp.concatenate(grad_up_rows, axis=0)
    grad_hidden = dot(grad_up_rows, up)
    grad_low = grad_hidden.astype(BF16)
    grad_up = gram(grad_up_rows, hidden).astype(BF16)
    grad_res = gram(mixed_all, grad_low).astype(BF16)
    up_started = cross_x([grad_res, grad_up])
    grad_mixed = dot_t(after(grad_low, grad_up, grad_res), res).reshape(micros, coarse, width)
    grad_mixed, over_y = fold_core([grad_mixed[j] for j in range(4)])
    over_y, send = lax.optimization_barrier((over_y, swap(send, 1)))
    grad_attn = grad_attn.astype(F32) + send.astype(F32)
    grad_attn = split_rows(grad_attn.astype(BF16))
    grad_attn = lax.psum_scatter(grad_attn, "seq", scatter_dimension=0, tiled=False)
    grad_mixed = grad_mixed + line.send((over_y, 2))[0].astype(F32)
    grad_conv_low = (gelu_grad(conv_out) * grad_mixed).astype(BF16)
    grad_conv_low, grad_mlp, up_started = lax.optimization_barrier((grad_conv_low, grad_mlp, tuple(up_started)))
    grad_in, grad_down = grad_mlp[0].astype(F32), grad_mlp[1].astype(F32).T

    grad_conv_all = jnp.concatenate(line.spread(grad_conv_low), axis=0)
    grad_taps = dot(grad_conv_all, conv).reshape(micros, coarse, 3 * quarter)
    tap = [grad_taps[:, :, k * quarter : (k + 1) * quarter] for k in range(3)]
    rims = tap[0][:, :step].astype(BF16), tap[2][:, coarse - step :].astype(BF16)
    prior, later = edges(rims)
    grad_conv = gram(grad_conv_all, taps).astype(BF16)
    grad_vectors = fold(line, grad_vectors)
    grad_act = (
        tap[1]
        + jnp.concatenate([tap[0][:, step:], later.astype(F32)], axis=1)
        + jnp.concatenate([prior.astype(F32), tap[2][:, : coarse - step]], axis=1)
    ).reshape(micros * coarse, quarter)
    grad_embed = (grad_hidden + gelu_grad(embed) * grad_act).astype(BF16)
    pieces = line.exchange(grad_in_q)
    started = cross_x([gram(onehot, grad_embed), grad_conv, grad_vectors])
    up_started, near = lax.optimization_barrier((tuple(up_started), started[0]))
    pieces, near = lax.optimization_barrier((pieces, near))
    started = (near, *started[1:])
    grad_res, grad_up = cross_z(up_started, [w.shape for w in groups[1]])
    grad_table, grad_conv, grad_vectors = cross_z(started, [w.shape for w in groups[0]])
    grad_conv = grad_conv.reshape(-1, 3, quarter).transpose(1, 2, 0)
    input_grads = jnp.stack(pick(pieces, c))
    grad_attn = grad_attn[0].astype(F32) + line.send((grad_attn[1], 2))[0].astype(F32)
    grad_qkv, grad_out = grad_attn[:, : 3 * quarter], grad_attn[:, 3 * quarter :]
    grad_vectors = [grad_vectors[i, :lot] for i in range(4)]
    return (
        result,
        input_grads,
        grad_table,
        grad_conv,
        grad_res,
        grad_up.T,
        grad_vectors[0],
        grad_vectors[1],
        grad_qkv.reshape(qkv_weight.shape),
        grad_out.T,
        grad_vectors[2],
        grad_vectors[3],
        grad_in,
        grad_down,
    )


def solution(mesh):
    wide = P(("cond", "seq"))
    acts = P(None, "seq", "cond")
    weights = (
        P("seq", "cond"),
        P(None, "cond", "seq"),
        P("seq", "cond"),
        P("cond", "seq"),
        wide,
        wide,
        P("seq", None, "cond"),
        P("cond", "seq"),
        wide,
        wide,
        P("seq", "cond"),
        P("cond", "seq"),
    )
    return jax.shard_map(
        on_device,
        mesh=mesh,
        in_specs=(acts, P(None, "seq"), P(None, "seq"), acts) + weights,
        out_specs=(acts, acts) + weights,
        check_vma=False,
    )
```

```python
import math

import jax
import jax.numpy as jnp
from jax import lax
from jax.experimental import pallas as pl
from jax.experimental.pallas import tpu as pltpu
from jax.sharding import PartitionSpec as P

HEAD = 64
ROW = 64
CONV_DILATION = 27
EPSILON = 1e-05
NEG_FILL = -1e30
LANES = 128
BF16 = jnp.bfloat16
F32 = jnp.float32


def tuned():
    return lax.axis_size("seq") == 8


def swap(x, j):
    return lax.ppermute(x, "cond", [(i, i ^ j) for i in range(4)])


def hop(x, k):
    return lax.ppermute(x, "seq", [(i, i ^ k) for i in range(8)])


def place():
    c = lax.axis_index("cond")
    return c, (lax.axis_index("seq") & 1 if tuned() else jnp.zeros((), jnp.int32))


def after(value, *before):
    return lax.optimization_barrier((value, *before))[0]


def dot(a, b, dims=((1,), (0,))):
    return lax.dot_general(a, b, (dims, ((), ())), preferred_element_type=F32)


def gram(a, b):
    return dot(a, b, ((0,), (0,)))


def dot_t(a, b):
    return dot(a, b, ((1,), (1,)))


def gelu(v):
    return 0.5 * v * (1.0 + lax.erf(v * math.sqrt(0.5)))


def gelu_grad(v):
    return 0.5 * (1.0 + lax.erf(v * math.sqrt(0.5))) + v * (
        math.sqrt(0.5 / math.pi) * jnp.exp(-0.5 * v * v)
    )


def pick(items, t):
    low, high = (t & 1) == 1, (t & 2) == 2
    items = [jnp.where(low, items[i ^ 1], items[i]) for i in range(4)]
    return [jnp.where(high, items[i ^ 2], items[i]) for i in range(4)]


def regroup(x, dim, outer, inner):
    n = x.shape[dim] // 8
    shape = x.shape
    x = x.reshape(shape[:dim] + (outer, inner, n) + shape[dim + 1 :])
    return jnp.swapaxes(x, dim, dim + 1).reshape(shape)


def cost(us):
    return pl.CostEstimate(flops=int(us * 1.5e9), transcendentals=0, bytes_accessed=0)


CELL = 256
ALONG_Z = [[0, 2, 4, 6], [1, 3, 5, 7]]
VMEM_ROOM = 48 * 1024 * 1024


def bundle(shards):
    return jnp.concatenate(
        [s[:, i : i + CELL] for s in shards for i in range(0, s.shape[1], CELL)], axis=0
    )


def along_z(x):
    return lax.all_to_all(x, "seq", 0, 0, axis_index_groups=ALONG_Z, tiled=True)


def unpack_body(shapes, near_ref, far_ref, *outs):
    p = pl.program_id(0)

    def copy(ref):
        at = 0
        for (r, w), out in zip(shapes, outs):
            for i in range(0, w, CELL):
                out[:, i : i + CELL] = ref[0, at : at + r]
                at += r

    pl.when(p < 4)(lambda: copy(near_ref))
    pl.when(p >= 4)(lambda: copy(far_ref))


def unpack(near, far, shapes):
    block = (1,) + near.shape[1:]
    return pl.pallas_call(
        lambda *refs: unpack_body(shapes, *refs),
        out_shape=[jax.ShapeDtypeStruct((8 * r, w), near.dtype) for r, w in shapes],
        grid=(8,),
        in_specs=[
            pl.BlockSpec(block, lambda p: (jnp.minimum(p, 3), 0, 0)),
            pl.BlockSpec(block, lambda p: (jnp.maximum(p - 4, 0), 0, 0)),
        ],
        out_specs=[pl.BlockSpec((r, w), lambda p: (p, 0)) for r, w in shapes],
        compiler_params=pltpu.CompilerParams(vmem_limit_bytes=VMEM_ROOM),
        name="unpack",
        cost_estimate=cost(3),
    )(near, far)


def gather_plain(shards):
    return [regroup(lax.all_gather(s, "seq", axis=0, tiled=True), 0, 4, 2) for s in shards]


def pack_body(count, *refs):
    half, at = pl.program_id(0), 0
    for ref in refs[:count]:
        r, w = ref.shape
        for i in range(0, w, CELL):
            for k, out in enumerate(refs[count:]):

                @pl.when(half == k)
                def _(out=out, ref=ref, at=at, r=r, i=i):
                    out[0, at : at + r] = ref[:, i : i + CELL]

            at += r


def pack(grads):
    shapes = [(g.shape[0] // 8, g.shape[1]) for g in grads]
    rows = sum(r * w for r, w in shapes) // CELL
    shape = jax.ShapeDtypeStruct((4, rows, CELL), BF16)
    return pl.pallas_call(
        lambda *refs: pack_body(len(grads), *refs),
        out_shape=(shape, shape),
        grid=(2, 4),
        in_specs=[pl.BlockSpec((r, w), lambda h, p: (4 * h + p, 0)) for r, w in shapes],
        out_specs=(
            pl.BlockSpec((1, rows, CELL), lambda h, p: (jnp.where(h == 0, p, 3), 0, 0)),
            pl.BlockSpec((1, rows, CELL), lambda h, p: (jnp.where(h == 1, p, 0), 0, 0)),
        ),
        compiler_params=pltpu.CompilerParams(vmem_limit_bytes=VMEM_ROOM),
        name="pack",
        cost_estimate=cost(2),
    )(*grads)


def total_body(shapes, in_ref, *outs):
    at = 0
    for (r, w), out in zip(shapes, outs):
        for i in range(0, w, CELL):
            cells = [in_ref[k, at : at + r].astype(F32) for k in range(4)]
            out[:, i : i + CELL] = (cells[0] + cells[1]) + (cells[2] + cells[3])
            at += r


def total(parts, shapes):
    return pl.pallas_call(
        lambda *refs: total_body(shapes, *refs),
        out_shape=[jax.ShapeDtypeStruct(shape, F32) for shape in shapes],
        compiler_params=pltpu.CompilerParams(vmem_limit_bytes=VMEM_ROOM),
        name="total",
        cost_estimate=cost(1),
    )(parts)


def cross_x(grads):
    grads = [g.astype(BF16) for g in grads]
    if tuned():
        near, far = pack(grads)
        return near, hop(far, 1)
    return grads


def cross_z(started, shapes):
    if tuned():
        near, far = started
        return total(along_z((near.astype(F32) + far.astype(F32)).astype(BF16)), shapes)
    return [
        lax.psum_scatter(
            regroup(g, 0, 2, 4), "seq", scatter_dimension=0, tiled=True
        ).astype(F32)
        for g in started
    ]


class Line:
    def __init__(self):
        self.last = ()

    def send(self, *items):
        items = [(after(x, *self.last) if self.last else x, j) for x, j in items]
        self.last = [swap(x, j) for x, j in items]
        return self.last

    def spread(self, x):
        (y,) = self.send((x, 2))
        return [x, swap(x, 1), y, swap(y, 1)]

    def exchange(self, items):
        two, three = self.send((items[2], 2), (items[3], 3))
        return [items[0], swap(items[1], 1), two, three]


def same(x, j):
    return x


def fold_core(items, wire=BF16, fix=same):
    one = fix(swap(items[1].astype(wire), 1), 1).astype(F32)
    three = fix(swap(items[3].astype(wire), 1), 1).astype(F32)
    return items[0].astype(F32) + one, (items[2].astype(F32) + three).astype(wire)


def fold(line, items, wire=BF16, fix=same):
    zero, two = fold_core(items, wire, fix)
    return zero + fix(line.send((two, 2))[0], 2).astype(F32)


def lane_block(i):
    return pl.ds(pl.multiple_of(i * LANES, LANES), LANES)


def enter_body(from_up, to_layer, up_ref, q0, q1, q2, q3, out_ref, held, spaced):
    coarse = up_ref.shape[0]
    quarter = q0.shape[1]
    for j, ref in enumerate((q0, q1, q2, q3)):
        held[:, j * quarter : (j + 1) * quarter] = ref[...]
    for r in range(4):
        for p in range(8):
            spaced[p, pl.ds(r, coarse, stride=4), :] = up_ref[:, lane_block(from_up[r * 8 + p])]
    for p in range(8):
        out_ref[:, p * LANES : (p + 1) * LANES] = spaced[p] + held[
            :, lane_block(to_layer[p])
        ].astype(F32)


def enter(up_terms, quarters, from_up, to_layer):
    coarse, wide = up_terms.shape
    whole = lambda shape: pl.BlockSpec(shape, lambda i, a, b: (0, 0))
    tokens, quarter = quarters[0].shape
    return pl.pallas_call(
        enter_body,
        out_shape=jax.ShapeDtypeStruct((tokens, wide // 4), F32),
        grid_spec=pltpu.PrefetchScalarGridSpec(
            num_scalar_prefetch=2,
            grid=(1,),
            in_specs=[whole((coarse, wide))] + [whole((tokens, quarter))] * 4,
            out_specs=whole((tokens, wide // 4)),
            scratch_shapes=[
                pltpu.VMEM((tokens, wide // 4), BF16),
                pltpu.VMEM((8, tokens, LANES), F32),
            ],
        ),
        compiler_params=pltpu.CompilerParams(vmem_limit_bytes=VMEM_ROOM),
        name="enter",
        cost_estimate=cost(2),
    )(from_up, to_layer, up_terms, *quarters)


def leave_body(to_up, to_quarters, in_ref, rows_ref, q0, q1, q2, q3, spaced):
    coarse = rows_ref.shape[0]
    for p in range(8):
        spaced[p] = in_ref[:, p * LANES : (p + 1) * LANES]
    for i in range(32):
        source = to_up[i]
        rows_ref[:, i * LANES : (i + 1) * LANES] = spaced[
            source & 7, pl.ds(source >> 3, coarse, stride=4), :
        ].astype(BF16)
    for j, ref in enumerate((q0, q1, q2, q3)):
        for half in range(2):
            ref[:, half * LANES : (half + 1) * LANES] = in_ref[
                :, lane_block(to_quarters[2 * j + half])
            ].astype(BF16)


def leave(grad, to_up, to_quarters):
    tokens, width = grad.shape
    whole = lambda shape: pl.BlockSpec(shape, lambda i, a, b: (0, 0))
    shapes = [(tokens // 4, 4 * width)] + [(tokens, width // 4)] * 4
    return pl.pallas_call(
        leave_body,
        out_shape=[jax.ShapeDtypeStruct(shape, BF16) for shape in shapes],
        grid_spec=pltpu.PrefetchScalarGridSpec(
            num_scalar_prefetch=2,
            grid=(1,),
            in_specs=[whole((tokens, width))],
            out_specs=[whole(shape) for shape in shapes],
            scratch_shapes=[pltpu.VMEM((8, tokens, LANES), F32)],
        ),
        compiler_params=pltpu.CompilerParams(vmem_limit_bytes=VMEM_ROOM),
        name="leave",
        cost_estimate=cost(2),
    )(to_up, to_quarters, grad)


TILE = 128
SCALE = 1.0 / math.sqrt(HEAD)


def by_head(x):
    heads = x.shape[1] // HEAD
    feature = lax.broadcasted_iota(jnp.int32, x.shape, 1) // HEAD
    return jnp.concatenate(
        [jnp.where(feature == h, x, jnp.zeros_like(x)) for h in range(heads)], axis=0
    )


def of_heads(x):
    heads = x.shape[1] // HEAD
    feature = lax.broadcasted_iota(jnp.int32, (TILE, x.shape[1]), 1) // HEAD
    out = x[:TILE]
    for h in range(1, heads):
        out = jnp.where(feature == h, x[h * TILE : (h + 1) * TILE], out)
    return out


def visible(column, row):
    i = lax.broadcasted_iota(jnp.int32, (TILE, TILE), 0)
    j = lax.broadcasted_iota(jnp.int32, (TILE, TILE), 1)
    return (column == row) & (i >= j) & (i // ROW == j // ROW)


def soft(query, keys, allowed):
    scores = dot_t(query, keys) * SCALE
    probs = []
    for h in range(scores.shape[1] // TILE):
        part = jnp.where(allowed, scores[:, h * TILE : (h + 1) * TILE], NEG_FILL)
        exps = jnp.exp(part - jnp.max(part, axis=1, keepdims=True))
        probs.append(exps * (1.0 / jnp.sum(exps, axis=1, keepdims=True)))
    return probs


def attend_tile(qkv, allowed):
    n = qkv.shape[1] // 3
    probs = soft(qkv[:, :n], by_head(qkv[:, n : 2 * n]), allowed)
    low = jnp.concatenate([p.astype(BF16) for p in probs], axis=1)
    return dot(low, by_head(qkv[:, 2 * n :])).astype(BF16)


def attend_back_tile(qkv, grad, allowed):
    n = grad.shape[1]
    query = qkv[:, :n]
    keys = by_head(qkv[:, n : 2 * n])
    probs = soft(query, keys, allowed)
    grad_probs = dot_t(grad, by_head(qkv[:, 2 * n :]))
    grads = []
    for h, p in enumerate(probs):
        part = grad_probs[:, h * TILE : (h + 1) * TILE]
        inner = jnp.sum(p * part, axis=1, keepdims=True)
        grads.append((p * (part - inner)).astype(BF16))
    grads = jnp.concatenate(grads, axis=1)
    low = jnp.concatenate([p.astype(BF16) for p in probs], axis=1)
    return jnp.concatenate(
        [
            (dot(grads, keys) * SCALE).astype(BF16),
            (of_heads(gram(grads, query)) * SCALE).astype(BF16),
            of_heads(gram(low, grad)).astype(BF16),
        ],
        axis=1,
    )


def standard(stream):
    mean = jnp.mean(stream, axis=1, keepdims=True)
    centred = stream - mean
    rstd = lax.rsqrt(jnp.mean(centred * centred, axis=1, keepdims=True) + EPSILON)
    return centred * rstd, rstd


def standard_back(normed, rstd, gain, grad):
    scaled = grad * gain
    return rstd * (
        scaled
        - jnp.mean(scaled, axis=1, keepdims=True)
        - normed * jnp.mean(scaled * normed, axis=1, keepdims=True)
    )


ANYWHERE = jax.ShapeDtypeStruct
LAYER_TILE = 256
SUBS = LAYER_TILE // TILE


def joined(ref, start, stop):
    return ref[:, :, :, start:stop].reshape(-1, stop - start)


def masks(column_ref, row_ref):
    return [
        visible(column_ref[i * TILE : (i + 1) * TILE], row_ref[i]) for i in range(SUBS)
    ]


def forward_body(*refs):
    column_ref, row_ref, stream_ref, vec_ref = refs[:4]
    weights = refs[4:8]
    norm_ref, out_ref, norm_two_ref = refs[8:11]
    qkvs, contexts = refs[11:15], refs[15:19]
    allowed = masks(column_ref, row_ref)
    stream = stream_ref[...]
    normed, _ = standard(stream)
    norm_ref[...] = (normed * vec_ref[0:1] + vec_ref[1:2]).astype(BF16)
    for weight, qkv_ref, context_ref in zip(weights, qkvs, contexts):
        n = context_ref.shape[1]
        qkv_ref[...] = dot(norm_ref[...], joined(weight, 0, 3 * n)).astype(BF16)
        for i in range(SUBS):
            at = slice(i * TILE, (i + 1) * TILE)
            context_ref[at] = attend_tile(qkv_ref[at], allowed[i])
        stream = stream + dot_t(context_ref[...], joined(weight, 3 * n, 4 * n))
    out_ref[...] = stream
    normed, _ = standard(stream)
    norm_two_ref[...] = (normed * vec_ref[2:3] + vec_ref[3:4]).astype(BF16)


def backward_body(*refs):
    column_ref, row_ref, zero_ref, one_ref, vec_ref, keep_ref, core_ref, y_ref, cot_ref = refs[:9]
    weights, qkvs = refs[9:13], refs[13:17]
    att_ref, input_ref, vec_grad_ref = refs[17:20]
    rows = refs[20:24]
    allowed = masks(column_ref, row_ref)
    grad = keep_ref[...] + core_ref[...].astype(F32) + y_ref[...].astype(F32)
    normed, rstd = standard(one_ref[...])
    sums = [jnp.sum(grad * normed, axis=0, keepdims=True), jnp.sum(grad, axis=0, keepdims=True)]
    stream = cot_ref[...].astype(F32) + standard_back(normed, rstd, vec_ref[2:3], grad)
    att_ref[...] = stream.astype(BF16)
    grad = None
    for weight, qkv_ref, row_grad_ref in zip(weights, qkvs, rows):
        n = qkv_ref.shape[1] // 3
        context = dot(att_ref[...], joined(weight, 3 * n, 4 * n)).astype(BF16)
        for i in range(SUBS):
            at = slice(i * TILE, (i + 1) * TILE)
            row_grad_ref[at] = attend_back_tile(qkv_ref[at], context[at], allowed[i])
        part = dot_t(row_grad_ref[...], joined(weight, 0, 3 * n))
        grad = part if grad is None else grad + part
    normed, rstd = standard(zero_ref[...])
    sums = [
        jnp.sum(grad * normed, axis=0, keepdims=True),
        jnp.sum(grad, axis=0, keepdims=True),
    ] + sums
    input_ref[...] = stream + standard_back(normed, rstd, vec_ref[0:1], grad)

    @pl.when(pl.program_id(0) == 0)
    def _():
        vec_grad_ref[...] = jnp.zeros_like(vec_grad_ref)

    for i, v in enumerate(sums):
        vec_grad_ref[i : i + 1] += v


def layer_call(body, segments, arrays, fixed, weights, more, outs, name, us):
    tokens = segments.shape[0]
    wide = lambda w: pl.BlockSpec((LAYER_TILE, w), lambda i: (i, 0))
    still = lambda shape: pl.BlockSpec(shape, lambda i: (0,) * len(shape))
    _, _, n, w = weights[0].shape
    tiles = tokens // TILE
    return pl.pallas_call(
        body,
        out_shape=[space(shape, dtype) for space, shape, dtype in outs],
        grid=(tokens // LAYER_TILE,),
        in_specs=[wide(1), pl.BlockSpec((SUBS, 1, TILE), lambda i: (i, 0, 0))]
        + [wide(a.shape[1]) for a in arrays]
        + [still(fixed.shape)]
        + [wide(a.shape[1]) for a in more[0]]
        + [pl.BlockSpec((8, 1, n, w), lambda i, k=k: (0, k, 0, 0)) for k in (0, 0, 1, 1)]
        + [wide(a.shape[1]) for a in more[1]],
        out_specs=[
            wide(shape[1]) if shape[0] == tokens else still(shape) for _, shape, _ in outs
        ],
        compiler_params=pltpu.CompilerParams(vmem_limit_bytes=VMEM_ROOM),
        name=name,
        cost_estimate=cost(us),
    )(
        segments.reshape(tokens, 1),
        segments.reshape(tiles, 1, TILE),
        *arrays,
        fixed,
        *more[0],
        weights[0],
        weights[1],
        weights[0],
        weights[1],
        *more[1],
    )


def layer_forward(segments, stream, vectors, weights):
    tokens, width = stream.shape
    quarter = width // 4
    outs = (
        [
            (pltpu.HBM, (tokens, width), BF16),
            (ANYWHERE, (tokens, width), F32),
            (ANYWHERE, (tokens, width), BF16),
        ]
        + [(pltpu.HBM, (tokens, 3 * quarter), BF16)] * 4
        + [(pltpu.HBM, (tokens, quarter), BF16)] * 4
    )
    norm_one, stream_one, norm_two, *rest = layer_call(
        forward_body, segments, [stream], vectors, weights, ([], []), outs, "layer_forward", 18
    )
    return norm_one, stream_one, norm_two, rest[:4], rest[4:]


def layer_backward(segments, streams, vectors, grads, cot, weights, qkv):
    tokens, width = cot.shape
    outs = [
        (ANYWHERE, (tokens, width), BF16),
        (ANYWHERE, (tokens, width), F32),
        (ANYWHERE, vectors.shape, F32),
    ]
    outs += [(ANYWHERE, q.shape, BF16) for q in qkv]
    return layer_call(
        backward_body, segments, streams, vectors, weights, ([*grads, cot], qkv), outs,
        "layer_backward",
        24,
    )


def layer_grads_body(norm_ref, att_ref, *refs):
    rows, contexts, outs = refs[:4], refs[4:8], refs[8:]
    blocks, _, n, _ = outs[0].shape
    for j in range(4):
        out, k = outs[j & 1], j >> 1
        w = rows[j].shape[1]
        left = gram(norm_ref[...], rows[j][...]).astype(BF16)
        right = gram(att_ref[...], contexts[j][...]).astype(BF16)
        for i in range(blocks):
            out[i, k, :, :w] = left[i * n : (i + 1) * n]
            out[i, k, :, w:] = right[i * n : (i + 1) * n]


def layer_grads(norm, att, rows, contexts):
    tokens, width = norm.shape
    n = width // 8
    part = pl.BlockSpec((tokens, 2 * n), lambda i: (0, i))
    whole = lambda a: pl.BlockSpec(a.shape, lambda i: (0, 0))
    shape = jax.ShapeDtypeStruct((8, 2, n, width), BF16)
    out = pl.BlockSpec((2, 2, n, width), lambda i: (i, 0, 0, 0))
    return pl.pallas_call(
        layer_grads_body,
        out_shape=(shape, shape),
        grid=(4,),
        in_specs=[part, part] + [whole(a) for a in (*rows, *contexts)],
        out_specs=(out, out),
        compiler_params=pltpu.CompilerParams(vmem_limit_bytes=VMEM_ROOM),
        name="layer_grads",
        cost_estimate=cost(8),
    )(norm, att, *rows, *contexts)


def vector_owner(c, x):
    i = jnp.arange(32)
    source = i & 7
    piece = ((i >> 3) ^ c) * 8 + ((((source & 1) ^ x) << 2) | (source >> 1))
    return piece[:, None] == jnp.arange(32)[None, :]


PAD = 16


def vector_rows(vectors):
    ends = [(0, 0)] * (vectors.ndim - 2)
    count, n = vectors.shape[-2:]
    return jnp.pad(vectors, ends + [(0, PAD - count), (0, CELL - n)])


def join_vectors(spreads, n, c, x):
    pieces = jnp.stack([s.reshape(8, -1, PAD, CELL)[:, :, :4, :n] for s in spreads])
    pieces = pieces.transpose(3, 0, 1, 2, 4).reshape(4, 32, -1)
    owner = vector_owner(c, x).astype(BF16)
    full = jnp.einsum("dp,vpn->vdn", owner, pieces, preferred_element_type=F32)
    return full.reshape(4, -1)


def split_vectors(full, n, c, x):
    owner = vector_owner(c, x).astype(F32)
    pieces = jnp.einsum(
        "dp,vdn->pvn",
        owner,
        full.reshape(4, 32, -1),
        precision=lax.Precision.HIGHEST,
        preferred_element_type=F32,
    )
    pieces = pieces.reshape(4, 8, 4, -1, n).swapaxes(2, 3)
    rows = vector_rows(pieces)
    return [rows[j].reshape(-1, CELL) for j in range(4)]


MLP_TILE = 256
TURNS = 8


def order_of(k):
    return ((k & 1) << 1) | (k >> 1)


def mlp_body(index, *refs):
    (n0, n1, n2, n3, q0, q1, q2, q3, in_ref, down_ref, stream_ref) = refs[:11]
    (act_ref, grad_ref, norm_ref, cot_ref, d0, d1, d2, d3, keep_ref, send_ref, mine_ref) = refs[11:22]
    (wide,) = refs[22:]
    tile = pl.program_id(0)
    k = tile // 2
    for at, ref in enumerate((n0, n2, n1, n3)):

        @pl.when(k == at)
        def _(ref=ref):
            norm_ref[...] = ref[...]

    quarters = [pl.ds(pl.multiple_of(index[j] * 256, 256), 256) for j in range(4)]
    for j, ref in enumerate((q0, q1, q2, q3)):
        cot_ref[:, quarters[j]] = ref[...]
    weight_in = in_ref[...].reshape(-1, in_ref.shape[-1])
    weight_down = down_ref[...].reshape(-1, down_ref.shape[-1])
    pre = dot(norm_ref[...], weight_in)
    half = 0.5 + 0.5 * lax.erf(pre * math.sqrt(0.5))
    act = (pre * half).astype(BF16)
    act_ref[...] = act
    slope = half + pre * (math.sqrt(0.5 / math.pi) * jnp.exp(-0.5 * pre * pre))
    grad = (slope * dot(cot_ref[...], weight_down)).astype(BF16)
    grad_ref[...] = grad
    wide[...] = dot_t(act, weight_down)

    @pl.when(tile < 2)
    def _():
        wide[...] = wide[...] + stream_ref[...]
        mine_ref[...] = cot_ref[...]

    for j, ref in enumerate((d0, d1, d2, d3)):
        ref[...] = wide[:, quarters[j]].astype(BF16)
    other = dot_t(grad, weight_in)

    @pl.when(tile < 4)
    def _():
        keep_ref[...] = other

    @pl.when(tile >= 4)
    def _():
        send_ref[...] = other.astype(BF16)


def mlp(norms, cots, weights, stream, index):
    tokens, width = norms[0].shape
    rows, quarter = cots[0].shape
    hidden = weights.shape[-1]
    n = weights.shape[2]
    tile = MLP_TILE
    per = tokens // tile
    assert per == 2
    held = lambda start, count: lambda i, index: (jnp.clip(i - start, 0, count - 1), 0)
    norm_specs = [
        pl.BlockSpec((tile, width), held(2 * order_of(m), 2)) for m in range(4)
    ]
    cot_specs = [
        pl.BlockSpec(
            (tile, quarter),
            lambda i, index, j=j: (
                jnp.bitwise_xor(order_of(i // 2), j) * 2 + lax.rem(i, 2),
                0,
            ),
        )
        for j in range(4)
    ]
    weight_specs = [
        pl.BlockSpec((8, 1, n, hidden), lambda i, index, k=k: (0, k, 0, 0)) for k in range(2)
    ]
    each = lambda w: pl.BlockSpec((tile, w), lambda i, index: (i, 0))
    shape = jax.ShapeDtypeStruct
    return pl.pallas_call(
        mlp_body,
        out_shape=[
            shape((rows, hidden), BF16),
            shape((rows, hidden), BF16),
            shape((rows, width), BF16),
            shape((rows, width), BF16),
            *[shape((rows, quarter), BF16)] * 4,
            shape((rows // 2, width), F32),
            shape((rows // 2, width), BF16),
            shape((tokens, width), BF16),
        ],
        grid_spec=pltpu.PrefetchScalarGridSpec(
            num_scalar_prefetch=1,
            grid=(TURNS,),
            in_specs=norm_specs
            + cot_specs
            + weight_specs
            + [pl.BlockSpec((tile, width), held(0, 2))],
            out_specs=[each(hidden), each(hidden), each(width), each(width)]
            + [each(quarter)] * 4
            + [
                pl.BlockSpec((tile, width), held(0, 4)),
                pl.BlockSpec((tile, width), held(4, 4)),
                pl.BlockSpec((tile, width), held(0, 2)),
            ],
            scratch_shapes=[pltpu.VMEM((tile, width), F32)],
        ),
        compiler_params=pltpu.CompilerParams(vmem_limit_bytes=VMEM_ROOM),
        name="mlp",
        cost_estimate=cost(30),
    )(index, *norms, *cots, weights, weights, stream)


def mlp_grads_body(norm_ref, cot_ref, act_ref, grad_ref, out_ref):
    for k, (left, right) in enumerate(((norm_ref, grad_ref), (cot_ref, act_ref))):
        block = gram(left[...], right[...]).astype(BF16)
        n = out_ref.shape[2]
        for i in range(out_ref.shape[0]):
            out_ref[i, k] = block[i * n : (i + 1) * n]


def mlp_grads(norm, cot, act, grad):
    rows, width = norm.shape
    hidden = act.shape[1]
    n = width // 8
    whole = pl.BlockSpec((rows, hidden), lambda i: (0, 0))
    part = pl.BlockSpec((rows, 2 * n), lambda i: (0, i))
    return pl.pallas_call(
        mlp_grads_body,
        out_shape=pltpu.HBM((8, 2, n, hidden), BF16),
        grid=(4,),
        in_specs=[part, part, whole, whole],
        out_specs=pl.BlockSpec((2, 2, n, hidden), lambda i: (i, 0, 0, 0)),
        compiler_params=pltpu.CompilerParams(vmem_limit_bytes=VMEM_ROOM),
        name="mlp_grads",
        cost_estimate=cost(14),
    )(norm, cot, act, grad)


def join_rows(packed):
    pieces, _, n, w = packed.shape
    return (
        packed.reshape(8, pieces // 8, 2, n, w).swapaxes(1, 2).reshape(8, 2, n * pieces // 8, w)
    )


def split_rows(packed):
    _, _, n, w = packed.shape
    share = lax.axis_size("seq") // 8
    return (
        packed.reshape(8, 2, share, n // share, w).swapaxes(1, 2).reshape(8 * share, 2, n // share, w)
    )


def edges(cells):
    count = lax.axis_size("seq")
    head, tail = cells
    return (
        lax.ppermute(tail, "seq", [(i, i + 1) for i in range(count - 1)]),
        lax.ppermute(head, "seq", [(i + 1, i) for i in range(count - 1)]),
    )


def on_device(
    inputs,
    coarse_ids,
    segment_ids,
    cotangent,
    embed_table,
    conv_weight,
    res_weight,
    up_weight,
    gain_one,
    shift_one,
    qkv_weight,
    out_weight,
    gain_two,
    shift_two,
    in_weight,
    down_weight,
):
    c, x = place()
    micros, tokens, quarter = inputs.shape
    width = 4 * quarter
    coarse = coarse_ids.shape[1]
    step = CONV_DILATION
    slot = jnp.arange(8, dtype=jnp.int32)
    quarters = (((slot >> 1) ^ c) << 1) | (slot & 1)

    line = Line()
    stream_in = line.exchange(pick([inputs[i] for i in range(4)], c))
    attn_shard = jnp.concatenate([qkv_weight.reshape(-1, 3 * quarter), out_weight.T], axis=1)
    attn_shard = jnp.stack([attn_shard, *line.send((attn_shard, 2))])
    mlp_shard = jnp.stack([in_weight, down_weight.T])
    cots = line.spread(jnp.concatenate(pick([cotangent[i] for i in range(4)], c), axis=0))

    lot = gain_one.shape[0]
    vectors = vector_rows(jnp.stack([gain_one, shift_one, gain_two, shift_two]))
    conv_shard = conv_weight.transpose(2, 0, 1).reshape(-1, 3 * quarter)
    groups = ((embed_table, conv_shard, vectors), (res_weight, up_weight.T))
    if tuned():
        first, second = (bundle(group) for group in groups)
        first = along_z(jnp.broadcast_to(first, (4,) + first.shape))
        second = after(second, first, *stream_in, attn_shard)
        second = along_z(jnp.broadcast_to(second, (4,) + second.shape))
        first_far = hop(first, 1)
        second_far = hop(after(second, first_far), 1)
        table, conv, vectors = unpack(first, after(first_far, *cots), [w.shape for w in groups[0]])
        attn_shard = after(attn_shard, second, table)
        res, up = unpack(second, second_far, [w.shape for w in groups[1]])
    else:
        (table, conv, vectors), (res, up) = (gather_plain(group) for group in groups)
    attn_w = lax.all_gather(attn_shard, "seq", axis=0)
    mlp_w = lax.all_gather(after(mlp_shard, attn_w), "seq", axis=0)
    vectors = jnp.pad(join_vectors(line.spread(vectors), lot, c, x), ((0, 4), (0, 0)))

    ids = jnp.concatenate(pick([coarse_ids[i] for i in range(4)], c))
    vocab = table.shape[0]
    code = jnp.arange(vocab, dtype=jnp.int32)
    block = vocab // 8
    slot_of = code // block
    code = (((slot_of & 3) << 1) | ((slot_of >> 2) ^ x)) * block + code % block
    onehot = (ids[:, None] == code[None, :]).astype(BF16)
    embed = dot(onehot, table)
    act = gelu(embed).astype(BF16).reshape(micros, coarse, quarter)
    prior, later = edges((act[:, :step], act[:, coarse - step :]))
    padded = jnp.concatenate([prior, act, later], axis=1)
    taps = jnp.concatenate(
        [padded[:, k * step : k * step + coarse] for k in range(3)], axis=2
    ).reshape(micros * coarse, 3 * quarter)
    conv_terms = dot_t(taps, conv).reshape(micros, coarse, width)
    conv_out = fold(line, [conv_terms[j] for j in range(4)])
    mixed = after(gelu(conv_out).astype(BF16), res, up)
    mixed_all = jnp.concatenate(line.spread(mixed), axis=0)
    hidden = (embed + dot(mixed_all, res)).astype(BF16)
    up_terms = dot_t(hidden, up).reshape(micros, coarse, 4 * width)
    up_terms = fold(line, [up_terms[j] for j in range(4)])
    i = jnp.arange(32, dtype=jnp.int32)
    from_up = (((i >> 2) & 1) ^ x) * 16 + (i >> 3) * 4 + (i & 3)
    to_up = ((i >> 2) & 3) * 8 + ((i >> 4) ^ x) * 4 + (i & 3)
    stream_zero = enter(up_terms, stream_in, from_up, quarters)
    segments = lax.dynamic_index_in_dim(segment_ids, c, 0, keepdims=False)
    attn_w = join_rows(attn_w)
    attn_w = (attn_w, swap(attn_w, 1))
    norm_one, stream_one, norm_two, qkv, context = layer_forward(
        segments, stream_zero, vectors, attn_w
    )

    norm_all = line.spread(norm_two)
    mlp_act, grad_pre, norm_rows, cot_rows, *outs, keep, send, cot_mine = mlp(
        norm_all, cots, join_rows(mlp_w), stream_one, jnp.arange(4, dtype=jnp.int32) ^ c
    )
    from_core = swap(send, 1)
    over_y = (keep[tokens:] + from_core[tokens:].astype(F32)).astype(BF16)
    (from_y,) = line.send((over_y, 2))
    grad_mlp = mlp_grads(after(norm_rows, over_y), cot_rows, mlp_act, grad_pre)
    turned = lambda v, j: jnp.stack([v[m ^ order_of(j)] for m in range(4)])
    result, over_y = fold_core(
        [d.reshape(micros, tokens, quarter) for d in outs], fix=turned
    )
    terms = lax.optimization_barrier((keep, from_core, from_y, grad_mlp, over_y))
    grads, over_y = terms[:3], terms[4]
    (from_y,) = line.send((over_y, 2))
    result = (result + turned(from_y, 2).astype(F32)).astype(BF16)
    act_done = from_y
    result = jnp.stack(pick([result[order_of(m)] for m in range(4)], c))
    grad_mlp = lax.psum_scatter(split_rows(terms[3]), "seq", scatter_dimension=0, tiled=False)

    att, input_grad, grad_vectors, *grad_rows = layer_backward(
        segments, [stream_zero, stream_one], vectors, grads, cot_mine, attn_w, qkv
    )
    grad_vectors = split_vectors(grad_vectors[:4], lot, c, x)
    leave_rows, *grad_in_q = leave(input_grad, to_up, quarters)
    grad_rows[0] = after(grad_rows[0], leave_rows, act_done)
    grad_attn, send = layer_grads(norm_one, att, grad_rows, context)
    leave_rows, from_y, send = lax.optimization_barrier(
        (leave_rows, *line.send((leave_rows, 2)), send)
    )
    grad_up_rows = [leave_rows, swap(leave_rows, 1), from_y, swap(from_y, 1)]
    grad_up_rows = jnp.concatenate(grad_up_rows, axis=0)
    grad_hidden = dot(grad_up_rows, up)
    grad_low = grad_hidden.astype(BF16)
    grad_up = gram(grad_up_rows, hidden).astype(BF16)
    grad_res = gram(mixed_all, grad_low).astype(BF16)
    up_started = cross_x([grad_res, grad_up])
    grad_mixed = dot_t(after(grad_low, grad_up, grad_res), res).reshape(micros, coarse, width)
    grad_mixed, over_y = fold_core([grad_mixed[j] for j in range(4)])
    over_y, send = lax.optimization_barrier((over_y, swap(send, 1)))
    grad_attn = grad_attn.astype(F32) + send.astype(F32)
    grad_attn = split_rows(grad_attn.astype(BF16))
    grad_attn = lax.psum_scatter(grad_attn, "seq", scatter_dimension=0, tiled=False)
    grad_mixed = grad_mixed + line.send((over_y, 2))[0].astype(F32)
    grad_conv_low = (gelu_grad(conv_out) * grad_mixed).astype(BF16)
    grad_conv_low, grad_mlp, up_started = lax.optimization_barrier((grad_conv_low, grad_mlp, tuple(up_started)))
    grad_in, grad_down = grad_mlp[0].astype(F32), grad_mlp[1].astype(F32).T

    grad_conv_all = jnp.concatenate(line.spread(grad_conv_low), axis=0)
    grad_taps = dot(grad_conv_all, conv).reshape(micros, coarse, 3 * quarter)
    tap = [grad_taps[:, :, k * quarter : (k + 1) * quarter] for k in range(3)]
    rims = tap[0][:, :step].astype(BF16), tap[2][:, coarse - step :].astype(BF16)
    prior, later = edges(rims)
    grad_conv = gram(grad_conv_all, taps).astype(BF16)
    grad_vectors = fold(line, grad_vectors)
    grad_act = (
        tap[1]
        + jnp.concatenate([tap[0][:, step:], later.astype(F32)], axis=1)
        + jnp.concatenate([prior.astype(F32), tap[2][:, : coarse - step]], axis=1)
    ).reshape(micros * coarse, quarter)
    grad_embed = (grad_hidden + gelu_grad(embed) * grad_act).astype(BF16)
    pieces = line.exchange(grad_in_q)
    started = cross_x([gram(onehot, grad_embed), grad_conv, grad_vectors])
    up_started, near = lax.optimization_barrier((tuple(up_started), started[0]))
    pieces, near = lax.optimization_barrier((pieces, near))
    started = (near, *started[1:])
    grad_res, grad_up = cross_z(up_started, [w.shape for w in groups[1]])
    grad_table, grad_conv, grad_vectors = cross_z(started, [w.shape for w in groups[0]])
    grad_conv = grad_conv.reshape(-1, 3, quarter).transpose(1, 2, 0)
    input_grads = jnp.stack(pick(pieces, c))
    grad_attn = grad_attn[0].astype(F32) + line.send((grad_attn[1], 2))[0].astype(F32)
    grad_qkv, grad_out = grad_attn[:, : 3 * quarter], grad_attn[:, 3 * quarter :]
    grad_vectors = [grad_vectors[i, :lot] for i in range(4)]
    return (
        result,
        input_grads,
        grad_table,
        grad_conv,
        grad_res,
        grad_up.T,
        grad_vectors[0],
        grad_vectors[1],
        grad_qkv.reshape(qkv_weight.shape),
        grad_out.T,
        grad_vectors[2],
        grad_vectors[3],
        grad_in,
        grad_down,
    )


def solution(mesh):
    wide = P(("cond", "seq"))
    acts = P(None, "seq", "cond")
    weights = (
        P("seq", "cond"),
        P(None, "cond", "seq"),
        P("seq", "cond"),
        P("cond", "seq"),
        wide,
        wide,
        P("seq", None, "cond"),
        P("cond", "seq"),
        wide,
        wide,
        P("seq", "cond"),
        P("cond", "seq"),
    )
    return jax.shard_map(
        on_device,
        mesh=mesh,
        in_specs=(acts, P(None, "seq"), P(None, "seq"), acts) + weights,
        out_specs=(acts, acts) + weights,
        check_vma=False,
    )
```
